32 devices in a mesh: parts: 2 (over y), tm: 4 (over z), space: 4 (over x, core).
Axes of the slice: x: 2, y: 2, z: 4, core: 2. Of those that a mesh axis runs over, the one named last changes fastest.
Arguments:
- rhs: float32 [8, 16, 16, 1024], P(('parts', 'tm'), None, 'space'), parts along dimension 0, may hold values from -24 to 24
- diffusivity: float32 [32, 16, 1024], P('parts', 'space'), parts along dimension 0, may hold values from 0.5 to 2
- velocity: float32 [6], P('parts'), parts along dimension 0, may hold values from -1 to 1
Outputs:
- solution: float32 [8, 16, 16, 1024], P(('parts', 'tm'), None, 'space'), parts along dimension 0
The draws below stay inside these ranges and needn't reach their ends.
There are 2 independent parts, one for each index of `parts`. The reference program is written for one: setup_inputs(seed, part) draws one part's arguments, and reference() takes and returns one part's arrays. A program takes and returns all parts, laid end to end along the dimension named above; each array names one. Nothing has to cross between parts.
All inputs are finite; a program needn't handle non-finite values.
Results may differ from the reference program's by a relative error of at most 0.0002.
Values sent between devices are 32-bit elements; how exact they have to be, the bound alone decides.
No kernel may reach another device: no remote copies, remote signals or barrier semaphores. Data moves between devices by JAX's collectives and lax.ppermute only.
A program may use at most 64 MiB of HBM per device.

```python
import math
import jax
import jax.numpy as jnp

Z = 16
L = 4
NY = 16
NX = 1024


def block_scale(key, extent, shards, low, high):
    factor_of = 1.0
    for dim, parts in shards:
        draws = jax.random.uniform(jax.random.fold_in(jax.random.fold_in(key, 6), dim), (parts,), jnp.float32, low / len(shards), high / len(shards))
        factor_of = factor_of * jnp.repeat(jnp.exp(draws), extent[dim] // parts).reshape((-1,) + (1,) * (len(extent) - 1 - dim))
    return factor_of


def scatter_about(own_key, dims, scale, limit, shards=(), held_as=jnp.bfloat16):
    result = jax.random.normal(own_key, dims, jnp.float32) * scale
    if len(shards) > 0:
        result = block_scale(own_key, dims, shards, -0.22, 0.18) * result
    return jnp.clip(result, min=-limit, max=limit).astype(held_as)


def setup_inputs(seed: int = 0, part: int = 0) -> dict:
    key_list = jax.random.split(jax.random.key(seed), 4)
    own_keys = jax.random.split(jax.random.fold_in(key_list[3], part), 4)
    rhs = scatter_about(own_keys[0], (L, Z, NY, NX), 4.0, 24.0, ((0, 4), (2, 4)), jnp.float32)
    diffusivity = jnp.clip(jnp.exp(math.log(2.0) - 1.3862944 * jax.random.uniform(own_keys[1], (Z, NY, NX), jnp.float32) ** block_scale(own_keys[1], (Z, NY, NX), ((1, 4),), -0.2, 0.2)), 0.5, 2.0)
    velocity = jnp.clip(jax.random.uniform(own_keys[2], (3,), jnp.float32, -1.0, 1.0), -1.0, 1.0)
    return {"rhs": rhs, "diffusivity": diffusivity, "velocity": velocity}


circ_alpha = 0.1
relax_weights = (
    1.0 / (1.0 - 0.5 * math.cos(math.pi / 8.0)),
    1.0 / (1.0 - 0.5 * math.cos(3.0 * math.pi / 8.0)),
    1.0 / (1.0 - 0.5 * math.cos(5.0 * math.pi / 8.0)),
    1.0 / (1.0 - 0.5 * math.cos(7.0 * math.pi / 8.0)),
)


def stencil(extended, diffusivity, diag_re, diag_im, velocity):
    center = extended[:, :, :, 1:-1, :]
    upper_y = extended[:, :, :, 2:, :]
    lower_y = extended[:, :, :, :-2, :]
    zero_z = jnp.zeros_like(center[:, :, :1])
    upper_z = jnp.concatenate([center[:, :, 1:], zero_z], axis=2)
    lower_z = jnp.concatenate([zero_z, center[:, :, :-1]], axis=2)
    zero_x = jnp.zeros_like(center[:, :, :, :, :1])
    upper_x = jnp.concatenate([center[:, :, :, :, 1:], zero_x], axis=4)
    lower_x = jnp.concatenate([zero_x, center[:, :, :, :, :-1]], axis=4)
    coefficient = diffusivity[None, None]
    half_velocity = 0.5 * velocity
    beside = (coefficient - half_velocity[0]) * upper_z + (coefficient + half_velocity[0]) * lower_z
    beside = beside + (coefficient - half_velocity[1]) * upper_y + (coefficient + half_velocity[1]) * lower_y
    beside = beside + (coefficient - half_velocity[2]) * upper_x + (coefficient + half_velocity[2]) * lower_x
    denominator = diag_re + 6.0 * diffusivity
    center_re = center[:, 0]
    center_im = center[:, 1]
    total_re = denominator * center_re - diag_im * center_im
    total_im = denominator * center_im + diag_im * center_re
    return jnp.stack([total_re, total_im], axis=1) - beside


def divide(residual, diffusivity, diag_re, diag_im):
    denominator = diag_re + 6.0 * diffusivity
    modulus = denominator * denominator + diag_im * diag_im
    residual_re = residual[:, 0]
    residual_im = residual[:, 1]
    quotient_re = (residual_re * denominator + residual_im * diag_im) / modulus
    quotient_im = (residual_im * denominator - residual_re * diag_im) / modulus
    return jnp.stack([quotient_re, quotient_im], axis=1)


def reference(rhs, diffusivity, velocity):
    time_index = jnp.arange(L, dtype=jnp.float32)
    log_alpha = math.log(circ_alpha) / L
    scaled = rhs * jnp.exp(time_index * log_alpha)[:, None, None, None]
    spectrum = jnp.fft.fft(scaled, axis=0)
    source = jnp.stack([jnp.real(spectrum), jnp.imag(spectrum)], axis=1).astype(jnp.float32)
    phase_angle = time_index * (2.0 * math.pi / L)
    shift_factor = circ_alpha ** (1.0 / L)
    diag_re = (1.0 - shift_factor * jnp.cos(phase_angle))[:, None, None, None]
    diag_im = (shift_factor * jnp.sin(phase_angle))[:, None, None, None]
    field = relax_weights[0] * divide(source, diffusivity, diag_re, diag_im)
    for weight in relax_weights[1:]:
        extended = jnp.pad(field, ((0, 0), (0, 0), (0, 0), (1, 1), (0, 0)))
        applied = stencil(extended, diffusivity, diag_re, diag_im, velocity)
        field = field + weight * divide(source - applied, diffusivity, diag_re, diag_im)
    complex_field = field[:, 0] + 1j * field[:, 1]
    restored = jnp.real(jnp.fft.ifft(complex_field, axis=0))
    return (restored * jnp.exp(-time_index * log_alpha)[:, None, None, None]).astype(jnp.float32)
```

```python
import functools
import math

import jax
import jax.numpy as jnp
from jax import lax
from jax.experimental import pallas as pl
from jax.experimental.pallas import tpu as pltpu
from jax.sharding import PartitionSpec as P

circ_alpha = 0.1
relax_weights = (
    1.0 / (1.0 - 0.5 * math.cos(math.pi / 8.0)),
    1.0 / (1.0 - 0.5 * math.cos(3.0 * math.pi / 8.0)),
    1.0 / (1.0 - 0.5 * math.cos(5.0 * math.pi / 8.0)),
    1.0 / (1.0 - 0.5 * math.cos(7.0 * math.pi / 8.0)),
)


reach = len(relax_weights) - 1
lanes = 128
vmem = pl.BlockSpec(memory_space=pltpu.VMEM)
smem = pl.BlockSpec(memory_space=pltpu.SMEM)


def call(kernel, outs, *operands, specs=None, scratch=()):
    return pl.pallas_call(
        kernel,
        out_shape=[jax.ShapeDtypeStruct(o, jnp.float32) for o in outs],
        in_specs=specs or [vmem] * len(operands),
        out_specs=[vmem] * len(outs),
        scratch_shapes=scratch,
    )(*operands)


def column_mask(left, right, shape):
    lane = lax.broadcasted_iota(jnp.int32, shape, 1)
    keep_right = (lane < reach).astype(jnp.float32) * right
    keep_left = (lane >= lanes - reach).astype(jnp.float32) * left
    return keep_right, keep_left


def pick_block(source, write, owner, owners, depth, rows, tiles):
    total = owners * tiles
    left_tile = jnp.maximum(owner * tiles - 1, 0)
    right_tile = jnp.minimum((owner + 1) * tiles, total - 1)
    left = (owner > 0).astype(jnp.float32)
    right = (owner < owners - 1).astype(jnp.float32)
    keep_right, keep_left = column_mask(left, right, (depth, lanes))
    packed = None

    def tile_at(row, tile):
        return source[:, row, pl.ds(pl.multiple_of(tile * lanes, lanes), lanes)]

    for row in range(rows):
        for tile in range(tiles):
            write(row * tiles + tile, tile_at(row, owner * tiles + tile))
        halo = tile_at(row, right_tile) * keep_right + tile_at(row, left_tile) * keep_left
        if row:
            halo = pltpu.roll(halo, row * (lanes // rows), 1)
        packed = halo if packed is None else packed + halo
    write(rows * tiles, packed)


def pack_kernel(tm, log_alpha, steps, rhs, *outs):
    me = lax.axis_index(tm)
    depth, rows, columns = rhs.shape
    tiles = columns // steps // lanes
    scale = jnp.exp(jnp.full((depth, lanes), me.astype(jnp.float32) * log_alpha, jnp.float32))
    for ahead in range(steps):
        out = outs[ahead]

        def write(index, value, out=out):
            out[index] = value * scale

        pick_block(rhs, write, lax.rem(me + ahead, steps), steps, depth, rows, tiles)


def pack(rhs, steps):
    depth, rows, columns = rhs.shape
    tiles = columns // steps // lanes
    log_alpha = math.log(circ_alpha) / steps
    kernel = functools.partial(pack_kernel, "tm", log_alpha, steps)
    return call(kernel, [(rows * tiles + 1, depth, lanes)] * steps, rhs)


def halo_pieces(block, ahead, rows, tiles):
    first = (rows - reach) * tiles if ahead else 0
    return [first + i for i in range(reach * tiles)] + [rows * tiles]


def halo_kernel(rows, tiles, steps, *refs):
    blocks, (up, down) = refs[:steps], refs[steps:]
    piece = reach * tiles + 1
    for step, block in enumerate(blocks):
        for out, ahead in ((up, True), (down, False)):
            for place, index in enumerate(halo_pieces(block, ahead, rows, tiles)):
                out[step * piece + place] = block[index]


def halos(blocks, rows, tiles):
    depth = blocks[0].shape[1]
    out = (len(blocks) * (reach * tiles + 1), depth, lanes)
    kernel = functools.partial(halo_kernel, rows, tiles, len(blocks))
    return call(kernel, [out, out], *blocks)


def kappa_kernel(tm, rows, tiles, steps, kappa, own, up, down):
    me = lax.axis_index(tm)
    held = {}
    depth = kappa.shape[0]

    def write(index, value):
        own[index] = value
        held[index] = value

    pick_block(kappa, write, me, steps, depth, rows, tiles)
    for out, ahead in ((up, True), (down, False)):
        for place, index in enumerate(halo_pieces(own, ahead, rows, tiles)):
            out[place] = held[index]


def row_piece(own, below, above, step, row, tile, rows, tiles):
    piece = reach * tiles + 1
    if row < reach:
        source, base, local_row, place = below, step * piece, rows - reach + row, row
        packed = base + reach * tiles
    elif row < reach + rows:
        source, base, local_row, place = own, 0, row - reach, row - reach
        packed = rows * tiles
    else:
        source, base, local_row, place = above, step * piece, row - reach - rows, row - reach - rows
        packed = base + reach * tiles
    if tile < tiles:
        return source[base + place * tiles + tile]
    value = source[packed]
    shift = local_row * (lanes // rows)
    return pltpu.roll(value, lanes - shift, 1) if shift else value


def frequencies(steps):
    return [(k, 2 * k % steps != 0) for k in range(steps // 2 + 1)]


def coefficient_kernel(tm, space, rows, tiles, steps, own, below, above, kappa, *outs):
    me, slab = lax.axis_index(tm), lax.axis_index(space)
    slabs = lax.axis_size(space)
    depth = own.shape[1]
    keep_right, keep_left = column_mask(
        (me > 0).astype(jnp.float32), (me < steps - 1).astype(jnp.float32), (depth, lanes)
    )
    halo_mask = keep_right + keep_left
    shift_factor = circ_alpha ** (1.0 / steps)
    for row in range(rows + 2 * reach):
        inside = None
        if row < reach:
            inside = (slab > 0).astype(jnp.float32)
        elif row >= reach + rows:
            inside = (slab < slabs - 1).astype(jnp.float32)
        for tile in range(tiles + 1):
            value = row_piece(own, below, above, 0, row, tile, rows, tiles)
            kappa[row, tile] = value
            mask = halo_mask if tile == tiles else None
            if inside is not None:
                mask = mask * inside if mask is not None else jnp.full((depth, lanes), inside)
            place = 0
            for k, is_complex in frequencies(steps):
                phase = 2.0 * math.pi * k / steps
                real = (1.0 - shift_factor * math.cos(phase)) + 6.0 * value
                if is_complex:
                    imag = shift_factor * math.sin(phase)
                    inverse = 1.0 / (real * real + imag * imag)
                    pair = (real * inverse, imag * inverse)
                else:
                    pair = (1.0 / real,)
                for part in pair:
                    outs[0][place, row, tile] = part if mask is None else part * mask
                    place += 1


def combine(terms):
    total = None
    for factor, value in terms:
        if factor == 0.0:
            continue
        if total is None:
            total = value if factor == 1.0 else factor * value
        elif factor == 1.0:
            total = total + value
        elif factor == -1.0:
            total = total - value
        else:
            total = total + factor * value
    return total


def exact(value):
    return float(round(value)) if abs(value - round(value)) < 1e-12 else value


def cosine(product, steps):
    return exact(math.cos(2.0 * math.pi * (product % steps) / steps))


def sine(product, steps):
    return exact(math.sin(2.0 * math.pi * (product % steps) / steps))


def solve_kernel(rows, tiles, steps, *refs):
    blocks, refs = refs[:steps], refs[steps:]
    below, above, kappa, inverse, velocity = refs[:5]
    outs, (source, first, second) = refs[5 : 5 + steps], refs[5 + steps :]
    depth = blocks[0].shape[1]
    pad = 8
    middle = pl.ds(pad, depth)
    lane = lax.broadcasted_iota(jnp.int32, (depth, lanes), 1)
    at_first, at_last = lane == 0, lane == lanes - 1
    freqs = frequencies(steps)
    fields = sum(2 if c else 1 for _, c in freqs)
    half = [0.5 * velocity[j] for j in range(3)]
    extended = rows + 2 * reach
    wide = tiles + 1

    zero = jnp.zeros((8, lanes), jnp.float32)
    for ref in (first, second):
        for field in range(fields):
            for row in range(extended):
                for tile in range(wide):
                    ref[field, row, tile, pl.ds(0, 8), :] = zero
                    ref[field, row, tile, pl.ds(pad + depth, 8), :] = zero

    def divide(values, row, tile):
        result, place = [], 0
        for _, is_complex in freqs:
            if is_complex:
                re, im = values[place], values[place + 1]
                p, q = inverse[place, row, tile], inverse[place + 1, row, tile]
                result += [re * p + im * q, im * p - re * q]
                place += 2
            else:
                result.append(values[place] * inverse[place, row, tile])
                place += 1
        return result

    for row in range(extended):
        for tile in range(wide):
            if tile == tiles and not 1 <= row < extended - 1:
                continue
            held = [
                row_piece(blocks[b], below, above, b, row, tile, rows, tiles)
                for b in range(steps)
            ]
            values = []
            for k, is_complex in freqs:
                values.append(combine((cosine(k * b, steps), held[b]) for b in range(steps)))
                if is_complex:
                    values.append(combine((sine(k * b, steps), held[b]) for b in range(steps)))
            quotients = divide(values, row, tile)
            for field in range(fields):
                source[field, row, tile] = values[field]
                first[field, row, tile, middle, :] = relax_weights[0] * quotients[field]

    def sweep(row, old, weight, last):
        centers = [
            [old[field, row, tile, middle, :] for tile in range(wide)] for field in range(fields)
        ]
        shifted_down = [[pltpu.roll(c, 1, 1) for c in line] for line in centers]
        shifted_up = [[pltpu.roll(c, lanes - 1, 1) for c in line] for line in centers]
        for tile in range(tiles if last else wide):
            values = []
            coefficient = kappa[row, tile]
            for field in range(fields):
                lower_x = jnp.where(
                    at_first, shifted_down[field][(tile - 1) % wide], shifted_down[field][tile]
                )
                upper_x = jnp.where(
                    at_last, shifted_up[field][(tile + 1) % wide], shifted_up[field][tile]
                )
                lower_z = old[field, row, tile, pl.ds(pad - 1, depth), :]
                upper_z = old[field, row, tile, pl.ds(pad + 1, depth), :]
                lower_y = old[field, row - 1, tile, middle, :]
                upper_y = old[field, row + 1, tile, middle, :]
                around = (lower_z + upper_z) + (lower_y + upper_y) + (lower_x + upper_x)
                slope = (
                    half[0] * (lower_z - upper_z)
                    + half[1] * (lower_y - upper_y)
                    + half[2] * (lower_x - upper_x)
                )
                values.append(source[field, row, tile] + (coefficient * around + slope))
            quotients = divide(values, row, tile)
            yield tile, [
                (1.0 - weight) * centers[field][tile] + weight * quotients[field]
                for field in range(fields)
            ]

    def middle_level(level, old, new):
        def step(row, carry):
            for tile, results in sweep(row, old, relax_weights[level], False):
                for field in range(fields):
                    new[field, row, tile, middle, :] = results[field]
            return carry

        lax.fori_loop(level, extended - level, step, 0)

    middle_level(1, first, second)
    middle_level(2, second, first)

    def last_step(row, carry):
        for tile, results in sweep(row, first, relax_weights[reach], True):
            for ahead in range(steps):
                terms, place = [], 0
                for k, is_complex in freqs:
                    factor = (2.0 if is_complex else 1.0) / steps
                    terms.append((factor * cosine(k * ahead, steps), results[place]))
                    place += 1
                    if is_complex:
                        terms.append((-factor * sine(k * ahead, steps), results[place]))
                        place += 1
                outs[ahead][(row - reach) * tiles + tile] = combine(terms)
        return carry

    lax.fori_loop(reach, reach + rows, last_step, 0)


def unpack_kernel(tm, log_alpha, steps, *refs):
    blocks, out = refs[:steps], refs[steps]
    me = lax.axis_index(tm)
    depth, rows, columns = out.shape
    tiles = columns // steps // lanes
    scale = jnp.exp(jnp.full((depth, lanes), me.astype(jnp.float32) * -log_alpha, jnp.float32))
    for behind in range(steps):
        owner = lax.rem(me - behind + steps, steps)
        for row in range(rows):
            for tile in range(tiles):
                place = pl.multiple_of((owner * tiles + tile) * lanes, lanes)
                out[:, row, pl.ds(place, lanes)] = blocks[behind][row * tiles + tile] * scale


def exchange(blocks, steps):
    moved = [
        lax.ppermute(blocks[d], "tm", [(i, (i + d) % steps) for i in range(steps)])
        for d in range(1, steps)
    ]
    return [blocks[0]] + moved


def neighbours(up, down):
    size = lax.axis_size("space")
    ahead = [(i, i + 1) for i in range(size - 1)]
    return (
        lax.ppermute(up, "space", ahead),
        lax.ppermute(down, "space", [(j, i) for i, j in ahead]),
    )


def fast_local(rhs, diffusivity, velocity):
    _, depth, rows, columns = rhs.shape
    steps = lax.axis_size("tm")
    tiles = columns // steps // lanes
    log_alpha = math.log(circ_alpha) / steps
    extended, wide = rows + 2 * reach, tiles + 1
    fields = steps
    blocks = exchange(pack(rhs[0], steps), steps)
    piece = (reach * tiles + 1, depth, lanes)
    kappa_own, kappa_up, kappa_down = call(
        functools.partial(kappa_kernel, "tm", rows, tiles, steps),
        [(rows * tiles + 1, depth, lanes), piece, piece],
        diffusivity,
    )
    kappa_below, kappa_above = neighbours(kappa_up, kappa_down)
    kappa, inverse = call(
        functools.partial(coefficient_kernel, "tm", "space", rows, tiles, steps),
        [(extended, wide, depth, lanes), (fields, extended, wide, depth, lanes)],
        kappa_own,
        kappa_below,
        kappa_above,
    )
    below, above = neighbours(*halos(blocks, rows, tiles))
    padded = pltpu.VMEM((fields, extended, wide, depth + 16, lanes), jnp.float32)
    results = call(
        functools.partial(solve_kernel, rows, tiles, steps),
        [(rows * tiles, depth, lanes)] * steps,
        *blocks,
        below,
        above,
        kappa,
        inverse,
        velocity,
        specs=[vmem] * (steps + 4) + [smem],
        scratch=[
            pltpu.VMEM((fields, extended, wide, depth, lanes), jnp.float32),
            padded,
            padded,
        ],
    )
    returned = exchange(results, steps)
    (result,) = call(
        functools.partial(unpack_kernel, "tm", log_alpha, steps),
        [(depth, rows, columns)],
        *returned,
    )
    return result[None]


def padded(shard, sides, width):
    for axis, dim in sides:
        size, length = (lax.axis_size(axis), shard.shape[dim])
        up = [(i, (i + 1) % size) for i in range(size - 1)]
        down = [(j, i) for i, j in up]
        last = lax.slice_in_dim(shard, length - width, length, axis=dim)
        initial = lax.slice_in_dim(shard, 0, width, axis=dim)
        before = lax.ppermute(last, axis, up)
        after = lax.ppermute(initial, axis, down)
        shard = jnp.concatenate([before, shard, after], axis=dim)
    return shard


def stencil(extended, diffusivity, diag_re, diag_im, velocity):
    center = extended[:, :, :, 1:-1, :]
    upper_y = extended[:, :, :, 2:, :]
    lower_y = extended[:, :, :, :-2, :]
    zero_z = jnp.zeros_like(center[:, :, :1])
    upper_z = jnp.concatenate([center[:, :, 1:], zero_z], axis=2)
    lower_z = jnp.concatenate([zero_z, center[:, :, :-1]], axis=2)
    zero_x = jnp.zeros_like(center[:, :, :, :, :1])
    upper_x = jnp.concatenate([center[:, :, :, :, 1:], zero_x], axis=4)
    lower_x = jnp.concatenate([zero_x, center[:, :, :, :, :-1]], axis=4)
    coefficient = diffusivity[None, None]
    half_velocity = 0.5 * velocity
    beside = (coefficient - half_velocity[0]) * upper_z + (coefficient + half_velocity[0]) * lower_z
    beside = (
        beside
        + (coefficient - half_velocity[1]) * upper_y
        + (coefficient + half_velocity[1]) * lower_y
    )
    beside = (
        beside
        + (coefficient - half_velocity[2]) * upper_x
        + (coefficient + half_velocity[2]) * lower_x
    )
    denominator = diag_re + 6.0 * diffusivity
    center_re = center[:, 0]
    center_im = center[:, 1]
    total_re = denominator * center_re - diag_im * center_im
    total_im = denominator * center_im + diag_im * center_re
    return jnp.stack([total_re, total_im], axis=1) - beside


def divide(residual, diffusivity, diag_re, diag_im):
    denominator = diag_re + 6.0 * diffusivity
    modulus = denominator * denominator + diag_im * diag_im
    residual_re = residual[:, 0]
    residual_im = residual[:, 1]
    quotient_re = (residual_re * denominator + residual_im * diag_im) / modulus
    quotient_im = (residual_im * denominator - residual_re * diag_im) / modulus
    return jnp.stack([quotient_re, quotient_im], axis=1)


def highest(left, right):
    return jnp.dot(left, right, precision=lax.Precision.HIGHEST, preferred_element_type=jnp.float32)


def twiddle(row_index, column_index, length):
    product = row_index[:, None] * column_index[None, :] % length
    phase_table = product.astype(jnp.float32) * (2.0 * math.pi / length)
    return (jnp.cos(phase_table), jnp.sin(phase_table))


def general_local(rhs, diffusivity, velocity):
    local_steps, depth, rows_y, rows_x = rhs.shape
    length = local_steps * lax.axis_size("tm")
    first_step = lax.axis_index("tm") * local_steps
    own_index = first_step + jnp.arange(local_steps, dtype=jnp.int32)
    log_alpha = math.log(circ_alpha) / length
    cell_count = depth * rows_y * rows_x
    scaled = (
        rhs.reshape(local_steps, cell_count)
        * jnp.exp(own_index.astype(jnp.float32) * log_alpha)[:, None]
    )
    regrouped = lax.all_to_all(scaled, "tm", split_axis=1, concat_axis=0, tiled=True)
    full_index = jnp.arange(length, dtype=jnp.int32)
    cosine_table, sine_table = twiddle(full_index, full_index, length)
    spectrum_re = highest(cosine_table, regrouped)
    spectrum_im = -highest(sine_table, regrouped)
    source_re, source_im = (
        lax.all_to_all(spectrum_re, "tm", split_axis=0, concat_axis=1, tiled=True),
        lax.all_to_all(spectrum_im, "tm", split_axis=0, concat_axis=1, tiled=True),
    )
    source = jnp.stack([source_re, source_im], axis=1).reshape(
        local_steps, 2, depth, rows_y, rows_x
    )
    phase_angle = own_index.astype(jnp.float32) * (2.0 * math.pi / length)
    shift_factor = circ_alpha ** (1.0 / length)
    diag_re = (1.0 - shift_factor * jnp.cos(phase_angle))[:, None, None, None]
    diag_im = (shift_factor * jnp.sin(phase_angle))[:, None, None, None]
    field = relax_weights[0] * divide(source, diffusivity, diag_re, diag_im)
    for weight in relax_weights[1:]:
        extended = padded(field, (("space", 3),), 1)
        applied = stencil(extended, diffusivity, diag_re, diag_im, velocity)
        field = field + weight * divide(source - applied, diffusivity, diag_re, diag_im)
    field_re = field[:, 0].reshape(local_steps, cell_count)
    field_im = field[:, 1].reshape(local_steps, cell_count)
    mixed_re, mixed_im = (
        lax.all_to_all(field_re, "tm", split_axis=1, concat_axis=0, tiled=True),
        lax.all_to_all(field_im, "tm", split_axis=1, concat_axis=0, tiled=True),
    )
    values = (highest(cosine_table, mixed_re) - highest(sine_table, mixed_im)) / length
    restored = lax.all_to_all(values, "tm", split_axis=0, concat_axis=1, tiled=True)
    result = restored * jnp.exp(-own_index.astype(jnp.float32) * log_alpha)[:, None]
    return result.reshape(local_steps, depth, rows_y, rows_x)


def local(rhs, diffusivity, velocity):
    steps = lax.axis_size("tm")
    local_steps, depth, rows, columns = rhs.shape
    if local_steps == 1 and rows >= reach and lanes % rows == 0 and columns % (steps * lanes) == 0:
        return fast_local(rhs, diffusivity, velocity)
    return general_local(rhs, diffusivity, velocity)


def solution(mesh):
    return jax.shard_map(
        local,
        mesh=mesh,
        in_specs=(P(("parts", "tm"), None, "space", None), P("parts", "space", None), P("parts")),
        out_specs=P(("parts", "tm"), None, "space", None),
        check_vma=False,
    )
```

```python
import functools
import math

import jax
import jax.numpy as jnp
from jax import lax
from jax.experimental import pallas as pl
from jax.experimental.pallas import tpu as pltpu
from jax.sharding import PartitionSpec as P

circ_alpha = 0.1
relax_weights = (
    1.0 / (1.0 - 0.5 * math.cos(math.pi / 8.0)),
    1.0 / (1.0 - 0.5 * math.cos(3.0 * math.pi / 8.0)),
    1.0 / (1.0 - 0.5 * math.cos(5.0 * math.pi / 8.0)),
    1.0 / (1.0 - 0.5 * math.cos(7.0 * math.pi / 8.0)),
)


reach = len(relax_weights) - 1
lanes = 128
vmem = pl.BlockSpec(memory_space=pltpu.VMEM)
smem = pl.BlockSpec(memory_space=pltpu.SMEM)


def call(kernel, outs, *operands, from_hbm=0, kept=True, scratch=()):
    on_chip = [
        x if i < from_hbm or x.ndim == 1 else pltpu.with_memory_space_constraint(x, pltpu.VMEM)
        for i, x in enumerate(operands)
    ]
    make = pltpu.VMEM if kept else jax.ShapeDtypeStruct
    return pl.pallas_call(
        kernel,
        out_shape=[make(o, jnp.float32) for o in outs],
        in_specs=[smem if x.ndim == 1 else vmem for x in operands],
        out_specs=[vmem] * len(outs),
        scratch_shapes=scratch,
    )(*on_chip)


def column_mask(left, right, shape):
    lane = lax.broadcasted_iota(jnp.int32, shape, 1)
    keep_right = (lane < reach).astype(jnp.float32) * right
    keep_left = (lane >= lanes - reach).astype(jnp.float32) * left
    return keep_right, keep_left


def pick_block(source, write, owner, owners, depth, rows, tiles):
    total = owners * tiles
    left_tile = jnp.maximum(owner * tiles - 1, 0)
    right_tile = jnp.minimum((owner + 1) * tiles, total - 1)
    left = (owner > 0).astype(jnp.float32)
    right = (owner < owners - 1).astype(jnp.float32)
    keep_right, keep_left = column_mask(left, right, (depth, lanes))
    packed = None

    def tile_at(row, tile):
        return source[:, row, pl.ds(pl.multiple_of(tile * lanes, lanes), lanes)]

    for row in range(rows):
        for tile in range(tiles):
            write(row * tiles + tile, tile_at(row, owner * tiles + tile))
        halo = tile_at(row, right_tile) * keep_right + tile_at(row, left_tile) * keep_left
        if row:
            halo = pltpu.roll(halo, row * (lanes // rows), 1)
        packed = halo if packed is None else packed + halo
    write(rows * tiles, packed)


def pack_kernel(tm, log_alpha, steps, rhs, *outs):
    me = lax.axis_index(tm)
    depth, rows, columns = rhs.shape
    tiles = columns // steps // lanes
    scale = jnp.exp(jnp.full((depth, lanes), me.astype(jnp.float32) * log_alpha, jnp.float32))
    for ahead in range(steps):
        out = outs[ahead]

        def write(index, value, out=out):
            out[index] = value * scale

        pick_block(rhs, write, lax.rem(me + ahead, steps), steps, depth, rows, tiles)


def pack(rhs, steps):
    depth, rows, columns = rhs.shape
    tiles = columns // steps // lanes
    log_alpha = math.log(circ_alpha) / steps
    kernel = functools.partial(pack_kernel, "tm", log_alpha, steps)
    return call(kernel, [(rows * tiles + 1, depth, lanes)] * steps, rhs, from_hbm=1)


def halo_pieces(block, ahead, rows, tiles):
    first = (rows - reach) * tiles if ahead else 0
    return [first + i for i in range(reach * tiles)] + [rows * tiles]


def halo_kernel(rows, tiles, steps, *refs):
    blocks, (_, up, down) = refs[:steps], refs[steps:]
    piece = reach * tiles + 1
    for step, block in enumerate(blocks):
        for out, ahead in ((up, True), (down, False)):
            for place, index in enumerate(halo_pieces(block, ahead, rows, tiles)):
                out[step * piece + place] = block[index]


def halos(blocks, ready, rows, tiles):
    depth = blocks[0].shape[1]
    out = (len(blocks) * (reach * tiles + 1), depth, lanes)
    kernel = functools.partial(halo_kernel, rows, tiles, len(blocks))
    return call(kernel, [out, out], *blocks, ready)


def kappa_kernel(tm, rows, tiles, steps, kappa, own, up, down):
    me = lax.axis_index(tm)
    held = {}
    depth = kappa.shape[0]

    def write(index, value):
        own[index] = value
        held[index] = value

    pick_block(kappa, write, me, steps, depth, rows, tiles)
    for out, ahead in ((up, True), (down, False)):
        for place, index in enumerate(halo_pieces(own, ahead, rows, tiles)):
            out[place] = held[index]


def row_piece(own, below, above, step, row, tile, rows, tiles):
    piece = reach * tiles + 1
    if row < reach:
        source, base, local_row, place = below, step * piece, rows - reach + row, row
        packed = base + reach * tiles
    elif row < reach + rows:
        source, base, local_row, place = own, 0, row - reach, row - reach
        packed = rows * tiles
    else:
        source, base, local_row, place = above, step * piece, row - reach - rows, row - reach - rows
        packed = base + reach * tiles
    if tile < tiles:
        return source[base + place * tiles + tile]
    value = source[packed]
    shift = local_row * (lanes // rows)
    return pltpu.roll(value, lanes - shift, 1) if shift else value


def frequencies(steps):
    return [(k, 2 * k % steps != 0) for k in range(steps // 2 + 1)]


def coefficient_kernel(tm, space, rows, tiles, steps, own, below, above, kappa, *outs):
    me, slab = lax.axis_index(tm), lax.axis_index(space)
    slabs = lax.axis_size(space)
    depth = own.shape[1]
    keep_right, keep_left = column_mask(
        (me > 0).astype(jnp.float32), (me < steps - 1).astype(jnp.float32), (depth, lanes)
    )
    halo_mask = keep_right + keep_left
    shift_factor = circ_alpha ** (1.0 / steps)
    for row in range(rows + 2 * reach):
        inside = None
        if row < reach:
            inside = (slab > 0).astype(jnp.float32)
        elif row >= reach + rows:
            inside = (slab < slabs - 1).astype(jnp.float32)
        for tile in range(tiles + 1):
            value = row_piece(own, below, above, 0, row, tile, rows, tiles)
            kappa[row, tile] = value
            mask = halo_mask if tile == tiles else None
            if inside is not None:
                mask = mask * inside if mask is not None else jnp.full((depth, lanes), inside)
            place = 0
            for k, is_complex in frequencies(steps):
                phase = 2.0 * math.pi * k / steps
                real = (1.0 - shift_factor * math.cos(phase)) + 6.0 * value
                if is_complex:
                    imag = shift_factor * math.sin(phase)
                    inverse = 1.0 / (real * real + imag * imag)
                    pair = (real * inverse, imag * inverse)
                else:
                    pair = (1.0 / real,)
                for part in pair:
                    outs[0][place, row, tile] = part if mask is None else part * mask
                    place += 1


def combine(terms):
    total = None
    for factor, value in terms:
        if factor == 0.0:
            continue
        if total is None:
            total = value if factor == 1.0 else factor * value
        elif factor == 1.0:
            total = total + value
        elif factor == -1.0:
            total = total - value
        else:
            total = total + factor * value
    return total


def exact(value):
    return float(round(value)) if abs(value - round(value)) < 1e-12 else value


def cosine(product, steps):
    return exact(math.cos(2.0 * math.pi * (product % steps) / steps))


def sine(product, steps):
    return exact(math.sin(2.0 * math.pi * (product % steps) / steps))


def solve_kernel(rows, tiles, steps, *refs):
    blocks, refs = refs[:steps], refs[steps:]
    below, above, kappa, inverse, velocity = refs[:5]
    outs, (source, first, second) = refs[5 : 5 + steps], refs[5 + steps :]
    depth = blocks[0].shape[1]
    pad = 8
    middle = pl.ds(pad, depth)
    lane = lax.broadcasted_iota(jnp.int32, (depth, lanes), 1)
    at_first, at_last = lane == 0, lane == lanes - 1
    freqs = frequencies(steps)
    fields = sum(2 if c else 1 for _, c in freqs)
    half = [0.5 * velocity[j] for j in range(3)]
    extended = rows + 2 * reach
    wide = tiles + 1

    zero = jnp.zeros((8, lanes), jnp.float32)
    for ref in (first, second):
        for field in range(fields):
            for row in range(extended):
                for tile in range(wide):
                    ref[field, row, tile, pl.ds(0, 8), :] = zero
                    ref[field, row, tile, pl.ds(pad + depth, 8), :] = zero

    def divide(values, row, tile):
        result, place = [], 0
        for _, is_complex in freqs:
            if is_complex:
                re, im = values[place], values[place + 1]
                p, q = inverse[place, row, tile], inverse[place + 1, row, tile]
                result += [re * p + im * q, im * p - re * q]
                place += 2
            else:
                result.append(values[place] * inverse[place, row, tile])
                place += 1
        return result

    for row in range(extended):
        for tile in range(wide):
            if tile == tiles and not 1 <= row < extended - 1:
                continue
            held = [
                row_piece(blocks[b], below, above, b, row, tile, rows, tiles)
                for b in range(steps)
            ]
            values = []
            for k, is_complex in freqs:
                values.append(combine((cosine(k * b, steps), held[b]) for b in range(steps)))
                if is_complex:
                    values.append(combine((sine(k * b, steps), held[b]) for b in range(steps)))
            quotients = divide(values, row, tile)
            for field in range(fields):
                source[field, row, tile] = values[field]
                first[field, row, tile, middle, :] = relax_weights[0] * quotients[field]

    def sweep(row, old, weight, last):
        centers = [
            [old[field, row, tile, middle, :] for tile in range(wide)] for field in range(fields)
        ]
        shifted_down = [[pltpu.roll(c, 1, 1) for c in line] for line in centers]
        shifted_up = [[pltpu.roll(c, lanes - 1, 1) for c in line] for line in centers]
        for tile in range(tiles if last else wide):
            values = []
            coefficient = kappa[row, tile]
            for field in range(fields):
                lower_x = jnp.where(
                    at_first, shifted_down[field][(tile - 1) % wide], shifted_down[field][tile]
                )
                upper_x = jnp.where(
                    at_last, shifted_up[field][(tile + 1) % wide], shifted_up[field][tile]
                )
                lower_z = old[field, row, tile, pl.ds(pad - 1, depth), :]
                upper_z = old[field, row, tile, pl.ds(pad + 1, depth), :]
                lower_y = old[field, row - 1, tile, middle, :]
                upper_y = old[field, row + 1, tile, middle, :]
                around = (lower_z + upper_z) + (lower_y + upper_y) + (lower_x + upper_x)
                slope = (
                    half[0] * (lower_z - upper_z)
                    + half[1] * (lower_y - upper_y)
                    + half[2] * (lower_x - upper_x)
                )
                values.append(source[field, row, tile] + (coefficient * around + slope))
            quotients = divide(values, row, tile)
            yield tile, [
                (1.0 - weight) * centers[field][tile] + weight * quotients[field]
                for field in range(fields)
            ]

    def middle_level(level, old, new):
        def step(row, carry):
            for tile, results in sweep(row, old, relax_weights[level], False):
                for field in range(fields):
                    new[field, row, tile, middle, :] = results[field]
            return carry

        lax.fori_loop(level, extended - level, step, 0)

    middle_level(1, first, second)
    middle_level(2, second, first)

    def last_step(row, carry):
        for tile, results in sweep(row, first, relax_weights[reach], True):
            for ahead in range(steps):
                terms, place = [], 0
                for k, is_complex in freqs:
                    factor = (2.0 if is_complex else 1.0) / steps
                    terms.append((factor * cosine(k * ahead, steps), results[place]))
                    place += 1
                    if is_complex:
                        terms.append((-factor * sine(k * ahead, steps), results[place]))
                        place += 1
                outs[ahead][(row - reach) * tiles + tile] = combine(terms)
        return carry

    lax.fori_loop(reach, reach + rows, last_step, 0)


def unpack_kernel(tm, log_alpha, steps, *refs):
    blocks, out = refs[:steps], refs[steps]
    me = lax.axis_index(tm)
    depth, rows, columns = out.shape
    tiles = columns // steps // lanes
    scale = jnp.exp(jnp.full((depth, lanes), me.astype(jnp.float32) * -log_alpha, jnp.float32))
    for behind in range(steps):
        owner = lax.rem(me - behind + steps, steps)
        for row in range(rows):
            for tile in range(tiles):
                place = pl.multiple_of((owner * tiles + tile) * lanes, lanes)
                out[:, row, pl.ds(place, lanes)] = blocks[behind][row * tiles + tile] * scale


def exchange(blocks, steps):
    moved = [
        lax.ppermute(blocks[d], "tm", [(i, (i + d) % steps) for i in range(steps)])
        for d in range(1, steps)
    ]
    return [blocks[0]] + moved


def neighbours(up, down):
    size = lax.axis_size("space")
    ahead = [(i, i + 1) for i in range(size - 1)]
    return (
        lax.ppermute(up, "space", ahead),
        lax.ppermute(down, "space", [(j, i) for i, j in ahead]),
    )


def fast_local(rhs, diffusivity, velocity):
    _, depth, rows, columns = rhs.shape
    steps = lax.axis_size("tm")
    tiles = columns // steps // lanes
    log_alpha = math.log(circ_alpha) / steps
    extended, wide = rows + 2 * reach, tiles + 1
    fields = steps
    blocks = exchange(pack(rhs[0], steps), steps)
    piece = (reach * tiles + 1, depth, lanes)
    kappa_own, kappa_up, kappa_down = call(
        functools.partial(kappa_kernel, "tm", rows, tiles, steps),
        [(rows * tiles + 1, depth, lanes), piece, piece],
        diffusivity,
        from_hbm=1,
    )
    kappa_below, kappa_above = neighbours(kappa_up, kappa_down)
    kappa, inverse = call(
        functools.partial(coefficient_kernel, "tm", "space", rows, tiles, steps),
        [(extended, wide, depth, lanes), (fields, extended, wide, depth, lanes)],
        kappa_own,
        kappa_below,
        kappa_above,
    )
    below, above = neighbours(*halos(blocks, kappa, rows, tiles))
    padded = pltpu.VMEM((fields, extended, wide, depth + 16, lanes), jnp.float32)
    results = call(
        functools.partial(solve_kernel, rows, tiles, steps),
        [(rows * tiles, depth, lanes)] * steps,
        *blocks,
        below,
        above,
        kappa,
        inverse,
        velocity,
        scratch=[
            pltpu.VMEM((fields, extended, wide, depth, lanes), jnp.float32),
            padded,
            padded,
        ],
    )
    returned = exchange(results, steps)
    (result,) = call(
        functools.partial(unpack_kernel, "tm", log_alpha, steps),
        [(depth, rows, columns)],
        *returned,
        kept=False,
    )
    return result[None]


def padded(shard, sides, width):
    for axis, dim in sides:
        size, length = (lax.axis_size(axis), shard.shape[dim])
        up = [(i, (i + 1) % size) for i in range(size - 1)]
        down = [(j, i) for i, j in up]
        last = lax.slice_in_dim(shard, length - width, length, axis=dim)
        initial = lax.slice_in_dim(shard, 0, width, axis=dim)
        before = lax.ppermute(last, axis, up)
        after = lax.ppermute(initial, axis, down)
        shard = jnp.concatenate([before, shard, after], axis=dim)
    return shard


def stencil(extended, diffusivity, diag_re, diag_im, velocity):
    center = extended[:, :, :, 1:-1, :]
    upper_y = extended[:, :, :, 2:, :]
    lower_y = extended[:, :, :, :-2, :]
    zero_z = jnp.zeros_like(center[:, :, :1])
    upper_z = jnp.concatenate([center[:, :, 1:], zero_z], axis=2)
    lower_z = jnp.concatenate([zero_z, center[:, :, :-1]], axis=2)
    zero_x = jnp.zeros_like(center[:, :, :, :, :1])
    upper_x = jnp.concatenate([center[:, :, :, :, 1:], zero_x], axis=4)
    lower_x = jnp.concatenate([zero_x, center[:, :, :, :, :-1]], axis=4)
    coefficient = diffusivity[None, None]
    half_velocity = 0.5 * velocity
    beside = (coefficient - half_velocity[0]) * upper_z + (coefficient + half_velocity[0]) * lower_z
    beside = (
        beside
        + (coefficient - half_velocity[1]) * upper_y
        + (coefficient + half_velocity[1]) * lower_y
    )
    beside = (
        beside
        + (coefficient - half_velocity[2]) * upper_x
        + (coefficient + half_velocity[2]) * lower_x
    )
    denominator = diag_re + 6.0 * diffusivity
    center_re = center[:, 0]
    center_im = center[:, 1]
    total_re = denominator * center_re - diag_im * center_im
    total_im = denominator * center_im + diag_im * center_re
    return jnp.stack([total_re, total_im], axis=1) - beside


def divide(residual, diffusivity, diag_re, diag_im):
    denominator = diag_re + 6.0 * diffusivity
    modulus = denominator * denominator + diag_im * diag_im
    residual_re = residual[:, 0]
    residual_im = residual[:, 1]
    quotient_re = (residual_re * denominator + residual_im * diag_im) / modulus
    quotient_im = (residual_im * denominator - residual_re * diag_im) / modulus
    return jnp.stack([quotient_re, quotient_im], axis=1)


def highest(left, right):
    return jnp.dot(left, right, precision=lax.Precision.HIGHEST, preferred_element_type=jnp.float32)


def twiddle(row_index, column_index, length):
    product = row_index[:, None] * column_index[None, :] % length
    phase_table = product.astype(jnp.float32) * (2.0 * math.pi / length)
    return (jnp.cos(phase_table), jnp.sin(phase_table))


def general_local(rhs, diffusivity, velocity):
    local_steps, depth, rows_y, rows_x = rhs.shape
    length = local_steps * lax.axis_size("tm")
    first_step = lax.axis_index("tm") * local_steps
    own_index = first_step + jnp.arange(local_steps, dtype=jnp.int32)
    log_alpha = math.log(circ_alpha) / length
    cell_count = depth * rows_y * rows_x
    scaled = (
        rhs.reshape(local_steps, cell_count)
        * jnp.exp(own_index.astype(jnp.float32) * log_alpha)[:, None]
    )
    regrouped = lax.all_to_all(scaled, "tm", split_axis=1, concat_axis=0, tiled=True)
    full_index = jnp.arange(length, dtype=jnp.int32)
    cosine_table, sine_table = twiddle(full_index, full_index, length)
    spectrum_re = highest(cosine_table, regrouped)
    spectrum_im = -highest(sine_table, regrouped)
    source_re, source_im = (
        lax.all_to_all(spectrum_re, "tm", split_axis=0, concat_axis=1, tiled=True),
        lax.all_to_all(spectrum_im, "tm", split_axis=0, concat_axis=1, tiled=True),
    )
    source = jnp.stack([source_re, source_im], axis=1).reshape(
        local_steps, 2, depth, rows_y, rows_x
    )
    phase_angle = own_index.astype(jnp.float32) * (2.0 * math.pi / length)
    shift_factor = circ_alpha ** (1.0 / length)
    diag_re = (1.0 - shift_factor * jnp.cos(phase_angle))[:, None, None, None]
    diag_im = (shift_factor * jnp.sin(phase_angle))[:, None, None, None]
    field = relax_weights[0] * divide(source, diffusivity, diag_re, diag_im)
    for weight in relax_weights[1:]:
        extended = padded(field, (("space", 3),), 1)
        applied = stencil(extended, diffusivity, diag_re, diag_im, velocity)
        field = field + weight * divide(source - applied, diffusivity, diag_re, diag_im)
    field_re = field[:, 0].reshape(local_steps, cell_count)
    field_im = field[:, 1].reshape(local_steps, cell_count)
    mixed_re, mixed_im = (
        lax.all_to_all(field_re, "tm", split_axis=1, concat_axis=0, tiled=True),
        lax.all_to_all(field_im, "tm", split_axis=1, concat_axis=0, tiled=True),
    )
    values = (highest(cosine_table, mixed_re) - highest(sine_table, mixed_im)) / length
    restored = lax.all_to_all(values, "tm", split_axis=0, concat_axis=1, tiled=True)
    result = restored * jnp.exp(-own_index.astype(jnp.float32) * log_alpha)[:, None]
    return result.reshape(local_steps, depth, rows_y, rows_x)


def local(rhs, diffusivity, velocity):
    steps = lax.axis_size("tm")
    local_steps, depth, rows, columns = rhs.shape
    if local_steps == 1 and rows >= reach and lanes % rows == 0 and columns % (steps * lanes) == 0:
        return fast_local(rhs, diffusivity, velocity)
    return general_local(rhs, diffusivity, velocity)


def solution(mesh):
    return jax.shard_map(
        local,
        mesh=mesh,
        in_specs=(P(("parts", "tm"), None, "space", None), P("parts", "space", None), P("parts")),
        out_specs=P(("parts", "tm"), None, "space", None),
        check_vma=False,
    )
```

```python
import functools
import math

import jax
import jax.numpy as jnp
from jax import lax
from jax.experimental import pallas as pl
from jax.experimental.pallas import tpu as pltpu
from jax.sharding import PartitionSpec as P

circ_alpha = 0.1
relax_weights = (
    1.0 / (1.0 - 0.5 * math.cos(math.pi / 8.0)),
    1.0 / (1.0 - 0.5 * math.cos(3.0 * math.pi / 8.0)),
    1.0 / (1.0 - 0.5 * math.cos(5.0 * math.pi / 8.0)),
    1.0 / (1.0 - 0.5 * math.cos(7.0 * math.pi / 8.0)),
)


reach = len(relax_weights) - 1
lanes = 128
vmem = pl.BlockSpec(memory_space=pltpu.VMEM)
smem = pl.BlockSpec(memory_space=pltpu.SMEM)


def call(kernel, outs, *operands, from_hbm=0, kept=True, aliases=None):
    on_chip = [
        x if i < from_hbm or x.ndim == 1 else pltpu.with_memory_space_constraint(x, pltpu.VMEM)
        for i, x in enumerate(operands)
    ]
    make = pltpu.VMEM if kept else jax.ShapeDtypeStruct
    return pl.pallas_call(
        kernel,
        out_shape=[make(o, jnp.float32) for o in outs],
        in_specs=[smem if x.ndim == 1 else vmem for x in operands],
        out_specs=[vmem] * len(outs),
        input_output_aliases=aliases or {},
        compiler_params=pltpu.CompilerParams(vmem_limit_bytes=16 << 20),
    )(*on_chip)


def column_mask(left, right, shape):
    lane = lax.broadcasted_iota(jnp.int32, shape, 1)
    keep_right = (lane < reach).astype(jnp.float32) * right
    keep_left = (lane >= lanes - reach).astype(jnp.float32) * left
    return keep_right, keep_left


def upwards(space):
    return lax.rem(lax.axis_index(space), 2)


def row_of(y, rows, up):
    return up * y + (1 - up) * (rows - 1 - y)


def pick_block(source, write, owner, owners, up):
    depth, rows, columns = source.shape
    total = columns // lanes
    tiles = total // owners
    left_tile = jnp.maximum(owner * tiles - 1, 0)
    right_tile = jnp.minimum((owner + 1) * tiles, total - 1)
    left = (owner > 0).astype(jnp.float32)
    right = (owner < owners - 1).astype(jnp.float32)
    keep_right, keep_left = column_mask(left, right, (depth, lanes))
    packed = None

    def tile_at(y, tile):
        return source[:, y, pl.ds(pl.multiple_of(tile * lanes, lanes), lanes)]

    for y in range(rows):
        row = row_of(y, rows, up)
        for tile in range(tiles):
            write(row * tiles + tile, tile_at(y, owner * tiles + tile))
        halo = tile_at(y, right_tile) * keep_right + tile_at(y, left_tile) * keep_left
        halo = pltpu.roll(halo, row * (lanes // rows), 1)
        packed = halo if packed is None else packed + halo
    write(rows * tiles, packed)


def pack_kernel(tm, space, log_alpha, steps, rhs, *outs):
    me, up = lax.axis_index(tm), upwards(space)
    depth = rhs.shape[0]
    scale = jnp.exp(jnp.full((depth, lanes), me.astype(jnp.float32) * log_alpha, jnp.float32))
    for ahead in range(steps):
        out = outs[ahead]

        def write(index, value, out=out):
            out[index] = value * scale

        pick_block(rhs, write, lax.rem(me + ahead, steps), steps, up)


def pack(rhs, steps):
    depth, rows, columns = rhs.shape
    tiles = columns // steps // lanes
    log_alpha = math.log(circ_alpha) / steps
    kernel = functools.partial(pack_kernel, "tm", "space", log_alpha, steps)
    return call(kernel, [(rows * tiles + 1, depth, lanes)] * steps, rhs, from_hbm=1)


def first_row(near, rows):
    return 0 if near else rows - reach


def halo_kernel(rows, tiles, steps, *refs):
    blocks, (_, near, far) = refs[:steps], refs[steps:]
    piece = reach * tiles + 1
    for step, block in enumerate(blocks):
        for out, is_near in ((near, True), (far, False)):
            start = first_row(is_near, rows) * tiles
            for place in range(reach * tiles):
                out[step * piece + place] = block[start + place]
            out[step * piece + reach * tiles] = block[rows * tiles]


def halos(blocks, ready, rows, tiles):
    depth = blocks[0].shape[1]
    out = (len(blocks) * (reach * tiles + 1), depth, lanes)
    kernel = functools.partial(halo_kernel, rows, tiles, len(blocks))
    return call(kernel, [out, out], *blocks, ready)


def kappa_kernel(tm, space, rows, tiles, steps, kappa, own, near, far):
    me, up = lax.axis_index(tm), upwards(space)

    def write(index, value):
        own[index] = value

    pick_block(kappa, write, me, steps, up)
    for out, is_near in ((near, True), (far, False)):
        start = first_row(is_near, rows) * tiles
        for place in range(reach * tiles):
            out[place] = own[start + place]
        out[reach * tiles] = own[rows * tiles]


def row_piece(own, near, far, step, row, tile, rows, tiles):
    piece = reach * tiles + 1
    if row < reach:
        source, base, there, start = near, step * piece, reach - 1 - row, 0
        packed = base + reach * tiles
    elif row < reach + rows:
        source, base, there, start = own, 0, row - reach, 0
        packed = rows * tiles
    else:
        source, base, there = far, step * piece, 2 * rows + reach - 1 - row
        start = rows - reach
        packed = base + reach * tiles
    if tile < tiles:
        return source[base + (there - start) * tiles + tile]
    value = source[packed]
    shift = there * (lanes // rows)
    return pltpu.roll(value, lanes - shift, 1) if shift else value


def frequencies(steps):
    return [(k, 2 * k % steps != 0) for k in range(steps // 2 + 1)]


def coefficient_kernel(tm, space, rows, tiles, steps, own, near, far, kappa, inverse):
    me, slab, up = lax.axis_index(tm), lax.axis_index(space), upwards(space)
    slabs = lax.axis_size(space)
    depth = own.shape[1]
    keep_right, keep_left = column_mask(
        (me > 0).astype(jnp.float32), (me < steps - 1).astype(jnp.float32), (depth, lanes)
    )
    halo_mask = keep_right + keep_left
    shift_factor = circ_alpha ** (1.0 / steps)
    has_lower, has_upper = slab > 0, slab < slabs - 1
    has_near = jnp.where(up == 1, has_lower, has_upper).astype(jnp.float32)
    has_far = jnp.where(up == 1, has_upper, has_lower).astype(jnp.float32)
    for row in range(rows + 2 * reach):
        inside = has_near if row < reach else has_far if row >= reach + rows else None
        for tile in range(tiles + 1):
            value = row_piece(own, near, far, 0, row, tile, rows, tiles)
            kappa[row, tile] = value
            mask = halo_mask if tile == tiles else None
            if inside is not None:
                mask = mask * inside if mask is not None else jnp.full((depth, lanes), inside)
            place = 0
            for k, is_complex in frequencies(steps):
                phase = 2.0 * math.pi * k / steps
                real = (1.0 - shift_factor * math.cos(phase)) + 6.0 * value
                if is_complex:
                    imag = shift_factor * math.sin(phase)
                    reciprocal = 1.0 / (real * real + imag * imag)
                    pair = (real * reciprocal, imag * reciprocal)
                else:
                    pair = (1.0 / real,)
                for part in pair:
                    inverse[place, row, tile] = part if mask is None else part * mask
                    place += 1


def combine(terms):
    total = None
    for factor, value in terms:
        if factor == 0.0:
            continue
        if total is None:
            total = value if factor == 1.0 else factor * value
        elif factor == 1.0:
            total = total + value
        elif factor == -1.0:
            total = total - value
        else:
            total = total + factor * value
    return total


def exact(value):
    return float(round(value)) if abs(value - round(value)) < 1e-12 else value


def cosine(product, steps):
    return exact(math.cos(2.0 * math.pi * (product % steps) / steps))


def sine(product, steps):
    return exact(math.sin(2.0 * math.pi * (product % steps) / steps))


def solve_kernel(space, rows, tiles, steps, second_half, *refs):
    freqs = frequencies(steps)
    fields = sum(2 if c else 1 for _, c in freqs)
    levels = reach
    if second_half:
        far, kappa, inverse, velocity = refs[:4]
        refs = refs[5 + levels + steps :]
        source, *iterates = refs[: 1 + levels]
        outs = refs[1 + levels :]
        blocks, near = [None] * steps, None
    else:
        blocks, (near, kappa, inverse, velocity) = refs[:steps], refs[steps : steps + 4]
        source, *iterates = refs[steps + 4 : steps + 5 + levels]
        outs = refs[steps + 5 + levels :]
        far = None
    depth = kappa.shape[2]
    pad = 8
    middle = pl.ds(pad, depth)
    lane = lax.broadcasted_iota(jnp.int32, (depth, lanes), 1)
    at_first, at_last = lane == 0, lane == lanes - 1
    direction = (2 * upwards(space) - 1).astype(jnp.float32)
    half = [0.5 * velocity[0], 0.5 * direction * velocity[1], 0.5 * velocity[2]]
    known = reach + rows
    extended = known + reach
    wide = tiles + 1

    def rows_of(level):
        split = known - level
        return (split, extended - level) if second_half else (level, split)

    if not second_half:
        zero = jnp.zeros((8, lanes), jnp.float32)
        for level, ref in enumerate(iterates):
            for field in range(fields):
                for row in range(level, extended - level):
                    for tile in range(wide):
                        ref[field, row, tile, pl.ds(0, 8), :] = zero
                        ref[field, row, tile, pl.ds(pad + depth, 8), :] = zero

    def divide(values, row, tile):
        result, place = [], 0
        for _, is_complex in freqs:
            if is_complex:
                re, im = values[place], values[place + 1]
                p, q = inverse[place, row, tile], inverse[place + 1, row, tile]
                result += [re * p + im * q, im * p - re * q]
                place += 2
            else:
                result.append(values[place] * inverse[place, row, tile])
                place += 1
        return result

    for row in range(*rows_of(0)):
        for tile in range(wide):
            if tile == tiles and not 1 <= row < extended - 1:
                continue
            held = [
                row_piece(blocks[b], near, far, b, row, tile, rows, tiles) for b in range(steps)
            ]
            values = []
            for k, is_complex in freqs:
                values.append(combine((cosine(k * b, steps), held[b]) for b in range(steps)))
                if is_complex:
                    values.append(combine((sine(k * b, steps), held[b]) for b in range(steps)))
            quotients = divide(values, row, tile)
            for field in range(fields):
                source[field, row, tile] = values[field]
                iterates[0][field, row, tile, middle, :] = relax_weights[0] * quotients[field]

    def sweep(row, old, weight, last):
        centers = [
            [old[field, row, tile, middle, :] for tile in range(wide)] for field in range(fields)
        ]
        shifted_down = [[pltpu.roll(c, 1, 1) for c in line] for line in centers]
        shifted_up = [[pltpu.roll(c, lanes - 1, 1) for c in line] for line in centers]
        for tile in range(tiles if last else wide):
            values = []
            coefficient = kappa[row, tile]
            for field in range(fields):
                lower_x = jnp.where(
                    at_first, shifted_down[field][(tile - 1) % wide], shifted_down[field][tile]
                )
                upper_x = jnp.where(
                    at_last, shifted_up[field][(tile + 1) % wide], shifted_up[field][tile]
                )
                lower_z = old[field, row, tile, pl.ds(pad - 1, depth), :]
                upper_z = old[field, row, tile, pl.ds(pad + 1, depth), :]
                lower_y = old[field, row - 1, tile, middle, :]
                upper_y = old[field, row + 1, tile, middle, :]
                around = (lower_z + upper_z) + (lower_y + upper_y) + (lower_x + upper_x)
                slope = (
                    half[0] * (lower_z - upper_z)
                    + half[1] * (lower_y - upper_y)
                    + half[2] * (lower_x - upper_x)
                )
                values.append(source[field, row, tile] + (coefficient * around + slope))
            quotients = divide(values, row, tile)
            yield tile, [
                (1.0 - weight) * centers[field][tile] + weight * quotients[field]
                for field in range(fields)
            ]

    for level in range(1, levels):

        def step(row, carry, level=level):
            for tile, results in sweep(row, iterates[level - 1], relax_weights[level], False):
                for field in range(fields):
                    iterates[level][field, row, tile, middle, :] = results[field]
            return carry

        lax.fori_loop(*rows_of(level), step, 0)

    def last_step(row, carry):
        for tile, results in sweep(row, iterates[levels - 1], relax_weights[levels], True):
            for ahead in range(steps):
                terms, place = [], 0
                for k, is_complex in freqs:
                    factor = (2.0 if is_complex else 1.0) / steps
                    terms.append((factor * cosine(k * ahead, steps), results[place]))
                    place += 1
                    if is_complex:
                        terms.append((-factor * sine(k * ahead, steps), results[place]))
                        place += 1
                outs[ahead][(row - reach) * tiles + tile] = combine(terms)
        return carry

    lax.fori_loop(*rows_of(levels), last_step, 0)


def unpack_kernel(tm, space, log_alpha, steps, *refs):
    blocks, out = refs[:steps], refs[steps]
    me, up = lax.axis_index(tm), upwards(space)
    depth, rows, columns = out.shape
    tiles = columns // steps // lanes
    scale = jnp.exp(jnp.full((depth, lanes), me.astype(jnp.float32) * -log_alpha, jnp.float32))
    for behind in range(steps):
        owner = lax.rem(me - behind + steps, steps)
        for y in range(rows):
            row = row_of(y, rows, up)
            for tile in range(tiles):
                place = pl.multiple_of((owner * tiles + tile) * lanes, lanes)
                out[:, y, pl.ds(place, lanes)] = blocks[behind][row * tiles + tile] * scale


def exchange(blocks, steps):
    moved = [
        lax.ppermute(blocks[d], "tm", [(i, (i + d) % steps) for i in range(steps)])
        for d in range(1, steps)
    ]
    return [blocks[0]] + moved


def swap(value, first):
    size = lax.axis_size("space")
    pairs = []
    for slab in range(size):
        partner = slab + 1 if (slab - first) % 2 == 0 else slab - 1
        pairs.append((slab, partner if 0 <= partner < size else slab))
    return lax.ppermute(value, "space", pairs)


def fast_local(rhs, diffusivity, velocity):
    _, depth, rows, columns = rhs.shape
    steps = lax.axis_size("tm")
    tiles = columns // steps // lanes
    log_alpha = math.log(circ_alpha) / steps
    extended, wide = rows + 2 * reach, tiles + 1
    fields = steps
    blocks = exchange(pack(rhs[0], steps), steps)
    piece = (reach * tiles + 1, depth, lanes)
    kappa_own, kappa_near, kappa_far = call(
        functools.partial(kappa_kernel, "tm", "space", rows, tiles, steps),
        [(rows * tiles + 1, depth, lanes), piece, piece],
        diffusivity,
        from_hbm=1,
    )
    kappa, inverse = call(
        functools.partial(coefficient_kernel, "tm", "space", rows, tiles, steps),
        [(extended, wide, depth, lanes), (fields, extended, wide, depth, lanes)],
        kappa_own,
        swap(kappa_near, 0),
        swap(kappa_far, 1),
    )
    near, far = halos(blocks, kappa, rows, tiles)
    far, near = swap(far, 1), swap(near, 0)
    state = [(fields, extended, wide, depth, lanes)]
    state += [(fields, extended, wide, depth + 16, lanes)] * reach
    state += [(rows * tiles, depth, lanes)] * steps
    solve = functools.partial(solve_kernel, "space", rows, tiles, steps)
    held = call(
        functools.partial(solve, False), state, *blocks, near, kappa, inverse, velocity
    )
    held = call(
        functools.partial(solve, True),
        state,
        far,
        kappa,
        inverse,
        velocity,
        *held,
        aliases={4 + i: i for i in range(len(state))},
    )
    returned = exchange(held[1 + reach :], steps)
    (result,) = call(
        functools.partial(unpack_kernel, "tm", "space", log_alpha, steps),
        [(depth, rows, columns)],
        *returned,
        kept=False,
    )
    return result[None]


def padded(shard, sides, width):
    for axis, dim in sides:
        size, length = (lax.axis_size(axis), shard.shape[dim])
        up = [(i, (i + 1) % size) for i in range(size - 1)]
        down = [(j, i) for i, j in up]
        last = lax.slice_in_dim(shard, length - width, length, axis=dim)
        initial = lax.slice_in_dim(shard, 0, width, axis=dim)
        before = lax.ppermute(last, axis, up)
        after = lax.ppermute(initial, axis, down)
        shard = jnp.concatenate([before, shard, after], axis=dim)
    return shard


def stencil(extended, diffusivity, diag_re, diag_im, velocity):
    center = extended[:, :, :, 1:-1, :]
    upper_y = extended[:, :, :, 2:, :]
    lower_y = extended[:, :, :, :-2, :]
    zero_z = jnp.zeros_like(center[:, :, :1])
    upper_z = jnp.concatenate([center[:, :, 1:], zero_z], axis=2)
    lower_z = jnp.concatenate([zero_z, center[:, :, :-1]], axis=2)
    zero_x = jnp.zeros_like(center[:, :, :, :, :1])
    upper_x = jnp.concatenate([center[:, :, :, :, 1:], zero_x], axis=4)
    lower_x = jnp.concatenate([zero_x, center[:, :, :, :, :-1]], axis=4)
    coefficient = diffusivity[None, None]
    half_velocity = 0.5 * velocity
    beside = (coefficient - half_velocity[0]) * upper_z + (coefficient + half_velocity[0]) * lower_z
    beside = (
        beside
        + (coefficient - half_velocity[1]) * upper_y
        + (coefficient + half_velocity[1]) * lower_y
    )
    beside = (
        beside
        + (coefficient - half_velocity[2]) * upper_x
        + (coefficient + half_velocity[2]) * lower_x
    )
    denominator = diag_re + 6.0 * diffusivity
    center_re = center[:, 0]
    center_im = center[:, 1]
    total_re = denominator * center_re - diag_im * center_im
    total_im = denominator * center_im + diag_im * center_re
    return jnp.stack([total_re, total_im], axis=1) - beside


def divide(residual, diffusivity, diag_re, diag_im):
    denominator = diag_re + 6.0 * diffusivity
    modulus = denominator * denominator + diag_im * diag_im
    residual_re = residual[:, 0]
    residual_im = residual[:, 1]
    quotient_re = (residual_re * denominator + residual_im * diag_im) / modulus
    quotient_im = (residual_im * denominator - residual_re * diag_im) / modulus
    return jnp.stack([quotient_re, quotient_im], axis=1)


def highest(left, right):
    return jnp.dot(left, right, precision=lax.Precision.HIGHEST, preferred_element_type=jnp.float32)


def twiddle(row_index, column_index, length):
    product = row_index[:, None] * column_index[None, :] % length
    phase_table = product.astype(jnp.float32) * (2.0 * math.pi / length)
    return (jnp.cos(phase_table), jnp.sin(phase_table))


def general_local(rhs, diffusivity, velocity):
    local_steps, depth, rows_y, rows_x = rhs.shape
    length = local_steps * lax.axis_size("tm")
    first_step = lax.axis_index("tm") * local_steps
    own_index = first_step + jnp.arange(local_steps, dtype=jnp.int32)
    log_alpha = math.log(circ_alpha) / length
    cell_count = depth * rows_y * rows_x
    scaled = (
        rhs.reshape(local_steps, cell_count)
        * jnp.exp(own_index.astype(jnp.float32) * log_alpha)[:, None]
    )
    regrouped = lax.all_to_all(scaled, "tm", split_axis=1, concat_axis=0, tiled=True)
    full_index = jnp.arange(length, dtype=jnp.int32)
    cosine_table, sine_table = twiddle(full_index, full_index, length)
    spectrum_re = highest(cosine_table, regrouped)
    spectrum_im = -highest(sine_table, regrouped)
    source_re, source_im = (
        lax.all_to_all(spectrum_re, "tm", split_axis=0, concat_axis=1, tiled=True),
        lax.all_to_all(spectrum_im, "tm", split_axis=0, concat_axis=1, tiled=True),
    )
    source = jnp.stack([source_re, source_im], axis=1).reshape(
        local_steps, 2, depth, rows_y, rows_x
    )
    phase_angle = own_index.astype(jnp.float32) * (2.0 * math.pi / length)
    shift_factor = circ_alpha ** (1.0 / length)
    diag_re = (1.0 - shift_factor * jnp.cos(phase_angle))[:, None, None, None]
    diag_im = (shift_factor * jnp.sin(phase_angle))[:, None, None, None]
    field = relax_weights[0] * divide(source, diffusivity, diag_re, diag_im)
    for weight in relax_weights[1:]:
        extended = padded(field, (("space", 3),), 1)
        applied = stencil(extended, diffusivity, diag_re, diag_im, velocity)
        field = field + weight * divide(source - applied, diffusivity, diag_re, diag_im)
    field_re = field[:, 0].reshape(local_steps, cell_count)
    field_im = field[:, 1].reshape(local_steps, cell_count)
    mixed_re, mixed_im = (
        lax.all_to_all(field_re, "tm", split_axis=1, concat_axis=0, tiled=True),
        lax.all_to_all(field_im, "tm", split_axis=1, concat_axis=0, tiled=True),
    )
    values = (highest(cosine_table, mixed_re) - highest(sine_table, mixed_im)) / length
    restored = lax.all_to_all(values, "tm", split_axis=0, concat_axis=1, tiled=True)
    result = restored * jnp.exp(-own_index.astype(jnp.float32) * log_alpha)[:, None]
    return result.reshape(local_steps, depth, rows_y, rows_x)


def local(rhs, diffusivity, velocity):
    steps = lax.axis_size("tm")
    local_steps, depth, rows, columns = rhs.shape
    if local_steps == 1 and rows >= reach and lanes % rows == 0 and columns % (steps * lanes) == 0:
        return fast_local(rhs, diffusivity, velocity)
    return general_local(rhs, diffusivity, velocity)


def solution(mesh):
    return jax.shard_map(
        local,
        mesh=mesh,
        in_specs=(P(("parts", "tm"), None, "space", None), P("parts", "space", None), P("parts")),
        out_specs=P(("parts", "tm"), None, "space", None),
        check_vma=False,
    )
```

```python
import functools
import math

import jax
import jax.numpy as jnp
from jax import lax
from jax.experimental import pallas as pl
from jax.experimental.pallas import tpu as pltpu
from jax.sharding import PartitionSpec as P

circ_alpha = 0.1
relax_weights = (
    1.0 / (1.0 - 0.5 * math.cos(math.pi / 8.0)),
    1.0 / (1.0 - 0.5 * math.cos(3.0 * math.pi / 8.0)),
    1.0 / (1.0 - 0.5 * math.cos(5.0 * math.pi / 8.0)),
    1.0 / (1.0 - 0.5 * math.cos(7.0 * math.pi / 8.0)),
)


reach = len(relax_weights) - 1
lanes = 128
vmem = pl.BlockSpec(memory_space=pltpu.VMEM)
smem = pl.BlockSpec(memory_space=pltpu.SMEM)
hbm = pl.BlockSpec(memory_space=pltpu.HBM)


def call(kernel, outs, *operands, specs=None, kept=True, aliases=None, scratch=()):
    specs = specs or {}
    on_chip = [
        x
        if specs.get(i) is smem
        else pltpu.with_memory_space_constraint(x, pltpu.HBM if i in specs else pltpu.VMEM)
        for i, x in enumerate(operands)
    ]
    make = pltpu.VMEM if kept else jax.ShapeDtypeStruct
    return pl.pallas_call(
        kernel,
        out_shape=[make(o, jnp.float32) for o in outs],
        in_specs=[specs.get(i, vmem) for i in range(len(operands))],
        out_specs=[vmem if kept else hbm] * len(outs),
        scratch_shapes=scratch,
        input_output_aliases=aliases or {},
        compiler_params=pltpu.CompilerParams(vmem_limit_bytes=16 << 20),
    )(*on_chip)


def column_mask(left, right, shape):
    lane = lax.broadcasted_iota(jnp.int32, shape, 1)
    keep_right = (lane < reach).astype(jnp.float32) * right
    keep_left = (lane >= lanes - reach).astype(jnp.float32) * left
    return keep_right, keep_left


def upwards(space):
    return lax.rem(lax.axis_index(space), 2)


def row_of(y, rows, up):
    return up * y + (1 - up) * (rows - 1 - y)


def pick_block(source, write, owner, owners, up):
    depth, rows, columns = source.shape
    total = columns // lanes
    tiles = total // owners
    left_tile = jnp.maximum(owner * tiles - 1, 0)
    right_tile = jnp.minimum((owner + 1) * tiles, total - 1)
    left = (owner > 0).astype(jnp.float32)
    right = (owner < owners - 1).astype(jnp.float32)
    keep_right, keep_left = column_mask(left, right, (depth, lanes))
    packed = None

    def tile_at(y, tile):
        return source[:, y, pl.ds(pl.multiple_of(tile * lanes, lanes), lanes)]

    for y in range(rows):
        row = row_of(y, rows, up)
        for tile in range(tiles):
            write(row * tiles + tile, tile_at(y, owner * tiles + tile))
        halo = tile_at(y, right_tile) * keep_right + tile_at(y, left_tile) * keep_left
        halo = pltpu.roll(halo, row * (lanes // rows), 1)
        packed = halo if packed is None else packed + halo
    write(rows * tiles, packed)


def fetch(source, target, semaphores):
    pieces = semaphores.shape[0]
    size = source.shape[0] // pieces
    copies = [
        pltpu.make_async_copy(
            source.at[pl.ds(i * size, size)], target.at[pl.ds(i * size, size)], semaphores.at[i]
        )
        for i in range(pieces)
    ]
    for copy in copies:
        copy.start()
    for copy in copies:
        copy.wait()


def pack_kernel(tm, space, log_alpha, steps, rhs, *refs):
    outs, (held, semaphores) = refs[:steps], refs[steps:]
    me, up = lax.axis_index(tm), upwards(space)
    depth = rhs.shape[0]
    fetch(rhs, held, semaphores)
    scale = jnp.exp(jnp.full((depth, lanes), me.astype(jnp.float32) * log_alpha, jnp.float32))
    for ahead in range(steps):
        out = outs[ahead]

        def write(index, value, out=out):
            out[index] = value * scale

        pick_block(held, write, lax.rem(me + ahead, steps), steps, up)


def staging(shape):
    pieces = math.gcd(shape[0], 4)
    return [pltpu.VMEM(shape, jnp.float32), pltpu.SemaphoreType.DMA((pieces,))]


def pack(rhs, steps):
    depth, rows, columns = rhs.shape
    tiles = columns // steps // lanes
    log_alpha = math.log(circ_alpha) / steps
    kernel = functools.partial(pack_kernel, "tm", "space", log_alpha, steps)
    out = (rows * tiles + 1, depth, lanes)
    return call(kernel, [out] * steps, rhs, specs={0: hbm}, scratch=staging(rhs.shape))


def first_row(near, rows):
    return 0 if near else rows - reach


def halo_kernel(rows, tiles, count, *refs):
    blocks, (near, far) = refs[:count], refs[count:]
    piece = reach * tiles + 1
    for step, block in enumerate(blocks):
        for out, is_near in ((near, True), (far, False)):
            start = first_row(is_near, rows) * tiles
            for place in range(reach * tiles):
                out[step * piece + place] = block[start + place]
            out[step * piece + reach * tiles] = block[rows * tiles]


def halos(blocks, rows, tiles):
    depth = blocks[0].shape[1]
    out = (len(blocks) * (reach * tiles + 1), depth, lanes)
    kernel = functools.partial(halo_kernel, rows, tiles, len(blocks))
    return call(kernel, [out, out], *blocks)


def row_piece(own, near, far, step, row, tile, rows, tiles):
    piece = reach * tiles + 1
    if row < reach:
        source, base, there, start = near, step * piece, reach - 1 - row, 0
        packed = base + reach * tiles
    elif row < reach + rows:
        source, base, there, start = own, 0, row - reach, 0
        packed = rows * tiles
    else:
        source, base, there = far, step * piece, 2 * rows + reach - 1 - row
        start = rows - reach
        packed = base + reach * tiles
    if tile < tiles:
        return source[base + (there - start) * tiles + tile]
    value = source[packed]
    shift = there * (lanes // rows)
    return pltpu.roll(value, lanes - shift, 1) if shift else value


def frequencies(steps):
    return [(k, 2 * k % steps != 0) for k in range(steps // 2 + 1)]


def write_coefficients(row, tile, value, mask, steps, kappa, inverse):
    shift_factor = circ_alpha ** (1.0 / steps)
    kappa[row, tile] = value
    place = 0
    for k, is_complex in frequencies(steps):
        phase = 2.0 * math.pi * k / steps
        real = (1.0 - shift_factor * math.cos(phase)) + 6.0 * value
        if is_complex:
            imag = shift_factor * math.sin(phase)
            reciprocal = 1.0 / (real * real + imag * imag)
            pair = (real * reciprocal, imag * reciprocal)
        else:
            pair = (1.0 / real,)
        for part in pair:
            inverse[place, row, tile] = part if mask is None else part * mask
            place += 1


def side_mask(tm, steps, depth):
    me = lax.axis_index(tm)
    keep_right, keep_left = column_mask(
        (me > 0).astype(jnp.float32), (me < steps - 1).astype(jnp.float32), (depth, lanes)
    )
    return keep_right + keep_left


def prepare_kernel(tm, space, rows, tiles, steps, diffusivity, velocity, *refs):
    own, kappa, inverse, drift, *iterates = refs[:-2]
    held, semaphores = refs[-2:]
    up = upwards(space)
    depth = diffusivity.shape[0]
    direction = (2 * up - 1).astype(jnp.float32)
    for j in range(3):
        speed = 0.5 * velocity[j]
        drift[j] = jnp.full((depth, lanes), speed * direction if j == 1 else speed, jnp.float32)
    zero = jnp.zeros((8, lanes), jnp.float32)
    for level, ref in enumerate(iterates):
        fields, extended, wide = ref.shape[:3]
        for field in range(fields):
            for row in range(level, extended - level):
                for tile in range(wide):
                    ref[field, row, tile, pl.ds(0, 8), :] = zero
                    ref[field, row, tile, pl.ds(8 + depth, 8), :] = zero
    fetch(diffusivity, held, semaphores)

    def write(index, value):
        own[index] = value

    pick_block(held, write, lax.axis_index(tm), steps, up)
    halo_mask = side_mask(tm, steps, depth)
    for row in range(reach, reach + rows):
        for tile in range(tiles + 1):
            value = row_piece(own, None, None, 0, row, tile, rows, tiles)
            mask = halo_mask if tile == tiles else None
            write_coefficients(row, tile, value, mask, steps, kappa, inverse)


def combine(terms):
    total = None
    for factor, value in terms:
        if factor == 0.0:
            continue
        if total is None:
            total = value if factor == 1.0 else factor * value
        elif factor == 1.0:
            total = total + value
        elif factor == -1.0:
            total = total - value
        else:
            total = total + factor * value
    return total


def exact(value):
    return float(round(value)) if abs(value - round(value)) < 1e-12 else value


def cosine(product, steps):
    return exact(math.cos(2.0 * math.pi * (product % steps) / steps))


def sine(product, steps):
    return exact(math.sin(2.0 * math.pi * (product % steps) / steps))


def solve_kernel(tm, space, rows, tiles, steps, second_half, *refs):
    freqs = frequencies(steps)
    fields = sum(2 if c else 1 for _, c in freqs)
    levels = reach
    made = 2 + levels
    if second_half:
        far, drift = refs[:2]
        kappa, inverse, *iterates = refs[2 + made + 1 + steps :][:made]
        source, *outs = refs[2 + made + 1 + steps + made :]
        blocks, near = [None] * steps, None
    else:
        blocks, (near, drift) = refs[:steps], refs[steps : steps + 2]
        kappa, inverse, *iterates = refs[steps + 2 + made :][:made]
        source, *outs = refs[steps + 2 + made + made :]
        far = None
    depth = kappa.shape[2]
    pad = 8
    middle = pl.ds(pad, depth)
    lane = lax.broadcasted_iota(jnp.int32, (depth, lanes), 1)
    at_first, at_last = lane == 0, lane == lanes - 1
    half = [drift[j] for j in range(3)]
    known = reach + rows
    extended = known + reach
    wide = tiles + 1

    def rows_of(level):
        split = known - level
        return (split, extended - level) if second_half else (level, split)

    slab, slabs, up = lax.axis_index(space), lax.axis_size(space), upwards(space)
    beyond = slab < slabs - 1 if second_half else slab > 0
    before = slab > 0 if second_half else slab < slabs - 1
    inside = jnp.where(up == 1, beyond, before).astype(jnp.float32)
    halo_mask = side_mask(tm, steps, depth) * inside
    row_mask = jnp.full((depth, lanes), inside, jnp.float32)
    for row in range(known, extended) if second_half else range(reach):
        for tile in range(wide):
            value = row_piece(None, near, far, steps, row, tile, rows, tiles)
            mask = halo_mask if tile == tiles else row_mask
            write_coefficients(row, tile, value, mask, steps, kappa, inverse)

    def divide(values, row, tile):
        result, place = [], 0
        for _, is_complex in freqs:
            if is_complex:
                re, im = values[place], values[place + 1]
                p, q = inverse[place, row, tile], inverse[place + 1, row, tile]
                result += [re * p + im * q, im * p - re * q]
                place += 2
            else:
                result.append(values[place] * inverse[place, row, tile])
                place += 1
        return result

    for row in range(*rows_of(0)):
        for tile in range(wide):
            if tile == tiles and not 1 <= row < extended - 1:
                continue
            held = [
                row_piece(blocks[b], near, far, b, row, tile, rows, tiles) for b in range(steps)
            ]
            values = []
            for k, is_complex in freqs:
                values.append(combine((cosine(k * b, steps), held[b]) for b in range(steps)))
                if is_complex:
                    values.append(combine((sine(k * b, steps), held[b]) for b in range(steps)))
            quotients = divide(values, row, tile)
            for field in range(fields):
                source[field, row, tile] = values[field]
                iterates[0][field, row, tile, middle, :] = relax_weights[0] * quotients[field]

    def sweep(row, old, weight, last):
        centers = [
            [old[field, row, tile, middle, :] for tile in range(wide)] for field in range(fields)
        ]
        shifted_down = [[pltpu.roll(c, 1, 1) for c in line] for line in centers]
        shifted_up = [[pltpu.roll(c, lanes - 1, 1) for c in line] for line in centers]
        for tile in range(tiles if last else wide):
            values = []
            coefficient = kappa[row, tile]
            for field in range(fields):
                lower_x = jnp.where(
                    at_first, shifted_down[field][(tile - 1) % wide], shifted_down[field][tile]
                )
                upper_x = jnp.where(
                    at_last, shifted_up[field][(tile + 1) % wide], shifted_up[field][tile]
                )
                lower_z = old[field, row, tile, pl.ds(pad - 1, depth), :]
                upper_z = old[field, row, tile, pl.ds(pad + 1, depth), :]
                lower_y = old[field, row - 1, tile, middle, :]
                upper_y = old[field, row + 1, tile, middle, :]
                around = (lower_z + upper_z) + (lower_y + upper_y) + (lower_x + upper_x)
                slope = (
                    half[0] * (lower_z - upper_z)
                    + half[1] * (lower_y - upper_y)
                    + half[2] * (lower_x - upper_x)
                )
                values.append(source[field, row, tile] + (coefficient * around + slope))
            quotients = divide(values, row, tile)
            yield tile, [
                (1.0 - weight) * centers[field][tile] + weight * quotients[field]
                for field in range(fields)
            ]

    for level in range(1, levels):

        def step(row, carry, level=level):
            for tile, results in sweep(row, iterates[level - 1], relax_weights[level], False):
                for field in range(fields):
                    iterates[level][field, row, tile, middle, :] = results[field]
            return carry

        lax.fori_loop(*rows_of(level), step, 0)

    def last_step(row, carry):
        for tile, results in sweep(row, iterates[levels - 1], relax_weights[levels], True):
            for ahead in range(steps):
                terms, place = [], 0
                for k, is_complex in freqs:
                    factor = (2.0 if is_complex else 1.0) / steps
                    terms.append((factor * cosine(k * ahead, steps), results[place]))
                    place += 1
                    if is_complex:
                        terms.append((-factor * sine(k * ahead, steps), results[place]))
                        place += 1
                outs[ahead][(row - reach) * tiles + tile] = combine(terms)
        return carry

    lax.fori_loop(*rows_of(levels), last_step, 0)


def unpack_kernel(tm, space, log_alpha, steps, *refs):
    blocks, (out, held, semaphores) = refs[:steps], refs[steps:]
    me, up = lax.axis_index(tm), upwards(space)
    depth, rows, columns = out.shape
    width = columns // steps
    tiles = width // lanes
    scale = jnp.exp(jnp.full((depth, lanes), me.astype(jnp.float32) * -log_alpha, jnp.float32))
    copies = []
    for behind in range(steps):
        owner = lax.rem(me - behind + steps, steps)
        for y in range(rows):
            row = row_of(y, rows, up)
            for tile in range(tiles):
                place = pl.multiple_of((owner * tiles + tile) * lanes, lanes)
                held[:, y, pl.ds(place, lanes)] = blocks[behind][row * tiles + tile] * scale
        part = pl.ds(pl.multiple_of(owner * width, lanes), width)
        copies.append(
            pltpu.make_async_copy(
                held.at[:, :, part], out.at[:, :, part], semaphores.at[behind]
            )
        )
        copies[-1].start()
    for copy in copies:
        copy.wait()


def exchange(blocks, steps):
    moved = [
        lax.ppermute(blocks[d], "tm", [(i, (i + d) % steps) for i in range(steps)])
        for d in range(1, steps)
    ]
    return [blocks[0]] + moved


def swap(value, first):
    size, steps = lax.axis_size("space"), lax.axis_size("tm")
    pairs = []
    for step in range(steps):
        beside = step ^ 1 if steps % 2 == 0 else (step + 1) % steps
        for slab in range(size):
            partner = slab + 1 if (slab - first) % 2 == 0 else slab - 1
            target = (step, partner) if 0 <= partner < size else (beside, slab)
            pairs.append((step * size + slab, target[0] * size + target[1]))
    return lax.ppermute(value, ("tm", "space"), pairs)


def fast_local(rhs, diffusivity, velocity):
    _, depth, rows, columns = rhs.shape
    steps = lax.axis_size("tm")
    tiles = columns // steps // lanes
    log_alpha = math.log(circ_alpha) / steps
    extended, wide = rows + 2 * reach, tiles + 1
    fields = steps
    blocks = exchange(pack(rhs[0], steps), steps)
    made = [(extended, wide, depth, lanes), (fields, extended, wide, depth, lanes)]
    iterates = [(fields, extended, wide, depth + 16, lanes)] * reach
    own, kappa, inverse, drift, *margins = call(
        functools.partial(prepare_kernel, "tm", "space", rows, tiles, steps),
        [(rows * tiles + 1, depth, lanes), *made, (3, depth, lanes), *iterates],
        diffusivity,
        velocity,
        specs={0: hbm, 1: smem},
        scratch=staging(diffusivity.shape),
    )
    near, far = halos([*blocks, own], rows, tiles)
    far, near = swap(far, 1), swap(near, 0)
    state = [*made, *iterates, made[1]] + [(rows * tiles, depth, lanes)] * steps
    solve = functools.partial(solve_kernel, "tm", "space", rows, tiles, steps)
    kept = [kappa, inverse, *margins]
    held = call(
        functools.partial(solve, False),
        state,
        *blocks,
        near,
        drift,
        *kept,
        aliases={steps + 2 + i: i for i in range(len(kept))},
    )
    held = call(
        functools.partial(solve, True),
        state,
        far,
        drift,
        *held,
        aliases={2 + i: i for i in range(len(state))},
    )
    returned = exchange(held[len(kept) + 1 :], steps)
    (result,) = call(
        functools.partial(unpack_kernel, "tm", "space", log_alpha, steps),
        [(depth, rows, columns)],
        *returned,
        kept=False,
        scratch=[
            pltpu.VMEM((depth, rows, columns), jnp.float32),
            pltpu.SemaphoreType.DMA((steps,)),
        ],
    )
    return result[None]


def padded(shard, sides, width):
    for axis, dim in sides:
        size, length = (lax.axis_size(axis), shard.shape[dim])
        up = [(i, (i + 1) % size) for i in range(size - 1)]
        down = [(j, i) for i, j in up]
        last = lax.slice_in_dim(shard, length - width, length, axis=dim)
        initial = lax.slice_in_dim(shard, 0, width, axis=dim)
        before = lax.ppermute(last, axis, up)
        after = lax.ppermute(initial, axis, down)
        shard = jnp.concatenate([before, shard, after], axis=dim)
    return shard


def stencil(extended, diffusivity, diag_re, diag_im, velocity):
    center = extended[:, :, :, 1:-1, :]
    upper_y = extended[:, :, :, 2:, :]
    lower_y = extended[:, :, :, :-2, :]
    zero_z = jnp.zeros_like(center[:, :, :1])
    upper_z = jnp.concatenate([center[:, :, 1:], zero_z], axis=2)
    lower_z = jnp.concatenate([zero_z, center[:, :, :-1]], axis=2)
    zero_x = jnp.zeros_like(center[:, :, :, :, :1])
    upper_x = jnp.concatenate([center[:, :, :, :, 1:], zero_x], axis=4)
    lower_x = jnp.concatenate([zero_x, center[:, :, :, :, :-1]], axis=4)
    coefficient = diffusivity[None, None]
    half_velocity = 0.5 * velocity
    beside = (coefficient - half_velocity[0]) * upper_z + (coefficient + half_velocity[0]) * lower_z
    beside = (
        beside
        + (coefficient - half_velocity[1]) * upper_y
        + (coefficient + half_velocity[1]) * lower_y
    )
    beside = (
        beside
        + (coefficient - half_velocity[2]) * upper_x
        + (coefficient + half_velocity[2]) * lower_x
    )
    denominator = diag_re + 6.0 * diffusivity
    center_re = center[:, 0]
    center_im = center[:, 1]
    total_re = denominator * center_re - diag_im * center_im
    total_im = denominator * center_im + diag_im * center_re
    return jnp.stack([total_re, total_im], axis=1) - beside


def divide(residual, diffusivity, diag_re, diag_im):
    denominator = diag_re + 6.0 * diffusivity
    modulus = denominator * denominator + diag_im * diag_im
    residual_re = residual[:, 0]
    residual_im = residual[:, 1]
    quotient_re = (residual_re * denominator + residual_im * diag_im) / modulus
    quotient_im = (residual_im * denominator - residual_re * diag_im) / modulus
    return jnp.stack([quotient_re, quotient_im], axis=1)


def highest(left, right):
    return jnp.dot(left, right, precision=lax.Precision.HIGHEST, preferred_element_type=jnp.float32)


def twiddle(row_index, column_index, length):
    product = row_index[:, None] * column_index[None, :] % length
    phase_table = product.astype(jnp.float32) * (2.0 * math.pi / length)
    return (jnp.cos(phase_table), jnp.sin(phase_table))


def general_local(rhs, diffusivity, velocity):
    local_steps, depth, rows_y, rows_x = rhs.shape
    length = local_steps * lax.axis_size("tm")
    first_step = lax.axis_index("tm") * local_steps
    own_index = first_step + jnp.arange(local_steps, dtype=jnp.int32)
    log_alpha = math.log(circ_alpha) / length
    cell_count = depth * rows_y * rows_x
    scaled = (
        rhs.reshape(local_steps, cell_count)
        * jnp.exp(own_index.astype(jnp.float32) * log_alpha)[:, None]
    )
    regrouped = lax.all_to_all(scaled, "tm", split_axis=1, concat_axis=0, tiled=True)
    full_index = jnp.arange(length, dtype=jnp.int32)
    cosine_table, sine_table = twiddle(full_index, full_index, length)
    spectrum_re = highest(cosine_table, regrouped)
    spectrum_im = -highest(sine_table, regrouped)
    source_re, source_im = (
        lax.all_to_all(spectrum_re, "tm", split_axis=0, concat_axis=1, tiled=True),
        lax.all_to_all(spectrum_im, "tm", split_axis=0, concat_axis=1, tiled=True),
    )
    source = jnp.stack([source_re, source_im], axis=1).reshape(
        local_steps, 2, depth, rows_y, rows_x
    )
    phase_angle = own_index.astype(jnp.float32) * (2.0 * math.pi / length)
    shift_factor = circ_alpha ** (1.0 / length)
    diag_re = (1.0 - shift_factor * jnp.cos(phase_angle))[:, None, None, None]
    diag_im = (shift_factor * jnp.sin(phase_angle))[:, None, None, None]
    field = relax_weights[0] * divide(source, diffusivity, diag_re, diag_im)
    for weight in relax_weights[1:]:
        extended = padded(field, (("space", 3),), 1)
        applied = stencil(extended, diffusivity, diag_re, diag_im, velocity)
        field = field + weight * divide(source - applied, diffusivity, diag_re, diag_im)
    field_re = field[:, 0].reshape(local_steps, cell_count)
    field_im = field[:, 1].reshape(local_steps, cell_count)
    mixed_re, mixed_im = (
        lax.all_to_all(field_re, "tm", split_axis=1, concat_axis=0, tiled=True),
        lax.all_to_all(field_im, "tm", split_axis=1, concat_axis=0, tiled=True),
    )
    values = (highest(cosine_table, mixed_re) - highest(sine_table, mixed_im)) / length
    restored = lax.all_to_all(values, "tm", split_axis=0, concat_axis=1, tiled=True)
    result = restored * jnp.exp(-own_index.astype(jnp.float32) * log_alpha)[:, None]
    return result.reshape(local_steps, depth, rows_y, rows_x)


def local(rhs, diffusivity, velocity):
    steps = lax.axis_size("tm")
    local_steps, depth, rows, columns = rhs.shape
    if local_steps == 1 and rows >= reach and lanes % rows == 0 and columns % (steps * lanes) == 0:
        return fast_local(rhs, diffusivity, velocity)
    return general_local(rhs, diffusivity, velocity)


def solution(mesh):
    return jax.shard_map(
        local,
        mesh=mesh,
        in_specs=(P(("parts", "tm"), None, "space", None), P("parts", "space", None), P("parts")),
        out_specs=P(("parts", "tm"), None, "space", None),
        check_vma=False,
    )
```

```python
import functools
import math

import jax
import jax.numpy as jnp
from jax import lax
from jax.experimental import pallas as pl
from jax.experimental.pallas import tpu as pltpu
from jax.sharding import PartitionSpec as P


circ_alpha = 0.1
relax_weights = (
    1.0 / (1.0 - 0.5 * math.cos(math.pi / 8.0)),
    1.0 / (1.0 - 0.5 * math.cos(3.0 * math.pi / 8.0)),
    1.0 / (1.0 - 0.5 * math.cos(5.0 * math.pi / 8.0)),
    1.0 / (1.0 - 0.5 * math.cos(7.0 * math.pi / 8.0)),
)


reach = len(relax_weights) - 1
lanes = 128
vmem = pl.BlockSpec(memory_space=pltpu.VMEM)
smem = pl.BlockSpec(memory_space=pltpu.SMEM)
hbm = pl.BlockSpec(memory_space=pltpu.HBM)


def call(kernel, outs, *operands, specs=None, kept=True, aliases=None, scratch=()):
    specs = specs or {}
    on_chip = [
        x
        if specs.get(i) is smem
        else pltpu.with_memory_space_constraint(x, pltpu.HBM if i in specs else pltpu.VMEM)
        for i, x in enumerate(operands)
    ]
    make = pltpu.VMEM if kept else jax.ShapeDtypeStruct
    return pl.pallas_call(
        kernel,
        out_shape=[make(o, jnp.float32) for o in outs],
        in_specs=[specs.get(i, vmem) for i in range(len(operands))],
        out_specs=[vmem if kept else hbm] * len(outs),
        scratch_shapes=scratch,
        input_output_aliases=aliases or {},
        compiler_params=pltpu.CompilerParams(vmem_limit_bytes=16 << 20),
    )(*on_chip)


def column_mask(left, right, shape):
    lane = lax.broadcasted_iota(jnp.int32, shape, 1)
    keep_right = (lane < reach).astype(jnp.float32) * right
    keep_left = (lane >= lanes - reach).astype(jnp.float32) * left
    return keep_right, keep_left


def upwards(space):
    return lax.rem(lax.axis_index(space), 2)


def row_of(y, rows, up):
    return up * y + (1 - up) * (rows - 1 - y)


def pick_block(source, write, owner, owners, up):
    depth, rows, columns = source.shape
    total = columns // lanes
    tiles = total // owners
    left_tile = jnp.maximum(owner * tiles - 1, 0)
    right_tile = jnp.minimum((owner + 1) * tiles, total - 1)
    left = (owner > 0).astype(jnp.float32)
    right = (owner < owners - 1).astype(jnp.float32)
    keep_right, keep_left = column_mask(left, right, (depth, lanes))
    packed = None

    def tile_at(y, tile):
        return source[:, y, pl.ds(pl.multiple_of(tile * lanes, lanes), lanes)]

    for y in range(rows):
        row = row_of(y, rows, up)
        for tile in range(tiles):
            write(row * tiles + tile, tile_at(y, owner * tiles + tile))
        halo = tile_at(y, right_tile) * keep_right + tile_at(y, left_tile) * keep_left
        halo = pltpu.roll(halo, row * (lanes // rows), 1)
        packed = halo if packed is None else packed + halo
    write(rows * tiles, packed)


def fetch(source, target, semaphores):
    pieces = semaphores.shape[0]
    size = source.shape[0] // pieces
    copies = [
        pltpu.make_async_copy(
            source.at[pl.ds(i * size, size)], target.at[pl.ds(i * size, size)], semaphores.at[i]
        )
        for i in range(pieces)
    ]
    for copy in copies:
        copy.start()
    for copy in copies:
        copy.wait()


def pack_kernel(tm, space, log_alpha, steps, rhs, *refs):
    outs, (held, semaphores) = refs[:steps], refs[steps:]
    me, up = lax.axis_index(tm), upwards(space)
    depth = rhs.shape[0]
    fetch(rhs, held, semaphores)
    scale = jnp.exp(jnp.full((depth, lanes), me.astype(jnp.float32) * log_alpha, jnp.float32))
    for ahead in range(steps):
        out = outs[ahead]

        def write(index, value, out=out):
            out[index] = value * scale

        pick_block(held, write, lax.rem(me + ahead, steps), steps, up)


def staging(shape):
    pieces = math.gcd(shape[0], 4)
    return [pltpu.VMEM(shape, jnp.float32), pltpu.SemaphoreType.DMA((pieces,))]


def pack(rhs, steps):
    depth, rows, columns = rhs.shape
    tiles = columns // steps // lanes
    log_alpha = math.log(circ_alpha) / steps
    kernel = functools.partial(pack_kernel, "tm", "space", log_alpha, steps)
    out = (rows * tiles + 1, depth, lanes)
    return call(kernel, [out] * steps, rhs, specs={0: hbm}, scratch=staging(rhs.shape))


def first_row(near, rows):
    return 0 if near else rows - reach


def halo_kernel(rows, tiles, count, *refs):
    blocks, (near, far) = refs[:count], refs[count:]
    piece = reach * tiles + 1
    for step, block in enumerate(blocks):
        for out, is_near in ((near, True), (far, False)):
            start = first_row(is_near, rows) * tiles
            for place in range(reach * tiles):
                out[step * piece + place] = block[start + place]
            out[step * piece + reach * tiles] = block[rows * tiles]


def halos(blocks, rows, tiles):
    depth = blocks[0].shape[1]
    out = (len(blocks) * (reach * tiles + 1), depth, lanes)
    kernel = functools.partial(halo_kernel, rows, tiles, len(blocks))
    return call(kernel, [out, out], *blocks)


def row_piece(own, near, far, step, row, tile, rows, tiles):
    piece = reach * tiles + 1
    if row < reach:
        source, base, there, start = near, step * piece, reach - 1 - row, 0
        packed = base + reach * tiles
    elif row < reach + rows:
        source, base, there, start = own, 0, row - reach, 0
        packed = rows * tiles
    else:
        source, base, there = far, step * piece, 2 * rows + reach - 1 - row
        start = rows - reach
        packed = base + reach * tiles
    if tile < tiles:
        return source[base + (there - start) * tiles + tile]
    value = source[packed]
    shift = there * (lanes // rows)
    return pltpu.roll(value, lanes - shift, 1) if shift else value


def frequencies(steps):
    return [(k, 2 * k % steps != 0) for k in range(steps // 2 + 1)]


def write_coefficients(row, tile, value, mask, steps, kappa, inverse):
    shift_factor = circ_alpha ** (1.0 / steps)
    kappa[row, tile] = value
    place = 0
    for k, is_complex in frequencies(steps):
        phase = 2.0 * math.pi * k / steps
        real = (1.0 - shift_factor * math.cos(phase)) + 6.0 * value
        if is_complex:
            imag = shift_factor * math.sin(phase)
            reciprocal = 1.0 / (real * real + imag * imag)
            pair = (real * reciprocal, imag * reciprocal)
        else:
            pair = (1.0 / real,)
        for part in pair:
            inverse[place, row, tile] = part if mask is None else part * mask
            place += 1


def side_mask(tm, steps, depth):
    me = lax.axis_index(tm)
    keep_right, keep_left = column_mask(
        (me > 0).astype(jnp.float32), (me < steps - 1).astype(jnp.float32), (depth, lanes)
    )
    return keep_right + keep_left


def prepare_kernel(tm, space, rows, tiles, steps, diffusivity, velocity, *refs):
    own, kappa, inverse, drift, *iterates = refs[:-2]
    held, semaphores = refs[-2:]
    up = upwards(space)
    depth = diffusivity.shape[0]
    direction = (2 * up - 1).astype(jnp.float32)
    for j in range(3):
        speed = 0.5 * velocity[j]
        drift[j] = jnp.full((depth, lanes), speed * direction if j == 1 else speed, jnp.float32)
    zero = jnp.zeros((8, lanes), jnp.float32)
    for level, ref in enumerate(iterates):
        fields, extended, wide = ref.shape[:3]
        for field in range(fields):
            for row in range(level, extended - level):
                for tile in range(wide):
                    ref[field, row, tile, pl.ds(0, 8), :] = zero
                    ref[field, row, tile, pl.ds(8 + depth, 8), :] = zero
    fetch(diffusivity, held, semaphores)

    def write(index, value):
        own[index] = value

    pick_block(held, write, lax.axis_index(tm), steps, up)
    halo_mask = side_mask(tm, steps, depth)
    for row in range(reach, reach + rows):
        for tile in range(tiles + 1):
            value = row_piece(own, None, None, 0, row, tile, rows, tiles)
            mask = halo_mask if tile == tiles else None
            write_coefficients(row, tile, value, mask, steps, kappa, inverse)


def combine(terms):
    total = None
    for factor, value in terms:
        if factor == 0.0:
            continue
        if total is None:
            total = value if factor == 1.0 else factor * value
        elif factor == 1.0:
            total = total + value
        elif factor == -1.0:
            total = total - value
        else:
            total = total + factor * value
    return total


def exact(value):
    return float(round(value)) if abs(value - round(value)) < 1e-12 else value


def cosine(product, steps):
    return exact(math.cos(2.0 * math.pi * (product % steps) / steps))


def sine(product, steps):
    return exact(math.sin(2.0 * math.pi * (product % steps) / steps))


def solve_kernel(tm, space, rows, tiles, steps, second_half, *refs):
    freqs = frequencies(steps)
    fields = sum(2 if c else 1 for _, c in freqs)
    levels = reach
    made = 2 + levels
    if second_half:
        far, drift = refs[:2]
        kappa, inverse, *iterates = refs[2 + made + 1 :][:made]
        source, *outs = refs[2 + made + 1 + made :]
        blocks, near = [None] * steps, None
    else:
        blocks, (near, drift) = refs[:steps], refs[steps : steps + 2]
        kappa, inverse, *iterates = refs[steps + 2 + made :][:made]
        source, *outs = refs[steps + 2 + made + made :]
        far = None
    depth = kappa.shape[2]
    pad = 8
    middle = pl.ds(pad, depth)
    lane = lax.broadcasted_iota(jnp.int32, (depth, lanes), 1)
    at_first, at_last = lane == 0, lane == lanes - 1
    half = [drift[j] for j in range(3)]
    known = reach + rows
    extended = known + reach
    wide = tiles + 1

    def rows_of(level):
        split = known - level
        return (split, extended - level) if second_half else (level, split)

    slab, slabs, up = lax.axis_index(space), lax.axis_size(space), upwards(space)
    beyond = slab < slabs - 1 if second_half else slab > 0
    before = slab > 0 if second_half else slab < slabs - 1
    inside = jnp.where(up == 1, beyond, before).astype(jnp.float32)
    halo_mask = side_mask(tm, steps, depth) * inside
    row_mask = jnp.full((depth, lanes), inside, jnp.float32)
    for row in range(known, extended) if second_half else range(reach):
        for tile in range(wide):
            value = row_piece(None, near, far, steps, row, tile, rows, tiles)
            mask = halo_mask if tile == tiles else row_mask
            write_coefficients(row, tile, value, mask, steps, kappa, inverse)

    def divide(values, row, tile):
        result, place = [], 0
        for _, is_complex in freqs:
            if is_complex:
                re, im = values[place], values[place + 1]
                p, q = inverse[place, row, tile], inverse[place + 1, row, tile]
                result += [re * p + im * q, im * p - re * q]
                place += 2
            else:
                result.append(values[place] * inverse[place, row, tile])
                place += 1
        return result

    for row in range(*rows_of(0)):
        for tile in range(wide):
            if tile == tiles and not 1 <= row < extended - 1:
                continue
            held = [
                row_piece(blocks[b], near, far, b, row, tile, rows, tiles) for b in range(steps)
            ]
            values = []
            for k, is_complex in freqs:
                values.append(combine((cosine(k * b, steps), held[b]) for b in range(steps)))
                if is_complex:
                    values.append(combine((sine(k * b, steps), held[b]) for b in range(steps)))
            quotients = divide(values, row, tile)
            for field in range(fields):
                source[field, row, tile] = values[field]
                iterates[0][field, row, tile, middle, :] = relax_weights[0] * quotients[field]

    def sweep(row, old, weight, last):
        centers = [
            [old[field, row, tile, middle, :] for tile in range(wide)] for field in range(fields)
        ]
        shifted_down = [[pltpu.roll(c, 1, 1) for c in line] for line in centers]
        shifted_up = [[pltpu.roll(c, lanes - 1, 1) for c in line] for line in centers]
        for tile in range(tiles if last else wide):
            values = []
            coefficient = kappa[row, tile]
            for field in range(fields):
                lower_x = jnp.where(
                    at_first, shifted_down[field][(tile - 1) % wide], shifted_down[field][tile]
                )
                upper_x = jnp.where(
                    at_last, shifted_up[field][(tile + 1) % wide], shifted_up[field][tile]
                )
                lower_z = old[field, row, tile, pl.ds(pad - 1, depth), :]
                upper_z = old[field, row, tile, pl.ds(pad + 1, depth), :]
                lower_y = old[field, row - 1, tile, middle, :]
                upper_y = old[field, row + 1, tile, middle, :]
                around = (lower_z + upper_z) + (lower_y + upper_y) + (lower_x + upper_x)
                slope = (
                    half[0] * (lower_z - upper_z)
                    + half[1] * (lower_y - upper_y)
                    + half[2] * (lower_x - upper_x)
                )
                values.append(source[field, row, tile] + (coefficient * around + slope))
            quotients = divide(values, row, tile)
            yield tile, [
                (1.0 - weight) * centers[field][tile] + weight * quotients[field]
                for field in range(fields)
            ]

    for level in range(1, levels):

        def step(row, carry, level=level):
            for tile, results in sweep(row, iterates[level - 1], relax_weights[level], False):
                for field in range(fields):
                    iterates[level][field, row, tile, middle, :] = results[field]
            return carry

        lax.fori_loop(*rows_of(level), step, 0)

    last_rows = rows_of(levels)

    def last_step(row, carry):
        for tile, results in sweep(row, iterates[levels - 1], relax_weights[levels], True):
            for ahead in range(steps):
                terms, place = [], 0
                for k, is_complex in freqs:
                    factor = (2.0 if is_complex else 1.0) / steps
                    terms.append((factor * cosine(k * ahead, steps), results[place]))
                    place += 1
                    if is_complex:
                        terms.append((-factor * sine(k * ahead, steps), results[place]))
                        place += 1
                outs[ahead][(row - last_rows[0]) * tiles + tile] = combine(terms)
        return carry

    lax.fori_loop(*last_rows, last_step, 0)


def unpack_kernel(tm, space, log_alpha, steps, *refs):
    early, late, (out, held, semaphores) = refs[:steps], refs[steps : 2 * steps], refs[2 * steps :]
    me, up = lax.axis_index(tm), upwards(space)
    depth, rows, columns = out.shape
    width = columns // steps
    tiles = width // lanes
    scale = jnp.exp(jnp.full((depth, lanes), me.astype(jnp.float32) * -log_alpha, jnp.float32))
    first = rows - reach
    rising = up == 1

    def at_row(behind, row, tile):
        if row < first:
            return early[behind][row * tiles + tile]
        return late[behind][(row - first) * tiles + tile]

    copies = []
    for behind in range(steps):
        owner = lax.rem(me - behind + steps, steps)
        for y in range(rows):
            for tile in range(tiles):
                if rows - reach <= min(y, rows - 1 - y):
                    value = late[behind][(row_of(y, rows, up) - first) * tiles + tile]
                else:
                    value = jnp.where(
                        rising, at_row(behind, y, tile), at_row(behind, rows - 1 - y, tile)
                    )
                place = pl.multiple_of((owner * tiles + tile) * lanes, lanes)
                held[:, y, pl.ds(place, lanes)] = value * scale
        part = pl.ds(pl.multiple_of(owner * width, lanes), width)
        copies.append(
            pltpu.make_async_copy(
                held.at[:, :, part], out.at[:, :, part], semaphores.at[behind]
            )
        )
        copies[-1].start()
    for copy in copies:
        copy.wait()


def exchange(blocks, steps):
    moved = []
    for d in range(1, steps):
        pairs = [(i, (i + d) % steps) for i in range(steps)]
        moved.append(lax.ppermute(blocks[d], "tm", pairs))
    return [blocks[0]] + moved


def swap(value, first):
    size, steps = lax.axis_size("space"), lax.axis_size("tm")
    pairs = []
    for step in range(steps):
        beside = step ^ 1 if steps % 2 == 0 else (step + 1) % steps
        for slab in range(size):
            partner = slab + 1 if (slab - first) % 2 == 0 else slab - 1
            target = (step, partner) if 0 <= partner < size else (beside, slab)
            pairs.append((step * size + slab, target[0] * size + target[1]))
    return lax.ppermute(value, ("tm", "space"), pairs)


def fast_local(rhs, diffusivity, velocity):
    _, depth, rows, columns = rhs.shape
    steps = lax.axis_size("tm")
    tiles = columns // steps // lanes
    log_alpha = math.log(circ_alpha) / steps
    extended, wide = rows + 2 * reach, tiles + 1
    fields = steps
    blocks = exchange(pack(rhs[0], steps), steps)
    made = [(extended, wide, depth, lanes), (fields, extended, wide, depth, lanes)]
    iterates = [(fields, extended, wide, depth + 16, lanes)] * reach
    own, kappa, inverse, drift, *margins = call(
        functools.partial(prepare_kernel, "tm", "space", rows, tiles, steps),
        [(rows * tiles + 1, depth, lanes), *made, (3, depth, lanes), *iterates],
        diffusivity,
        velocity,
        specs={0: hbm, 1: smem},
        scratch=staging(diffusivity.shape),
    )
    near, far = halos([*blocks, own], rows, tiles)
    far, near = swap(far, 1), swap(near, 0)
    state = [*made, *iterates, made[1]]
    early = rows - reach
    solve = functools.partial(solve_kernel, "tm", "space", rows, tiles, steps)
    kept = [kappa, inverse, *margins]
    held = call(
        functools.partial(solve, False),
        state + [(early * tiles, depth, lanes)] * steps,
        *blocks,
        near,
        drift,
        *kept,
        aliases={steps + 2 + i: i for i in range(len(kept))},
    )
    first_rows = exchange(held[len(state) :], steps)
    held = call(
        functools.partial(solve, True),
        state + [(reach * tiles, depth, lanes)] * steps,
        far,
        drift,
        *held[: len(state)],
        aliases={2 + i: i for i in range(len(state))},
    )
    last_rows = exchange(held[len(state) :], steps)
    (result,) = call(
        functools.partial(unpack_kernel, "tm", "space", log_alpha, steps),
        [(depth, rows, columns)],
        *first_rows,
        *last_rows,
        kept=False,
        scratch=[
            pltpu.VMEM((depth, rows, columns), jnp.float32),
            pltpu.SemaphoreType.DMA((steps,)),
        ],
    )
    return result[None]


def padded(shard, sides, width):
    for axis, dim in sides:
        size, length = (lax.axis_size(axis), shard.shape[dim])
        up = [(i, (i + 1) % size) for i in range(size - 1)]
        down = [(j, i) for i, j in up]
        last = lax.slice_in_dim(shard, length - width, length, axis=dim)
        initial = lax.slice_in_dim(shard, 0, width, axis=dim)
        before = lax.ppermute(last, axis, up)
        after = lax.ppermute(initial, axis, down)
        shard = jnp.concatenate([before, shard, after], axis=dim)
    return shard


def stencil(extended, diffusivity, diag_re, diag_im, velocity):
    center = extended[:, :, :, 1:-1, :]
    upper_y = extended[:, :, :, 2:, :]
    lower_y = extended[:, :, :, :-2, :]
    zero_z = jnp.zeros_like(center[:, :, :1])
    upper_z = jnp.concatenate([center[:, :, 1:], zero_z], axis=2)
    lower_z = jnp.concatenate([zero_z, center[:, :, :-1]], axis=2)
    zero_x = jnp.zeros_like(center[:, :, :, :, :1])
    upper_x = jnp.concatenate([center[:, :, :, :, 1:], zero_x], axis=4)
    lower_x = jnp.concatenate([zero_x, center[:, :, :, :, :-1]], axis=4)
    coefficient = diffusivity[None, None]
    half_velocity = 0.5 * velocity
    beside = (coefficient - half_velocity[0]) * upper_z + (coefficient + half_velocity[0]) * lower_z
    beside = (
        beside
        + (coefficient - half_velocity[1]) * upper_y
        + (coefficient + half_velocity[1]) * lower_y
    )
    beside = (
        beside
        + (coefficient - half_velocity[2]) * upper_x
        + (coefficient + half_velocity[2]) * lower_x
    )
    denominator = diag_re + 6.0 * diffusivity
    center_re = center[:, 0]
    center_im = center[:, 1]
    total_re = denominator * center_re - diag_im * center_im
    total_im = denominator * center_im + diag_im * center_re
    return jnp.stack([total_re, total_im], axis=1) - beside


def divide(residual, diffusivity, diag_re, diag_im):
    denominator = diag_re + 6.0 * diffusivity
    modulus = denominator * denominator + diag_im * diag_im
    residual_re = residual[:, 0]
    residual_im = residual[:, 1]
    quotient_re = (residual_re * denominator + residual_im * diag_im) / modulus
    quotient_im = (residual_im * denominator - residual_re * diag_im) / modulus
    return jnp.stack([quotient_re, quotient_im], axis=1)


def highest(left, right):
    return jnp.dot(left, right, precision=lax.Precision.HIGHEST, preferred_element_type=jnp.float32)


def twiddle(row_index, column_index, length):
    product = row_index[:, None] * column_index[None, :] % length
    phase_table = product.astype(jnp.float32) * (2.0 * math.pi / length)
    return (jnp.cos(phase_table), jnp.sin(phase_table))


def general_local(rhs, diffusivity, velocity):
    local_steps, depth, rows_y, rows_x = rhs.shape
    length = local_steps * lax.axis_size("tm")
    first_step = lax.axis_index("tm") * local_steps
    own_index = first_step + jnp.arange(local_steps, dtype=jnp.int32)
    log_alpha = math.log(circ_alpha) / length
    cell_count = depth * rows_y * rows_x
    scaled = (
        rhs.reshape(local_steps, cell_count)
        * jnp.exp(own_index.astype(jnp.float32) * log_alpha)[:, None]
    )
    regrouped = lax.all_to_all(scaled, "tm", split_axis=1, concat_axis=0, tiled=True)
    full_index = jnp.arange(length, dtype=jnp.int32)
    cosine_table, sine_table = twiddle(full_index, full_index, length)
    spectrum_re = highest(cosine_table, regrouped)
    spectrum_im = -highest(sine_table, regrouped)
    source_re, source_im = (
        lax.all_to_all(spectrum_re, "tm", split_axis=0, concat_axis=1, tiled=True),
        lax.all_to_all(spectrum_im, "tm", split_axis=0, concat_axis=1, tiled=True),
    )
    source = jnp.stack([source_re, source_im], axis=1).reshape(
        local_steps, 2, depth, rows_y, rows_x
    )
    phase_angle = own_index.astype(jnp.float32) * (2.0 * math.pi / length)
    shift_factor = circ_alpha ** (1.0 / length)
    diag_re = (1.0 - shift_factor * jnp.cos(phase_angle))[:, None, None, None]
    diag_im = (shift_factor * jnp.sin(phase_angle))[:, None, None, None]
    field = relax_weights[0] * divide(source, diffusivity, diag_re, diag_im)
    for weight in relax_weights[1:]:
        extended = padded(field, (("space", 3),), 1)
        applied = stencil(extended, diffusivity, diag_re, diag_im, velocity)
        field = field + weight * divide(source - applied, diffusivity, diag_re, diag_im)
    field_re = field[:, 0].reshape(local_steps, cell_count)
    field_im = field[:, 1].reshape(local_steps, cell_count)
    mixed_re, mixed_im = (
        lax.all_to_all(field_re, "tm", split_axis=1, concat_axis=0, tiled=True),
        lax.all_to_all(field_im, "tm", split_axis=1, concat_axis=0, tiled=True),
    )
    values = (highest(cosine_table, mixed_re) - highest(sine_table, mixed_im)) / length
    restored = lax.all_to_all(values, "tm", split_axis=0, concat_axis=1, tiled=True)
    result = restored * jnp.exp(-own_index.astype(jnp.float32) * log_alpha)[:, None]
    return result.reshape(local_steps, depth, rows_y, rows_x)


def local(rhs, diffusivity, velocity):
    steps = lax.axis_size("tm")
    local_steps, _, rows, columns = rhs.shape
    if local_steps == 1 and rows >= reach and lanes % rows == 0 and columns % (steps * lanes) == 0:
        return fast_local(rhs, diffusivity, velocity)
    return general_local(rhs, diffusivity, velocity)


def solution(mesh):
    return jax.shard_map(
        local,
        mesh=mesh,
        in_specs=(P(("parts", "tm"), None, "space", None), P("parts", "space", None), P("parts")),
        out_specs=P(("parts", "tm"), None, "space", None),
        check_vma=False,
    )
```

```python
import functools
import math

import jax
import jax.numpy as jnp
from jax import lax
from jax.experimental import pallas as pl
from jax.experimental.pallas import tpu as pltpu
from jax.sharding import PartitionSpec as P


circ_alpha = 0.1
relax_weights = (
    1.0 / (1.0 - 0.5 * math.cos(math.pi / 8.0)),
    1.0 / (1.0 - 0.5 * math.cos(3.0 * math.pi / 8.0)),
    1.0 / (1.0 - 0.5 * math.cos(5.0 * math.pi / 8.0)),
    1.0 / (1.0 - 0.5 * math.cos(7.0 * math.pi / 8.0)),
)


reach = len(relax_weights) - 1
lanes = 128
sublanes = 8
early_moves = (2, 3)
vmem = pl.BlockSpec(memory_space=pltpu.VMEM)
smem = pl.BlockSpec(memory_space=pltpu.SMEM)
hbm = pl.BlockSpec(memory_space=pltpu.HBM)


def call(kernel, outs, *operands, specs=None, kept=True, aliases=None, scratch=()):
    specs = specs or {}
    on_chip = [
        x
        if specs.get(i) is smem
        else pltpu.with_memory_space_constraint(x, pltpu.HBM if i in specs else pltpu.VMEM)
        for i, x in enumerate(operands)
    ]
    make = pltpu.VMEM if kept else jax.ShapeDtypeStruct
    return pl.pallas_call(
        kernel,
        out_shape=[make(o, jnp.float32) for o in outs],
        in_specs=[specs.get(i, vmem) for i in range(len(operands))],
        out_specs=[vmem if kept else hbm] * len(outs),
        scratch_shapes=scratch,
        input_output_aliases=aliases or {},
        compiler_params=pltpu.CompilerParams(vmem_limit_bytes=16 << 20),
    )(*on_chip)


def column_mask(left, right, shape):
    lane = lax.broadcasted_iota(jnp.int32, shape, 1)
    keep_right = (lane < reach).astype(jnp.float32) * right
    keep_left = (lane >= lanes - reach).astype(jnp.float32) * left
    return keep_right, keep_left


def upwards(space):
    return lax.rem(lax.axis_index(space), 2)


def row_of(y, rows, up):
    return up * y + (1 - up) * (rows - 1 - y)


def heading(step, steps):
    return 1 - 2 * (step % 2) if steps % 2 == 0 else 1


def slot_time(step, slot, steps):
    return (step + heading(step, steps) * slot) % steps


def slot_owner(me, slot, steps):
    forwards = 1 - 2 * lax.rem(me, 2) if steps % 2 == 0 else 1
    turn = forwards * slot if steps % 2 == 0 and slot % 2 else -forwards * slot
    return lax.rem(me + turn + steps, steps)


def put(block, index, value):
    sheets = value.shape[0] // sublanes
    block[pl.ds(index * sheets, sheets)] = value.reshape(sheets, sublanes, lanes)


def slot_width(rows, sheets):
    return lanes // (rows * sheets)


def pick_block(source, write, write_halo, owner, owners, up):
    depth, rows, columns = source.shape
    sheets = depth // sublanes
    width = slot_width(rows, sheets)
    total = columns // lanes
    tiles = total // owners
    left_tile = jnp.maximum(owner * tiles - 1, 0)
    right_tile = jnp.minimum((owner + 1) * tiles, total - 1)
    left = (owner > 0).astype(jnp.float32)
    right = (owner < owners - 1).astype(jnp.float32)
    keep_right, keep_left = column_mask(left, right, (depth, lanes))
    packed = None

    def tile_at(y, tile):
        return source[:, y, pl.ds(pl.multiple_of(tile * lanes, lanes), lanes)]

    for y in range(rows):
        row = row_of(y, rows, up)
        for tile in range(tiles):
            write(row * tiles + tile, tile_at(y, owner * tiles + tile))
        halo = tile_at(y, right_tile) * keep_right + tile_at(y, left_tile) * keep_left
        for sheet in range(sheets):
            part = halo[sheet * sublanes : (sheet + 1) * sublanes]
            part = pltpu.roll(part, (row * sheets + sheet) * width, 1)
            packed = part if packed is None else packed + part
    write_halo(packed)


def fetch(source, target, semaphores):
    pieces = semaphores.shape[0]
    size = source.shape[0] // pieces
    copies = [
        pltpu.make_async_copy(
            source.at[pl.ds(i * size, size)], target.at[pl.ds(i * size, size)], semaphores.at[i]
        )
        for i in range(pieces)
    ]
    for copy in copies:
        copy.start()
    for copy in copies:
        copy.wait()


def pack_kernel(tm, space, log_alpha, steps, rhs, *refs):
    outs, (held, semaphores) = refs[:steps], refs[steps:]
    me, up = lax.axis_index(tm), upwards(space)
    fetch(rhs, held, semaphores)
    scale = jnp.exp(jnp.full((sublanes, lanes), me.astype(jnp.float32) * log_alpha, jnp.float32))
    tall = jnp.concatenate([scale] * (rhs.shape[0] // sublanes))
    for ahead in reversed(range(steps)):
        out = outs[ahead]

        def write(index, value, out=out):
            put(out, index, value * tall)

        def write_halo(value, out=out):
            out[out.shape[0] - 1] = value * scale

        pick_block(held, write, write_halo, slot_owner(me, ahead, steps), steps, up)


def staging(shape):
    pieces = math.gcd(shape[0], 4)
    return [pltpu.VMEM(shape, jnp.float32), pltpu.SemaphoreType.DMA((pieces,))]


def pack(rhs, steps):
    depth, rows, columns = rhs.shape
    tiles = columns // steps // lanes
    log_alpha = math.log(circ_alpha) / steps
    kernel = functools.partial(pack_kernel, "tm", "space", log_alpha, steps)
    out = (rows * tiles * depth // sublanes + 1, sublanes, lanes)
    return call(kernel, [out] * steps, rhs, specs={0: hbm}, scratch=staging(rhs.shape))


def copy_piece(block, is_near, piece, target, first):
    last = block.shape[0] - 1
    start = 0 if is_near else last - (piece - 1)
    target[pl.ds(first, piece - 1)] = block[pl.ds(start, piece - 1)]
    target[first + piece - 1] = block[last]


def halo_kernel(piece, *refs):
    blocks, (near, far) = refs[:-2], refs[-2:]
    for step, block in enumerate(blocks):
        copy_piece(block, True, piece, near, step * piece)
        if (step + 1) * piece <= far.shape[0]:
            copy_piece(block, False, piece, far, step * piece)


def halos(blocks, own, piece):
    outs = [(count * piece, sublanes, lanes) for count in (len(blocks) + 1, len(blocks))]
    return call(functools.partial(halo_kernel, piece), outs, *blocks, own)


def row_piece(own, near, far, step, row, tile, rows, tiles, depth):
    sheets = depth // sublanes
    piece = reach * tiles * sheets + 1
    base, start, held = step * piece, 0, reach
    if row < reach:
        source, there = near, reach - 1 - row
    elif row < reach + rows:
        source, base, there, held = own, 0, row - reach, rows
    else:
        source, there, start = far, 2 * rows + reach - 1 - row, rows - reach
    if tile < tiles:
        first = base + ((there - start) * tiles + tile) * sheets
        return source[pl.ds(first, sheets)].reshape(depth, lanes)
    value = source[base + held * tiles * sheets]
    width = slot_width(rows, sheets)
    parts = []
    for sheet in range(sheets):
        shift = (there * sheets + sheet) * width
        parts.append(pltpu.roll(value, lanes - shift, 1) if shift else value)
    return jnp.concatenate(parts)


def frequencies(steps):
    return [(k, 2 * k % steps != 0) for k in range(steps // 2 + 1)]


def write_coefficients(tm, row, tile, value, mask, steps, kappa, inverse):
    backwards = lax.rem(lax.axis_index(tm), 2) if steps % 2 == 0 else 0
    turn = jnp.float32(1 - 2 * backwards)
    shift_factor = circ_alpha ** (1.0 / steps)
    kappa[row, tile] = value
    place = 0
    for k, is_complex in frequencies(steps):
        phase = 2.0 * math.pi * k / steps
        real = (1.0 - shift_factor * math.cos(phase)) + 6.0 * value
        if is_complex:
            imag = shift_factor * math.sin(phase)
            reciprocal = 1.0 / (real * real + imag * imag)
            pair = (real * reciprocal, (imag * turn) * reciprocal)
        else:
            pair = (1.0 / real,)
        for part in pair:
            inverse[place, row, tile] = part if mask is None else part * mask
            place += 1


def side_mask(tm, steps, depth):
    me = lax.axis_index(tm)
    keep_right, keep_left = column_mask(
        (me > 0).astype(jnp.float32), (me < steps - 1).astype(jnp.float32), (depth, lanes)
    )
    return keep_right + keep_left


def prepare_kernel(tm, space, rows, tiles, steps, diffusivity, velocity, *refs):
    own, own_far, kappa, inverse, drift, *iterates = refs[:-2]
    held, semaphores = refs[-2:]
    up = upwards(space)
    depth = diffusivity.shape[0]
    direction = (2 * up - 1).astype(jnp.float32)
    for j in range(3):
        speed = 0.5 * velocity[j]
        drift[j] = jnp.full((depth, lanes), speed * direction if j == 1 else speed, jnp.float32)
    zero = jnp.zeros((8, lanes), jnp.float32)
    for level, ref in enumerate(iterates):
        fields, extended, wide = ref.shape[:3]
        for field in range(fields):
            for row in range(level, extended - level):
                for tile in range(wide):
                    ref[field, row, tile, pl.ds(0, 8), :] = zero
                    ref[field, row, tile, pl.ds(8 + depth, 8), :] = zero
    fetch(diffusivity, held, semaphores)

    def write(index, value):
        put(own, index, value)

    def write_halo(value):
        own[own.shape[0] - 1] = value

    pick_block(held, write, write_halo, lax.axis_index(tm), steps, up)
    copy_piece(own, False, own_far.shape[0], own_far, 0)
    halo_mask = side_mask(tm, steps, depth)
    for row in range(reach, reach + rows):
        for tile in range(tiles + 1):
            value = row_piece(own, None, None, 0, row, tile, rows, tiles, depth)
            mask = halo_mask if tile == tiles else None
            write_coefficients(tm, row, tile, value, mask, steps, kappa, inverse)


def combine(terms):
    total = None
    for factor, value in terms:
        if factor == 0.0:
            continue
        if total is None:
            total = value if factor == 1.0 else factor * value
        elif factor == 1.0:
            total = total + value
        elif factor == -1.0:
            total = total - value
        else:
            total = total + factor * value
    return total


def exact(value):
    return float(round(value)) if abs(value - round(value)) < 1e-12 else value


def cosine(product, steps):
    return exact(math.cos(2.0 * math.pi * (product % steps) / steps))


def sine(product, steps):
    return exact(math.sin(2.0 * math.pi * (product % steps) / steps))


def solve_kernel(tm, space, rows, tiles, steps, second_half, *refs):
    freqs = frequencies(steps)
    fields = sum(2 if c else 1 for _, c in freqs)
    levels = reach
    made = 2 + levels
    if second_half:
        far, kappa_far, drift = refs[:3]
        done = sum(ahead not in early_moves for ahead in range(1, steps))
        finished, refs = refs[4 + made : 4 + made + done], refs[4 + made + done :]
        kappa, inverse, *iterates = refs[:made]
        source, *outs = refs[made:]
        blocks, near = [None] * steps, None
    else:
        blocks, (near, drift) = refs[:steps], refs[steps : steps + 2]
        kappa, inverse, *iterates = refs[steps + 2 + made :][:made]
        source, *outs = refs[steps + 2 + made + made :]
        far, kappa_far = None, None
    depth = kappa.shape[2]
    pad = 8
    middle = pl.ds(pad, depth)
    lane = lax.broadcasted_iota(jnp.int32, (depth, lanes), 1)
    at_first, at_last = lane == 0, lane == lanes - 1
    half = [drift[j] for j in range(3)]
    known = reach + rows
    extended = known + reach
    wide = tiles + 1

    def rows_of(level):
        split = known - level
        return (split, extended - level) if second_half else (level, split)

    slab, slabs, up = lax.axis_index(space), lax.axis_size(space), upwards(space)
    beyond = slab < slabs - 1 if second_half else slab > 0
    before = slab > 0 if second_half else slab < slabs - 1
    inside = jnp.where(up == 1, beyond, before).astype(jnp.float32)
    halo_mask = side_mask(tm, steps, depth) * inside
    row_mask = jnp.full((depth, lanes), inside, jnp.float32)
    for row in range(known, extended) if second_half else range(reach):
        for tile in range(wide):
            step = 0 if second_half else steps
            value = row_piece(None, near, kappa_far, step, row, tile, rows, tiles, depth)
            mask = halo_mask if tile == tiles else row_mask
            write_coefficients(tm, row, tile, value, mask, steps, kappa, inverse)

    def divide(values, row, tile):
        result, place = [], 0
        for _, is_complex in freqs:
            if is_complex:
                re, im = values[place], values[place + 1]
                p, q = inverse[place, row, tile], inverse[place + 1, row, tile]
                result += [re * p + im * q, im * p - re * q]
                place += 2
            else:
                result.append(values[place] * inverse[place, row, tile])
                place += 1
        return result

    for row in range(*rows_of(0)):
        for tile in range(wide):
            if tile == tiles and not 1 <= row < extended - 1:
                continue
            held = [
                row_piece(blocks[b], near, far, b, row, tile, rows, tiles, depth)
                for b in range(steps)
            ]
            values = []
            for k, is_complex in freqs:
                values.append(combine((cosine(k * b, steps), held[b]) for b in range(steps)))
                if is_complex:
                    values.append(combine((-sine(k * b, steps), held[b]) for b in range(steps)))
            quotients = divide(values, row, tile)
            for field in range(fields):
                source[field, row, tile] = values[field]
                iterates[0][field, row, tile, middle, :] = relax_weights[0] * quotients[field]

    def sweep(row, old, weight, last):
        centers = [
            [old[field, row, tile, middle, :] for tile in range(wide)] for field in range(fields)
        ]
        shifted_down = [[pltpu.roll(c, 1, 1) for c in line] for line in centers]
        shifted_up = [[pltpu.roll(c, lanes - 1, 1) for c in line] for line in centers]
        for tile in range(tiles if last else wide):
            values = []
            coefficient = kappa[row, tile]
            for field in range(fields):
                lower_x = jnp.where(
                    at_first, shifted_down[field][(tile - 1) % wide], shifted_down[field][tile]
                )
                upper_x = jnp.where(
                    at_last, shifted_up[field][(tile + 1) % wide], shifted_up[field][tile]
                )
                lower_z = old[field, row, tile, pl.ds(pad - 1, depth), :]
                upper_z = old[field, row, tile, pl.ds(pad + 1, depth), :]
                lower_y = old[field, row - 1, tile, middle, :]
                upper_y = old[field, row + 1, tile, middle, :]
                around = (lower_z + upper_z) + (lower_y + upper_y) + (lower_x + upper_x)
                slope = (
                    half[0] * (lower_z - upper_z)
                    + half[1] * (lower_y - upper_y)
                    + half[2] * (lower_x - upper_x)
                )
                values.append(source[field, row, tile] + (coefficient * around + slope))
            quotients = divide(values, row, tile)
            yield tile, [
                (1.0 - weight) * centers[field][tile] + weight * quotients[field]
                for field in range(fields)
            ]

    for level in range(1, levels):

        def step(row, carry, level=level):
            for tile, results in sweep(row, iterates[level - 1], relax_weights[level], False):
                for field in range(fields):
                    iterates[level][field, row, tile, middle, :] = results[field]
            return carry

        lax.fori_loop(*rows_of(level), step, 0)

    last_rows = rows_of(levels)
    skipped = [0] * steps
    if second_half:
        whole = [ahead for ahead in range(1, steps) if ahead not in early_moves]
        for ahead, block in zip(whole, finished, strict=True):
            skipped[ahead] = (rows - reach) * tiles
            outs[ahead][pl.ds(0, block.shape[0])] = block[...]

    def last_step(row, carry):
        for tile, results in sweep(row, iterates[levels - 1], relax_weights[levels], True):
            for ahead in range(steps):
                terms, field = [], 0
                for k, is_complex in freqs:
                    factor = (2.0 if is_complex else 1.0) / steps
                    terms.append((factor * cosine(k * ahead, steps), results[field]))
                    field += 1
                    if is_complex:
                        terms.append((-factor * sine(k * ahead, steps), results[field]))
                        field += 1
                place = (row - last_rows[0]) * tiles + tile + skipped[ahead]
                outs[ahead][place] = combine(terms)
        return carry

    lax.fori_loop(*last_rows, last_step, 0)


def unpack_kernel(tm, space, log_alpha, steps, early, *refs):
    refs = list(refs)
    heads = [refs.pop(0) if two else None for two in early]
    tails, (out, held, semaphores) = refs[:steps], refs[steps:]
    me, up = lax.axis_index(tm), upwards(space)
    depth, rows, columns = out.shape
    width = columns // steps
    tiles = width // lanes
    scale = jnp.exp(jnp.full((depth, lanes), me.astype(jnp.float32) * -log_alpha, jnp.float32))
    first = rows - reach
    rising = up == 1

    def at_row(behind, row, tile):
        if heads[behind] is None:
            return tails[behind][row * tiles + tile]
        if row < first:
            return heads[behind][row * tiles + tile]
        return tails[behind][(row - first) * tiles + tile]

    copies = []
    for behind in range(steps):
        owner = slot_owner(me, behind, steps)
        for y in range(rows):
            for tile in range(tiles):
                value = jnp.where(
                    rising, at_row(behind, y, tile), at_row(behind, rows - 1 - y, tile)
                )
                place = pl.multiple_of((owner * tiles + tile) * lanes, lanes)
                held[:, y, pl.ds(place, lanes)] = value * scale
        part = pl.ds(pl.multiple_of(owner * width, lanes), width)
        copies.append(
            pltpu.make_async_copy(
                held.at[:, :, part], out.at[:, :, part], semaphores.at[behind]
            )
        )
        copies[-1].start()
    for copy in copies:
        copy.wait()


def gather(blocks, steps):
    result = [blocks[0]] + [None] * (steps - 1)
    for d in reversed(range(1, steps)):
        pairs = [(slot_time(t, d, steps), t) for t in range(steps)]
        result[d] = lax.ppermute(blocks[d], "tm", pairs)
    return result


def scatter(blocks, steps):
    result = list(blocks)
    for d in reversed(range(1, steps)):
        if blocks[d] is not None:
            pairs = [(t, slot_time(t, d, steps)) for t in range(steps)]
            result[d] = lax.ppermute(blocks[d], "tm", pairs)
    return result


def swap(value, first):
    names = ("parts", "tm", "space")
    parts, steps, size = (lax.axis_size(name) for name in names)
    pairs = []
    for part in range(parts):
        for step in range(steps):
            beside = (part ^ 1, step) if parts % 2 == 0 else (part, (step + 1) % steps)
            for slab in range(size):
                partner = slab + 1 if (slab - first) % 2 == 0 else slab - 1
                target = (part, step, partner) if 0 <= partner < size else (*beside, slab)
                here, there = (
                    (p * steps + t) * size + c for p, t, c in ((part, step, slab), target)
                )
                pairs.append((here, there))
    return lax.ppermute(value, names, pairs)


def fast_local(rhs, diffusivity, velocity):
    _, depth, rows, columns = rhs.shape
    steps = lax.axis_size("tm")
    tiles = columns // steps // lanes
    sheets = depth // sublanes
    log_alpha = math.log(circ_alpha) / steps
    extended, wide = rows + 2 * reach, tiles + 1
    fields = steps
    blocks = gather(pack(rhs[0], steps), steps)
    piece = reach * tiles * sheets + 1
    made = [(extended, wide, depth, lanes), (fields, extended, wide, depth, lanes)]
    iterates = [(fields, extended, wide, depth + 16, lanes)] * reach
    own, own_far, kappa, inverse, drift, *margins = call(
        functools.partial(prepare_kernel, "tm", "space", rows, tiles, steps),
        [
            (rows * tiles * sheets + 1, sublanes, lanes),
            (piece, sublanes, lanes),
            *made,
            (3, depth, lanes),
            *iterates,
        ],
        diffusivity,
        velocity,
        specs={0: hbm, 1: smem},
        scratch=staging(diffusivity.shape),
    )
    kappa_far = swap(own_far, 1)
    near, far = halos(blocks, own, piece)
    far, near = swap(far, 1), swap(near, 0)
    state = [*made, *iterates, made[1]]
    early = rows - reach
    solve = functools.partial(solve_kernel, "tm", "space", rows, tiles, steps)
    kept = [kappa, inverse, *margins]
    held = call(
        functools.partial(solve, False),
        state + [(early * tiles, depth, lanes)] * steps,
        *blocks,
        near,
        drift,
        *kept,
        aliases={steps + 2 + i: i for i in range(len(kept))},
    )
    state_now, finished = held[: len(state)], held[len(state) :]
    in_two = [d == 0 or d in early_moves for d in range(steps)]
    heads = scatter([finished[d] if in_two[d] else None for d in range(steps)], steps)
    heads = [head for head in heads if head is not None]
    held = call(
        functools.partial(solve, True),
        state + [((reach if two else rows) * tiles, depth, lanes) for two in in_two],
        far,
        kappa_far,
        drift,
        *state_now,
        *(finished[d] for d in range(steps) if not in_two[d]),
        aliases={3 + i: i for i in range(len(state))},
    )
    tails = scatter(held[len(state) :], steps)
    (result,) = call(
        functools.partial(unpack_kernel, "tm", "space", log_alpha, steps, tuple(in_two)),
        [(depth, rows, columns)],
        *heads,
        *tails,
        kept=False,
        scratch=[
            pltpu.VMEM((depth, rows, columns), jnp.float32),
            pltpu.SemaphoreType.DMA((steps,)),
        ],
    )
    return result[None]


def padded(shard, sides, width):
    for axis, dim in sides:
        size, length = (lax.axis_size(axis), shard.shape[dim])
        up = [(i, (i + 1) % size) for i in range(size - 1)]
        down = [(j, i) for i, j in up]
        last = lax.slice_in_dim(shard, length - width, length, axis=dim)
        initial = lax.slice_in_dim(shard, 0, width, axis=dim)
        before = lax.ppermute(last, axis, up)
        after = lax.ppermute(initial, axis, down)
        shard = jnp.concatenate([before, shard, after], axis=dim)
    return shard


def stencil(extended, diffusivity, diag_re, diag_im, velocity):
    center = extended[:, :, :, 1:-1, :]
    upper_y = extended[:, :, :, 2:, :]
    lower_y = extended[:, :, :, :-2, :]
    zero_z = jnp.zeros_like(center[:, :, :1])
    upper_z = jnp.concatenate([center[:, :, 1:], zero_z], axis=2)
    lower_z = jnp.concatenate([zero_z, center[:, :, :-1]], axis=2)
    zero_x = jnp.zeros_like(center[:, :, :, :, :1])
    upper_x = jnp.concatenate([center[:, :, :, :, 1:], zero_x], axis=4)
    lower_x = jnp.concatenate([zero_x, center[:, :, :, :, :-1]], axis=4)
    coefficient = diffusivity[None, None]
    half_velocity = 0.5 * velocity
    beside = (coefficient - half_velocity[0]) * upper_z + (coefficient + half_velocity[0]) * lower_z
    beside = (
        beside
        + (coefficient - half_velocity[1]) * upper_y
        + (coefficient + half_velocity[1]) * lower_y
    )
    beside = (
        beside
        + (coefficient - half_velocity[2]) * upper_x
        + (coefficient + half_velocity[2]) * lower_x
    )
    denominator = diag_re + 6.0 * diffusivity
    center_re = center[:, 0]
    center_im = center[:, 1]
    total_re = denominator * center_re - diag_im * center_im
    total_im = denominator * center_im + diag_im * center_re
    return jnp.stack([total_re, total_im], axis=1) - beside


def divide(residual, diffusivity, diag_re, diag_im):
    denominator = diag_re + 6.0 * diffusivity
    modulus = denominator * denominator + diag_im * diag_im
    residual_re = residual[:, 0]
    residual_im = residual[:, 1]
    quotient_re = (residual_re * denominator + residual_im * diag_im) / modulus
    quotient_im = (residual_im * denominator - residual_re * diag_im) / modulus
    return jnp.stack([quotient_re, quotient_im], axis=1)


def highest(left, right):
    return jnp.dot(left, right, precision=lax.Precision.HIGHEST, preferred_element_type=jnp.float32)


def twiddle(row_index, column_index, length):
    product = row_index[:, None] * column_index[None, :] % length
    phase_table = product.astype(jnp.float32) * (2.0 * math.pi / length)
    return (jnp.cos(phase_table), jnp.sin(phase_table))


def general_local(rhs, diffusivity, velocity):
    local_steps, depth, rows_y, rows_x = rhs.shape
    length = local_steps * lax.axis_size("tm")
    first_step = lax.axis_index("tm") * local_steps
    own_index = first_step + jnp.arange(local_steps, dtype=jnp.int32)
    log_alpha = math.log(circ_alpha) / length
    cell_count = depth * rows_y * rows_x
    scaled = (
        rhs.reshape(local_steps, cell_count)
        * jnp.exp(own_index.astype(jnp.float32) * log_alpha)[:, None]
    )
    regrouped = lax.all_to_all(scaled, "tm", split_axis=1, concat_axis=0, tiled=True)
    full_index = jnp.arange(length, dtype=jnp.int32)
    cosine_table, sine_table = twiddle(full_index, full_index, length)
    spectrum_re = highest(cosine_table, regrouped)
    spectrum_im = -highest(sine_table, regrouped)
    source_re, source_im = (
        lax.all_to_all(spectrum_re, "tm", split_axis=0, concat_axis=1, tiled=True),
        lax.all_to_all(spectrum_im, "tm", split_axis=0, concat_axis=1, tiled=True),
    )
    source = jnp.stack([source_re, source_im], axis=1).reshape(
        local_steps, 2, depth, rows_y, rows_x
    )
    phase_angle = own_index.astype(jnp.float32) * (2.0 * math.pi / length)
    shift_factor = circ_alpha ** (1.0 / length)
    diag_re = (1.0 - shift_factor * jnp.cos(phase_angle))[:, None, None, None]
    diag_im = (shift_factor * jnp.sin(phase_angle))[:, None, None, None]
    field = relax_weights[0] * divide(source, diffusivity, diag_re, diag_im)
    for weight in relax_weights[1:]:
        extended = padded(field, (("space", 3),), 1)
        applied = stencil(extended, diffusivity, diag_re, diag_im, velocity)
        field = field + weight * divide(source - applied, diffusivity, diag_re, diag_im)
    field_re = field[:, 0].reshape(local_steps, cell_count)
    field_im = field[:, 1].reshape(local_steps, cell_count)
    mixed_re, mixed_im = (
        lax.all_to_all(field_re, "tm", split_axis=1, concat_axis=0, tiled=True),
        lax.all_to_all(field_im, "tm", split_axis=1, concat_axis=0, tiled=True),
    )
    values = (highest(cosine_table, mixed_re) - highest(sine_table, mixed_im)) / length
    restored = lax.all_to_all(values, "tm", split_axis=0, concat_axis=1, tiled=True)
    result = restored * jnp.exp(-own_index.astype(jnp.float32) * log_alpha)[:, None]
    return result.reshape(local_steps, depth, rows_y, rows_x)


def local(rhs, diffusivity, velocity):
    steps = lax.axis_size("tm")
    local_steps, depth, rows, columns = rhs.shape
    slots = rows * (depth // sublanes)
    tiled = columns % (steps * lanes) == 0 and depth % sublanes == 0
    if local_steps == 1 and rows >= reach and tiled and 2 * reach * slots <= lanes:
        return fast_local(rhs, diffusivity, velocity)
    return general_local(rhs, diffusivity, velocity)


def solution(mesh):
    return jax.shard_map(
        local,
        mesh=mesh,
        in_specs=(P(("parts", "tm"), None, "space", None), P("parts", "space", None), P("parts")),
        out_specs=P(("parts", "tm"), None, "space", None),
        check_vma=False,
    )
```

```python
import functools
import math

import jax
import jax.numpy as jnp
from jax import lax
from jax.experimental import pallas as pl
from jax.experimental.pallas import tpu as pltpu
from jax.sharding import PartitionSpec as P


circ_alpha = 0.1
relax_weights = (
    1.0 / (1.0 - 0.5 * math.cos(math.pi / 8.0)),
    1.0 / (1.0 - 0.5 * math.cos(3.0 * math.pi / 8.0)),
    1.0 / (1.0 - 0.5 * math.cos(5.0 * math.pi / 8.0)),
    1.0 / (1.0 - 0.5 * math.cos(7.0 * math.pi / 8.0)),
)


reach = len(relax_weights) - 1
lanes = 128
sublanes = 8
early_moves = (2, 3)
vmem = pl.BlockSpec(memory_space=pltpu.VMEM)
smem = pl.BlockSpec(memory_space=pltpu.SMEM)
hbm = pl.BlockSpec(memory_space=pltpu.HBM)


def call(kernel, outs, *operands, specs=None, kept=True, aliases=None, scratch=()):
    specs = specs or {}
    on_chip = [
        x
        if specs.get(i) is smem
        else pltpu.with_memory_space_constraint(x, pltpu.HBM if i in specs else pltpu.VMEM)
        for i, x in enumerate(operands)
    ]
    make = pltpu.VMEM if kept else jax.ShapeDtypeStruct
    return pl.pallas_call(
        kernel,
        out_shape=[make(o, jnp.float32) for o in outs],
        in_specs=[specs.get(i, vmem) for i in range(len(operands))],
        out_specs=[vmem if kept else hbm] * len(outs),
        scratch_shapes=scratch,
        input_output_aliases=aliases or {},
        compiler_params=pltpu.CompilerParams(vmem_limit_bytes=16 << 20),
    )(*on_chip)


def column_mask(left, right, shape):
    lane = lax.broadcasted_iota(jnp.int32, shape, 1)
    keep_right = (lane < reach).astype(jnp.float32) * right
    keep_left = (lane >= lanes - reach).astype(jnp.float32) * left
    return keep_right, keep_left


def upwards(space):
    return lax.rem(lax.axis_index(space), 2)


def row_of(y, rows, up):
    return up * y + (1 - up) * (rows - 1 - y)


def heading(step, steps):
    return 1 - 2 * (step % 2) if steps % 2 == 0 else 1


def slot_time(step, slot, steps):
    return (step + heading(step, steps) * slot) % steps


def slot_owner(me, slot, steps):
    forwards = 1 - 2 * lax.rem(me, 2) if steps % 2 == 0 else 1
    turn = forwards * slot if steps % 2 == 0 and slot % 2 else -forwards * slot
    return lax.rem(me + turn + steps, steps)


def put(block, index, value):
    sheets = value.shape[0] // sublanes
    block[pl.ds(index * sheets, sheets)] = value.reshape(sheets, sublanes, lanes)


def slot_width(rows, sheets):
    return lanes // (rows * sheets)


def turn(source, target, scale=None):
    _, rows, columns = source.shape
    for tile in range(columns // lanes):
        column = pltpu.einshape("zyx->yzx", source[:, :, tile * lanes : (tile + 1) * lanes])
        target[pl.ds(tile * rows, rows)] = column if scale is None else column * scale


def pick_block(source, rows, out, owner, owners, up):
    count, depth, _ = source.shape
    sheets = depth // sublanes
    width = slot_width(rows, sheets)
    total = count // rows
    tiles = total // owners
    left_tile = jnp.maximum(owner * tiles - 1, 0)
    right_tile = jnp.minimum((owner + 1) * tiles, total - 1)
    left = (owner > 0).astype(jnp.float32)
    right = (owner < owners - 1).astype(jnp.float32)
    keep_right, keep_left = column_mask(left, right, (depth, lanes))
    packed = None
    for y in range(rows):
        row = row_of(y, rows, up)
        for tile in range(tiles):
            put(out, row * tiles + tile, source[(owner * tiles + tile) * rows + y])
        halo = source[right_tile * rows + y] * keep_right + source[left_tile * rows + y] * keep_left
        for sheet in range(sheets):
            part = halo[sheet * sublanes : (sheet + 1) * sublanes]
            part = pltpu.roll(part, (row * sheets + sheet) * width, 1)
            packed = part if packed is None else packed + part
    out[out.shape[0] - 1] = packed


def fetch(source, target, semaphores):
    pieces = semaphores.shape[0]
    size = source.shape[0] // pieces
    copies = [
        pltpu.make_async_copy(
            source.at[pl.ds(i * size, size)], target.at[pl.ds(i * size, size)], semaphores.at[i]
        )
        for i in range(pieces)
    ]
    for copy in copies:
        copy.start()
    for copy in copies:
        copy.wait()


def pack_kernel(tm, space, log_alpha, steps, rhs, *refs):
    outs, (held, semaphores, turned) = refs[:steps], refs[steps:]
    me, up = lax.axis_index(tm), upwards(space)
    fetch(rhs, held, semaphores)
    shape = (1, rhs.shape[0], lanes)
    turn(held, turned, jnp.exp(jnp.full(shape, me.astype(jnp.float32) * log_alpha, jnp.float32)))
    for ahead in reversed(range(steps)):
        pick_block(turned, rhs.shape[1], outs[ahead], slot_owner(me, ahead, steps), steps, up)


def staging(shape):
    depth, rows, columns = shape
    return [
        pltpu.VMEM(shape, jnp.float32),
        pltpu.SemaphoreType.DMA((math.gcd(depth, 4),)),
        pltpu.VMEM((columns // lanes * rows, depth, lanes), jnp.float32),
    ]


def pack(rhs, steps):
    depth, rows, columns = rhs.shape
    tiles = columns // steps // lanes
    log_alpha = math.log(circ_alpha) / steps
    kernel = functools.partial(pack_kernel, "tm", "space", log_alpha, steps)
    out = (rows * tiles * depth // sublanes + 1, sublanes, lanes)
    return call(kernel, [out] * steps, rhs, specs={0: hbm}, scratch=staging(rhs.shape))


def copy_piece(block, is_near, piece, target, first):
    last = block.shape[0] - 1
    start = 0 if is_near else last - (piece - 1)
    target[pl.ds(first, piece - 1)] = block[pl.ds(start, piece - 1)]
    target[first + piece - 1] = block[last]


def halo_kernel(piece, *refs):
    blocks, (near, far) = refs[:-3], refs[-2:]
    for step, block in enumerate(blocks):
        copy_piece(block, True, piece, near, step * piece)
        if (step + 1) * piece <= far.shape[0]:
            copy_piece(block, False, piece, far, step * piece)


def halos(blocks, own, ready, piece):
    outs = [(count * piece, sublanes, lanes) for count in (len(blocks) + 1, len(blocks))]
    return call(functools.partial(halo_kernel, piece), outs, *blocks, own, ready)


def row_piece(own, near, far, step, row, tile, rows, tiles, depth):
    sheets = depth // sublanes
    piece = reach * tiles * sheets + 1
    base, start, held = step * piece, 0, reach
    if row < reach:
        source, there = near, reach - 1 - row
    elif row < reach + rows:
        source, base, there, held = own, 0, row - reach, rows
    else:
        source, there, start = far, 2 * rows + reach - 1 - row, rows - reach
    if tile < tiles:
        first = base + ((there - start) * tiles + tile) * sheets
        return source[pl.ds(first, sheets)].reshape(depth, lanes)
    value = source[base + held * tiles * sheets]
    width = slot_width(rows, sheets)
    parts = []
    for sheet in range(sheets):
        shift = (there * sheets + sheet) * width
        parts.append(pltpu.roll(value, lanes - shift, 1) if shift else value)
    return jnp.concatenate(parts)


def frequencies(steps):
    return [(k, 2 * k % steps != 0) for k in range(steps // 2 + 1)]


def write_coefficients(tm, row, tile, value, mask, steps, kappa, inverse):
    backwards = lax.rem(lax.axis_index(tm), 2) if steps % 2 == 0 else 0
    turn = jnp.float32(1 - 2 * backwards)
    shift_factor = circ_alpha ** (1.0 / steps)
    kappa[row, tile] = value
    place = 0
    for k, is_complex in frequencies(steps):
        phase = 2.0 * math.pi * k / steps
        real = (1.0 - shift_factor * math.cos(phase)) + 6.0 * value
        if is_complex:
            imag = shift_factor * math.sin(phase)
            reciprocal = 1.0 / (real * real + imag * imag)
            pair = (real * reciprocal, (imag * turn) * reciprocal)
        else:
            pair = (1.0 / real,)
        for part in pair:
            inverse[place, row, tile] = part if mask is None else part * mask
            place += 1


def side_mask(tm, steps, depth):
    me = lax.axis_index(tm)
    keep_right, keep_left = column_mask(
        (me > 0).astype(jnp.float32), (me < steps - 1).astype(jnp.float32), (depth, lanes)
    )
    return keep_right + keep_left


def kappa_kernel(tm, space, steps, diffusivity, velocity, *refs):
    own, own_far, drift, held, semaphores, turned, speeds, semaphore = refs
    up = upwards(space)
    copy = pltpu.make_async_copy(velocity, speeds, semaphore)
    copy.start()
    fetch(diffusivity, held, semaphores)

    turn(held, turned)
    pick_block(turned, diffusivity.shape[1], own, lax.axis_index(tm), steps, up)
    copy_piece(own, False, own_far.shape[0], own_far, 0)
    copy.wait()
    direction = (2 * up - 1).astype(jnp.float32)
    for j in range(3):
        speed = 0.5 * speeds[j]
        drift[j] = jnp.full(drift.shape[1:], speed * direction if j == 1 else speed, jnp.float32)


def prepare_kernel(tm, rows, tiles, steps, own, kappa, inverse, *iterates):
    depth = kappa.shape[2]
    zero = jnp.zeros((8, lanes), jnp.float32)
    for level, ref in enumerate(iterates):
        fields, extended, wide = ref.shape[:3]
        for field in range(fields):
            for row in range(level, extended - level):
                for tile in range(wide):
                    ref[field, row, tile, pl.ds(0, 8), :] = zero
                    ref[field, row, tile, pl.ds(8 + depth, 8), :] = zero
    halo_mask = side_mask(tm, steps, depth)
    for row in range(reach, reach + rows):
        for tile in range(tiles + 1):
            value = row_piece(own, None, None, 0, row, tile, rows, tiles, depth)
            mask = halo_mask if tile == tiles else None
            write_coefficients(tm, row, tile, value, mask, steps, kappa, inverse)


def combine(terms):
    total = None
    for factor, value in terms:
        if factor == 0.0:
            continue
        if total is None:
            total = value if factor == 1.0 else factor * value
        elif factor == 1.0:
            total = total + value
        elif factor == -1.0:
            total = total - value
        else:
            total = total + factor * value
    return total


def exact(value):
    return float(round(value)) if abs(value - round(value)) < 1e-12 else value


def cosine(product, steps):
    return exact(math.cos(2.0 * math.pi * (product % steps) / steps))


def sine(product, steps):
    return exact(math.sin(2.0 * math.pi * (product % steps) / steps))


def solve_kernel(tm, space, rows, tiles, steps, second_half, *refs):
    freqs = frequencies(steps)
    fields = sum(2 if c else 1 for _, c in freqs)
    levels = reach
    made = 2 + levels
    if second_half:
        far, kappa_far, drift = refs[:3]
        done = sum(ahead not in early_moves for ahead in range(1, steps))
        finished, refs = refs[3 + made : 3 + made + done], refs[3 + made + done :]
        kappa, inverse, *iterates = refs[:made]
        outs = refs[made:]
        blocks, near = [None] * steps, None
    else:
        blocks, (near, drift) = refs[:steps], refs[steps : steps + 2]
        kappa, inverse, *iterates = refs[steps + 2 + made :][:made]
        outs = refs[steps + 2 + made + made :]
        far, kappa_far = None, None
    depth = kappa.shape[2]
    pad = 8
    middle = pl.ds(pad, depth)
    lane = lax.broadcasted_iota(jnp.int32, (depth, lanes), 1)
    at_first, at_last = lane == 0, lane == lanes - 1
    half = [drift[j] for j in range(3)]
    known = reach + rows
    extended = known + reach
    wide = tiles + 1

    def rows_of(level):
        split = known - level
        return (split, extended - level) if second_half else (level, split)

    slab, slabs, up = lax.axis_index(space), lax.axis_size(space), upwards(space)
    beyond = slab < slabs - 1 if second_half else slab > 0
    before = slab > 0 if second_half else slab < slabs - 1
    inside = jnp.where(up == 1, beyond, before).astype(jnp.float32)
    halo_mask = side_mask(tm, steps, depth) * inside
    row_mask = jnp.full((depth, lanes), inside, jnp.float32)
    for row in range(known, extended) if second_half else range(reach):
        for tile in range(wide):
            step = 0 if second_half else steps
            value = row_piece(None, near, kappa_far, step, row, tile, rows, tiles, depth)
            mask = halo_mask if tile == tiles else row_mask
            write_coefficients(tm, row, tile, value, mask, steps, kappa, inverse)

    def divide(values, row, tile):
        result, place = [], 0
        for _, is_complex in freqs:
            if is_complex:
                re, im = values[place], values[place + 1]
                p, q = inverse[place, row, tile], inverse[place + 1, row, tile]
                result += [re * p + im * q, im * p - re * q]
                place += 2
            else:
                result.append(values[place] * inverse[place, row, tile])
                place += 1
        return result

    for row in range(*rows_of(0)):
        for tile in range(wide):
            if tile == tiles and not 1 <= row < extended - 1:
                continue
            held = [
                row_piece(blocks[b], near, far, b, row, tile, rows, tiles, depth)
                for b in range(steps)
            ]
            values = []
            for k, is_complex in freqs:
                values.append(combine((cosine(k * b, steps), held[b]) for b in range(steps)))
                if is_complex:
                    values.append(combine((-sine(k * b, steps), held[b]) for b in range(steps)))
            quotients = divide(values, row, tile)
            for field in range(fields):
                iterates[0][field, row, tile, middle, :] = quotients[field]


    def sweep(row, level):
        with_halo = level < row < extended - 1 - level and level < levels
        old = iterates[level - 1]
        scale, weight = relax_weights[level - 1], relax_weights[level]
        keep = (1.0 - weight) * scale / weight + (1.0 if level == 1 else 0.0)
        tilt = [scale * h for h in half]
        centers = [
            [old[field, row, tile, middle, :] for tile in range(wide)] for field in range(fields)
        ]
        shifted_down = [[pltpu.roll(c, 1, 1) for c in line] for line in centers]
        shifted_up = [[pltpu.roll(c, lanes - 1, 1) for c in line] for line in centers]
        for tile in range(wide if with_halo else tiles):
            values = []
            scaled = scale * kappa[row, tile]
            below = [scaled + t for t in tilt]
            above = [scaled - t for t in tilt]
            for field in range(fields):
                lower_x = jnp.where(
                    at_first, shifted_down[field][(tile - 1) % wide], shifted_down[field][tile]
                )
                upper_x = jnp.where(
                    at_last, shifted_up[field][(tile + 1) % wide], shifted_up[field][tile]
                )
                lower_z = old[field, row, tile, pl.ds(pad - 1, depth), :]
                upper_z = old[field, row, tile, pl.ds(pad + 1, depth), :]
                lower_y = old[field, row - 1, tile, middle, :]
                upper_y = old[field, row + 1, tile, middle, :]
                values.append(
                    (below[0] * lower_z + above[0] * upper_z)
                    + (below[1] * lower_y + above[1] * upper_y)
                    + (below[2] * lower_x + above[2] * upper_x)
                )
            quotients = divide(values, row, tile)
            results = []
            for field in range(fields):
                value = keep * centers[field][tile] + quotients[field]
                if level > 1:
                    value = value + iterates[0][field, row, tile, middle, :]
                results.append(value)
            yield tile, results

    for level in range(1, levels):
        for row in range(*rows_of(level)):
            for tile, results in sweep(row, level):
                for field in range(fields):
                    iterates[level][field, row, tile, middle, :] = results[field]

    last_rows = rows_of(levels)
    skipped = [0] * steps
    if second_half:
        whole = [ahead for ahead in range(1, steps) if ahead not in early_moves]
        for ahead, block in zip(whole, finished, strict=True):
            skipped[ahead] = (rows - reach) * tiles
            outs[ahead][pl.ds(0, block.shape[0])] = block[...]

    for row in range(*last_rows):
        for tile, results in sweep(row, levels):
            for ahead in range(steps):
                terms, field = [], 0
                for k, is_complex in freqs:
                    factor = relax_weights[levels] * (2.0 if is_complex else 1.0) / steps
                    terms.append((factor * cosine(k * ahead, steps), results[field]))
                    field += 1
                    if is_complex:
                        terms.append((-factor * sine(k * ahead, steps), results[field]))
                        field += 1
                place = (row - last_rows[0]) * tiles + tile + skipped[ahead]
                outs[ahead][place] = combine(terms)


def unpack_kernel(tm, space, log_alpha, steps, early, *refs):
    refs = list(refs)
    heads = [refs.pop(0) if two else None for two in early]
    tails, (out, held, semaphores) = refs[:steps], refs[steps:]
    me, up = lax.axis_index(tm), upwards(space)
    depth, rows, columns = out.shape
    width = columns // steps
    tiles = width // lanes
    shape = (1, depth, lanes)
    scale = jnp.exp(jnp.full(shape, me.astype(jnp.float32) * -log_alpha, jnp.float32))
    first = rows - reach
    rising = up == 1

    def at_row(behind, row, tile):
        if heads[behind] is None:
            return tails[behind][row * tiles + tile]
        if row < first:
            return heads[behind][row * tiles + tile]
        return tails[behind][(row - first) * tiles + tile]

    copies = []
    for behind in range(steps):
        owner = slot_owner(me, behind, steps)
        for tile in range(tiles):
            column = [
                jnp.where(rising, at_row(behind, y, tile), at_row(behind, rows - 1 - y, tile))
                for y in range(rows)
            ]
            column = pltpu.einshape("yzx->zyx", jnp.stack(column) * scale)
            place = pl.multiple_of((owner * tiles + tile) * lanes, lanes)
            held[:, :, pl.ds(place, lanes)] = column
        part = pl.ds(pl.multiple_of(owner * width, lanes), width)
        copies.append(
            pltpu.make_async_copy(
                held.at[:, :, part], out.at[:, :, part], semaphores.at[behind]
            )
        )
        copies[-1].start()
    for copy in copies:
        copy.wait()


def gather(blocks, steps):
    result = [blocks[0]] + [None] * (steps - 1)
    for d in reversed(range(1, steps)):
        pairs = [(slot_time(t, d, steps), t) for t in range(steps)]
        result[d] = lax.ppermute(blocks[d], "tm", pairs)
    return result


def scatter(blocks, steps):
    result = list(blocks)
    for d in reversed(range(1, steps)):
        if blocks[d] is not None:
            pairs = [(t, slot_time(t, d, steps)) for t in range(steps)]
            result[d] = lax.ppermute(blocks[d], "tm", pairs)
    return result


def swap(value, first):
    names = ("parts", "tm", "space")
    parts, steps, size = (lax.axis_size(name) for name in names)
    pairs = []
    for part in range(parts):
        for step in range(steps):
            beside = (part ^ 1, step) if parts % 2 == 0 else (part, (step + 1) % steps)
            for slab in range(size):
                partner = slab + 1 if (slab - first) % 2 == 0 else slab - 1
                target = (part, step, partner) if 0 <= partner < size else (*beside, slab)
                here, there = (
                    (p * steps + t) * size + c for p, t, c in ((part, step, slab), target)
                )
                pairs.append((here, there))
    return lax.ppermute(value, names, pairs)


def fast_local(rhs, diffusivity, velocity):
    _, depth, rows, columns = rhs.shape
    steps = lax.axis_size("tm")
    tiles = columns // steps // lanes
    sheets = depth // sublanes
    log_alpha = math.log(circ_alpha) / steps
    extended, wide = rows + 2 * reach, tiles + 1
    fields = steps
    blocks = gather(pack(rhs[0], steps), steps)
    piece = reach * tiles * sheets + 1
    made = [(extended, wide, depth, lanes), (fields, extended, wide, depth, lanes)]
    iterates = [(fields, extended, wide, depth + 16, lanes)] * reach
    own, own_far, drift = call(
        functools.partial(kappa_kernel, "tm", "space", steps),
        [
            (rows * tiles * sheets + 1, sublanes, lanes),
            (piece, sublanes, lanes),
            (3, depth, lanes),
        ],
        diffusivity,
        velocity,
        specs={0: hbm, 1: hbm},
        scratch=[
            *staging(diffusivity.shape),
            pltpu.SMEM(velocity.shape, jnp.float32),
            pltpu.SemaphoreType.DMA,
        ],
    )
    kappa_far = swap(own_far, 1)
    kappa, inverse, *margins = call(
        functools.partial(prepare_kernel, "tm", rows, tiles, steps), [*made, *iterates], own
    )
    near, far = halos(blocks, own, kappa, piece)
    far = swap(far, 1)
    near = swap(near, 0)
    state = [*made, *iterates]
    early = rows - reach
    solve = functools.partial(solve_kernel, "tm", "space", rows, tiles, steps)
    kept = [kappa, inverse, *margins]
    held = call(
        functools.partial(solve, False),
        state + [(early * tiles, depth, lanes)] * steps,
        *blocks,
        near,
        drift,
        *kept,
        aliases={steps + 2 + i: i for i in range(len(kept))},
    )
    state_now, finished = held[: len(state)], held[len(state) :]
    in_two = [d == 0 or d in early_moves for d in range(steps)]
    heads = scatter([finished[d] if in_two[d] else None for d in range(steps)], steps)
    heads = [head for head in heads if head is not None]
    held = call(
        functools.partial(solve, True),
        state + [((reach if two else rows) * tiles, depth, lanes) for two in in_two],
        far,
        kappa_far,
        drift,
        *state_now,
        *(finished[d] for d in range(steps) if not in_two[d]),
        aliases={3 + i: i for i in range(len(state))},
    )
    tails = scatter(held[len(state) :], steps)
    (result,) = call(
        functools.partial(unpack_kernel, "tm", "space", log_alpha, steps, tuple(in_two)),
        [(depth, rows, columns)],
        *heads,
        *tails,
        kept=False,
        scratch=[
            pltpu.VMEM((depth, rows, columns), jnp.float32),
            pltpu.SemaphoreType.DMA((steps,)),
        ],
    )
    return result[None]


def padded(shard, sides, width):
    for axis, dim in sides:
        size, length = (lax.axis_size(axis), shard.shape[dim])
        up = [(i, (i + 1) % size) for i in range(size - 1)]
        down = [(j, i) for i, j in up]
        last = lax.slice_in_dim(shard, length - width, length, axis=dim)
        initial = lax.slice_in_dim(shard, 0, width, axis=dim)
        before = lax.ppermute(last, axis, up)
        after = lax.ppermute(initial, axis, down)
        shard = jnp.concatenate([before, shard, after], axis=dim)
    return shard


def stencil(extended, diffusivity, diag_re, diag_im, velocity):
    center = extended[:, :, :, 1:-1, :]
    upper_y = extended[:, :, :, 2:, :]
    lower_y = extended[:, :, :, :-2, :]
    zero_z = jnp.zeros_like(center[:, :, :1])
    upper_z = jnp.concatenate([center[:, :, 1:], zero_z], axis=2)
    lower_z = jnp.concatenate([zero_z, center[:, :, :-1]], axis=2)
    zero_x = jnp.zeros_like(center[:, :, :, :, :1])
    upper_x = jnp.concatenate([center[:, :, :, :, 1:], zero_x], axis=4)
    lower_x = jnp.concatenate([zero_x, center[:, :, :, :, :-1]], axis=4)
    coefficient = diffusivity[None, None]
    half_velocity = 0.5 * velocity
    beside = (coefficient - half_velocity[0]) * upper_z + (coefficient + half_velocity[0]) * lower_z
    beside = (
        beside
        + (coefficient - half_velocity[1]) * upper_y
        + (coefficient + half_velocity[1]) * lower_y
    )
    beside = (
        beside
        + (coefficient - half_velocity[2]) * upper_x
        + (coefficient + half_velocity[2]) * lower_x
    )
    denominator = diag_re + 6.0 * diffusivity
    center_re = center[:, 0]
    center_im = center[:, 1]
    total_re = denominator * center_re - diag_im * center_im
    total_im = denominator * center_im + diag_im * center_re
    return jnp.stack([total_re, total_im], axis=1) - beside


def divide(residual, diffusivity, diag_re, diag_im):
    denominator = diag_re + 6.0 * diffusivity
    modulus = denominator * denominator + diag_im * diag_im
    residual_re = residual[:, 0]
    residual_im = residual[:, 1]
    quotient_re = (residual_re * denominator + residual_im * diag_im) / modulus
    quotient_im = (residual_im * denominator - residual_re * diag_im) / modulus
    return jnp.stack([quotient_re, quotient_im], axis=1)


def highest(left, right):
    return jnp.dot(left, right, precision=lax.Precision.HIGHEST, preferred_element_type=jnp.float32)


def twiddle(row_index, column_index, length):
    product = row_index[:, None] * column_index[None, :] % length
    phase_table = product.astype(jnp.float32) * (2.0 * math.pi / length)
    return (jnp.cos(phase_table), jnp.sin(phase_table))


def general_local(rhs, diffusivity, velocity):
    local_steps, depth, rows_y, rows_x = rhs.shape
    length = local_steps * lax.axis_size("tm")
    first_step = lax.axis_index("tm") * local_steps
    own_index = first_step + jnp.arange(local_steps, dtype=jnp.int32)
    log_alpha = math.log(circ_alpha) / length
    cell_count = depth * rows_y * rows_x
    scaled = (
        rhs.reshape(local_steps, cell_count)
        * jnp.exp(own_index.astype(jnp.float32) * log_alpha)[:, None]
    )
    regrouped = lax.all_to_all(scaled, "tm", split_axis=1, concat_axis=0, tiled=True)
    full_index = jnp.arange(length, dtype=jnp.int32)
    cosine_table, sine_table = twiddle(full_index, full_index, length)
    spectrum_re = highest(cosine_table, regrouped)
    spectrum_im = -highest(sine_table, regrouped)
    source_re, source_im = (
        lax.all_to_all(spectrum_re, "tm", split_axis=0, concat_axis=1, tiled=True),
        lax.all_to_all(spectrum_im, "tm", split_axis=0, concat_axis=1, tiled=True),
    )
    source = jnp.stack([source_re, source_im], axis=1).reshape(
        local_steps, 2, depth, rows_y, rows_x
    )
    phase_angle = own_index.astype(jnp.float32) * (2.0 * math.pi / length)
    shift_factor = circ_alpha ** (1.0 / length)
    diag_re = (1.0 - shift_factor * jnp.cos(phase_angle))[:, None, None, None]
    diag_im = (shift_factor * jnp.sin(phase_angle))[:, None, None, None]
    field = relax_weights[0] * divide(source, diffusivity, diag_re, diag_im)
    for weight in relax_weights[1:]:
        extended = padded(field, (("space", 3),), 1)
        applied = stencil(extended, diffusivity, diag_re, diag_im, velocity)
        field = field + weight * divide(source - applied, diffusivity, diag_re, diag_im)
    field_re = field[:, 0].reshape(local_steps, cell_count)
    field_im = field[:, 1].reshape(local_steps, cell_count)
    mixed_re, mixed_im = (
        lax.all_to_all(field_re, "tm", split_axis=1, concat_axis=0, tiled=True),
        lax.all_to_all(field_im, "tm", split_axis=1, concat_axis=0, tiled=True),
    )
    values = (highest(cosine_table, mixed_re) - highest(sine_table, mixed_im)) / length
    restored = lax.all_to_all(values, "tm", split_axis=0, concat_axis=1, tiled=True)
    result = restored * jnp.exp(-own_index.astype(jnp.float32) * log_alpha)[:, None]
    return result.reshape(local_steps, depth, rows_y, rows_x)


def local(rhs, diffusivity, velocity):
    steps = lax.axis_size("tm")
    local_steps, depth, rows, columns = rhs.shape
    slots = rows * (depth // sublanes)
    tiled = columns % (steps * lanes) == 0 and depth % sublanes == 0
    if local_steps == 1 and rows >= reach and tiled and 2 * reach * slots <= lanes:
        return fast_local(rhs, diffusivity, velocity)
    return general_local(rhs, diffusivity, velocity)


def solution(mesh):
    return jax.shard_map(
        local,
        mesh=mesh,
        in_specs=(P(("parts", "tm"), None, "space", None), P("parts", "space", None), P("parts")),
        out_specs=P(("parts", "tm"), None, "space", None),
        check_vma=False,
    )
```

```python
import functools
import math

import jax
import jax.numpy as jnp
from jax import lax
from jax.experimental import pallas as pl
from jax.experimental.pallas import tpu as pltpu
from jax.sharding import PartitionSpec as P


circ_alpha = 0.1
relax_weights = (
    1.0 / (1.0 - 0.5 * math.cos(math.pi / 8.0)),
    1.0 / (1.0 - 0.5 * math.cos(3.0 * math.pi / 8.0)),
    1.0 / (1.0 - 0.5 * math.cos(5.0 * math.pi / 8.0)),
    1.0 / (1.0 - 0.5 * math.cos(7.0 * math.pi / 8.0)),
)


reach = len(relax_weights) - 1
lanes = 128
sublanes = 8
vmem = pl.BlockSpec(memory_space=pltpu.VMEM)
smem = pl.BlockSpec(memory_space=pltpu.SMEM)
hbm = pl.BlockSpec(memory_space=pltpu.HBM)


def call(kernel, outs, *operands, specs=None, kept=True, aliases=None, scratch=()):
    specs = specs or {}
    on_chip = [
        x
        if specs.get(i) is smem
        else pltpu.with_memory_space_constraint(x, pltpu.HBM if i in specs else pltpu.VMEM)
        for i, x in enumerate(operands)
    ]
    make = pltpu.VMEM if kept else jax.ShapeDtypeStruct
    return pl.pallas_call(
        kernel,
        out_shape=[make(o, jnp.float32) for o in outs],
        in_specs=[specs.get(i, vmem) for i in range(len(operands))],
        out_specs=[vmem if kept else hbm] * len(outs),
        scratch_shapes=scratch,
        input_output_aliases=aliases or {},
        compiler_params=pltpu.CompilerParams(vmem_limit_bytes=16 << 20),
    )(*on_chip)


def column_mask(left, right, shape):
    lane = lax.broadcasted_iota(jnp.int32, shape, 1)
    keep_right = (lane < reach).astype(jnp.float32) * right
    keep_left = (lane >= lanes - reach).astype(jnp.float32) * left
    return keep_right, keep_left


def upwards(space):
    return lax.rem(lax.axis_index(space), 2)


def row_of(y, rows, up):
    return up * y + (1 - up) * (rows - 1 - y)


def heading(step, steps):
    return 1 - 2 * (step % 2) if steps % 2 == 0 else 1


def slot_time(step, slot, steps):
    return (step + heading(step, steps) * slot) % steps


def slot_owner(me, slot, steps):
    forwards = 1 - 2 * lax.rem(me, 2) if steps % 2 == 0 else 1
    turn = forwards * slot if steps % 2 == 0 and slot % 2 else -forwards * slot
    return lax.rem(me + turn + steps, steps)


def finished_place(slot, count):
    return (slot, 0) if slot < 3 else (2, count) if slot == 3 else (slot - 1, 0)


def in_one(slot):
    return slot == 1 or slot > 3


def put(block, index, value):
    sheets = value.shape[0] // sublanes
    block[pl.ds(index * sheets, sheets)] = value.reshape(sheets, sublanes, lanes)


def slot_width(rows, sheets):
    return lanes // (rows * sheets)


def turn(source, target, scale=None):
    _, rows, columns = source.shape
    for tile in range(columns // lanes):
        column = pltpu.einshape("zyx->yzx", source[:, :, tile * lanes : (tile + 1) * lanes])
        target[pl.ds(tile * rows, rows)] = column if scale is None else column * scale


def pick_block(source, rows, out, owner, owners, up):
    count, depth, _ = source.shape
    sheets = depth // sublanes
    width = slot_width(rows, sheets)
    total = count // rows
    tiles = total // owners
    left_tile = jnp.maximum(owner * tiles - 1, 0)
    right_tile = jnp.minimum((owner + 1) * tiles, total - 1)
    left = (owner > 0).astype(jnp.float32)
    right = (owner < owners - 1).astype(jnp.float32)
    keep_right, keep_left = column_mask(left, right, (depth, lanes))
    packed = None
    for y in range(rows):
        row = row_of(y, rows, up)
        for tile in range(tiles):
            put(out, row * tiles + tile, source[(owner * tiles + tile) * rows + y])
        halo = source[right_tile * rows + y] * keep_right + source[left_tile * rows + y] * keep_left
        for sheet in range(sheets):
            part = halo[sheet * sublanes : (sheet + 1) * sublanes]
            part = pltpu.roll(part, (row * sheets + sheet) * width, 1)
            packed = part if packed is None else packed + part
    out[out.shape[0] - 1] = packed


def fetch(source, target, semaphores):
    pieces = semaphores.shape[0]
    size = source.shape[0] // pieces
    copies = [
        pltpu.make_async_copy(
            source.at[pl.ds(i * size, size)], target.at[pl.ds(i * size, size)], semaphores.at[i]
        )
        for i in range(pieces)
    ]
    for copy in copies:
        copy.start()
    for copy in copies:
        copy.wait()


def pack_kernel(tm, space, log_alpha, steps, rhs, *refs):
    outs, (held, semaphores, turned) = refs[:steps], refs[steps:]
    me, up = lax.axis_index(tm), upwards(space)
    fetch(rhs, held, semaphores)
    shape = (1, rhs.shape[0], lanes)
    turn(held, turned, jnp.exp(jnp.full(shape, me.astype(jnp.float32) * log_alpha, jnp.float32)))
    for ahead in reversed(range(steps)):
        pick_block(turned, rhs.shape[1], outs[ahead], slot_owner(me, ahead, steps), steps, up)


def staging(shape):
    depth, rows, columns = shape
    return [
        pltpu.VMEM(shape, jnp.float32),
        pltpu.SemaphoreType.DMA((math.gcd(depth, 4),)),
        pltpu.VMEM((columns // lanes * rows, depth, lanes), jnp.float32),
    ]


def pack(rhs, steps):
    depth, rows, columns = rhs.shape
    tiles = columns // steps // lanes
    log_alpha = math.log(circ_alpha) / steps
    kernel = functools.partial(pack_kernel, "tm", "space", log_alpha, steps)
    out = (rows * tiles * depth // sublanes + 1, sublanes, lanes)
    return call(kernel, [out] * steps, rhs, specs={0: hbm}, scratch=staging(rhs.shape))


def copy_piece(block, is_near, piece, target, first):
    last = block.shape[0] - 1
    start = 0 if is_near else last - (piece - 1)
    target[pl.ds(first, piece - 1)] = block[pl.ds(start, piece - 1)]
    target[first + piece - 1] = block[last]


def halo_kernel(piece, *refs):
    blocks, (near, far) = refs[:-3], refs[-2:]
    for step, block in enumerate(blocks):
        copy_piece(block, True, piece, near, step * piece)
        if 0 < step < len(blocks) - 1:
            copy_piece(block, False, piece, far, (step - 1) * piece)


def halos(blocks, own, ready, piece):
    outs = [(count * piece, sublanes, lanes) for count in (len(blocks) + 1, len(blocks) - 1)]
    return call(functools.partial(halo_kernel, piece), outs, *blocks, own, ready)


def row_piece(own, near, far, step, row, tile, rows, tiles, depth):
    sheets = depth // sublanes
    piece = reach * tiles * sheets + 1
    base, start, held = step * piece, 0, reach
    if row < reach:
        source, there = near, reach - 1 - row
    elif row < reach + rows:
        source, base, there, held = own, 0, row - reach, rows
    else:
        source, there, start = far, 2 * rows + reach - 1 - row, rows - reach
    if tile < tiles:
        first = base + ((there - start) * tiles + tile) * sheets
        return source[pl.ds(first, sheets)].reshape(depth, lanes)
    value = source[base + held * tiles * sheets]
    width = slot_width(rows, sheets)
    parts = []
    for sheet in range(sheets):
        shift = (there * sheets + sheet) * width
        parts.append(pltpu.roll(value, lanes - shift, 1) if shift else value)
    return jnp.concatenate(parts)


def frequencies(steps):
    return [(k, 2 * k % steps != 0) for k in range(steps // 2 + 1)]


def write_coefficients(tm, row, tile, value, mask, steps, kappa, inverse):
    backwards = lax.rem(lax.axis_index(tm), 2) if steps % 2 == 0 else 0
    turn = jnp.float32(1 - 2 * backwards)
    shift_factor = circ_alpha ** (1.0 / steps)
    kappa[row, tile] = value
    place = 0
    for k, is_complex in frequencies(steps):
        phase = 2.0 * math.pi * k / steps
        real = (1.0 - shift_factor * math.cos(phase)) + 6.0 * value
        if is_complex:
            imag = shift_factor * math.sin(phase)
            reciprocal = 1.0 / (real * real + imag * imag)
            pair = (real * reciprocal, (imag * turn) * reciprocal)
        else:
            pair = (1.0 / real,)
        for part in pair:
            inverse[place, row, tile] = part if mask is None else part * mask
            place += 1


def side_mask(tm, steps, depth):
    me = lax.axis_index(tm)
    keep_right, keep_left = column_mask(
        (me > 0).astype(jnp.float32), (me < steps - 1).astype(jnp.float32), (depth, lanes)
    )
    return keep_right + keep_left


def kappa_kernel(tm, space, steps, diffusivity, velocity, block, *refs):
    own, own_far, drift, held, semaphores, turned, speeds, semaphore = refs
    up = upwards(space)
    copy = pltpu.make_async_copy(velocity, speeds, semaphore)
    copy.start()
    fetch(diffusivity, held, semaphores)

    turn(held, turned)
    pick_block(turned, diffusivity.shape[1], own, lax.axis_index(tm), steps, up)
    piece = own_far.shape[0] // 2
    copy_piece(own, False, piece, own_far, 0)
    copy_piece(block, False, piece, own_far, piece)
    copy.wait()
    direction = (2 * up - 1).astype(jnp.float32)
    for j in range(3):
        speed = 0.5 * speeds[j]
        drift[j] = jnp.full(drift.shape[1:], speed * direction if j == 1 else speed, jnp.float32)


def prepare_kernel(tm, rows, tiles, steps, own, kappa, inverse, *iterates):
    depth = kappa.shape[2]
    zero = jnp.zeros((8, lanes), jnp.float32)
    for level, ref in enumerate(iterates):
        fields, extended, wide = ref.shape[:3]
        for field in range(fields):
            for row in range(level, extended - level):
                for tile in range(wide):
                    ref[field, row, tile, pl.ds(0, 8), :] = zero
                    ref[field, row, tile, pl.ds(8 + depth, 8), :] = zero
    halo_mask = side_mask(tm, steps, depth)
    for row in range(reach, reach + rows):
        for tile in range(tiles + 1):
            value = row_piece(own, None, None, 0, row, tile, rows, tiles, depth)
            mask = halo_mask if tile == tiles else None
            write_coefficients(tm, row, tile, value, mask, steps, kappa, inverse)


def combine(terms):
    total = None
    for factor, value in terms:
        if factor == 0.0:
            continue
        if total is None:
            total = value if factor == 1.0 else factor * value
        elif factor == 1.0:
            total = total + value
        elif factor == -1.0:
            total = total - value
        else:
            total = total + factor * value
    return total


def exact(value):
    return float(round(value)) if abs(value - round(value)) < 1e-12 else value


def cosine(product, steps):
    return exact(math.cos(2.0 * math.pi * (product % steps) / steps))


def sine(product, steps):
    return exact(math.sin(2.0 * math.pi * (product % steps) / steps))


def solve_kernel(tm, space, rows, tiles, steps, second_half, *refs):
    freqs = frequencies(steps)
    fields = sum(2 if c else 1 for _, c in freqs)
    levels = reach
    made = 2 + levels
    if second_half:
        far, kappa_far, drift = refs[:3]
        done = sum(in_one(ahead) for ahead in range(steps))
        finished, refs = refs[3 + made : 3 + made + done], refs[3 + made + done :]
        kappa, inverse, *iterates = refs[:made]
        outs = refs[made:]
        blocks, near = [None] * steps, None
    else:
        blocks, (near, drift) = refs[:steps], refs[steps : steps + 2]
        kappa, inverse, *iterates = refs[steps + 2 + made :][:made]
        outs = refs[steps + 2 + made + made :]
        far, kappa_far = None, None
    depth = kappa.shape[2]
    pad = 8
    middle = pl.ds(pad, depth)
    lane = lax.broadcasted_iota(jnp.int32, (depth, lanes), 1)
    at_first, at_last = lane == 0, lane == lanes - 1
    half = [drift[j] for j in range(3)]
    known = reach + rows
    extended = known + reach
    wide = tiles + 1

    def rows_of(level):
        split = known - level
        return (split, extended - level) if second_half else (level, split)

    slab, slabs, up = lax.axis_index(space), lax.axis_size(space), upwards(space)
    beyond = slab < slabs - 1 if second_half else slab > 0
    before = slab > 0 if second_half else slab < slabs - 1
    inside = jnp.where(up == 1, beyond, before).astype(jnp.float32)
    halo_mask = side_mask(tm, steps, depth) * inside
    row_mask = jnp.full((depth, lanes), inside, jnp.float32)
    for row in range(known, extended) if second_half else range(reach):
        for tile in range(wide):
            step = 0 if second_half else steps
            value = row_piece(None, near, kappa_far, step, row, tile, rows, tiles, depth)
            mask = halo_mask if tile == tiles else row_mask
            write_coefficients(tm, row, tile, value, mask, steps, kappa, inverse)

    def divide(values, row, tile):
        result, place = [], 0
        for _, is_complex in freqs:
            if is_complex:
                re, im = values[place], values[place + 1]
                p, q = inverse[place, row, tile], inverse[place + 1, row, tile]
                result += [re * p + im * q, im * p - re * q]
                place += 2
            else:
                result.append(values[place] * inverse[place, row, tile])
                place += 1
        return result

    for row in range(*rows_of(0)):
        for tile in range(wide):
            if tile == tiles and not 1 <= row < extended - 1:
                continue
            held = [
                row_piece(
                    blocks[b],
                    near,
                    far if b else kappa_far,
                    (b - 1 if b else 1) if second_half else b,
                    row,
                    tile,
                    rows,
                    tiles,
                    depth,
                )
                for b in range(steps)
            ]
            values = []
            for k, is_complex in freqs:
                values.append(combine((cosine(k * b, steps), held[b]) for b in range(steps)))
                if is_complex:
                    values.append(combine((-sine(k * b, steps), held[b]) for b in range(steps)))
            quotients = divide(values, row, tile)
            for field in range(fields):
                iterates[0][field, row, tile, middle, :] = quotients[field]


    def sweep(row, level):
        with_halo = level < row < extended - 1 - level and level < levels
        old = iterates[level - 1]
        scale, weight = relax_weights[level - 1], relax_weights[level]
        keep = (1.0 - weight) * scale / weight + (1.0 if level == 1 else 0.0)
        tilt = [scale * h for h in half]
        centers = [
            [old[field, row, tile, middle, :] for tile in range(wide)] for field in range(fields)
        ]
        shifted_down = [[pltpu.roll(c, 1, 1) for c in line] for line in centers]
        shifted_up = [[pltpu.roll(c, lanes - 1, 1) for c in line] for line in centers]
        for tile in range(wide if with_halo else tiles):
            values = []
            scaled = scale * kappa[row, tile]
            below = [scaled + t for t in tilt]
            above = [scaled - t for t in tilt]
            for field in range(fields):
                lower_x = jnp.where(
                    at_first, shifted_down[field][(tile - 1) % wide], shifted_down[field][tile]
                )
                upper_x = jnp.where(
                    at_last, shifted_up[field][(tile + 1) % wide], shifted_up[field][tile]
                )
                lower_z = old[field, row, tile, pl.ds(pad - 1, depth), :]
                upper_z = old[field, row, tile, pl.ds(pad + 1, depth), :]
                lower_y = old[field, row - 1, tile, middle, :]
                upper_y = old[field, row + 1, tile, middle, :]
                values.append(
                    (below[0] * lower_z + above[0] * upper_z)
                    + (below[1] * lower_y + above[1] * upper_y)
                    + (below[2] * lower_x + above[2] * upper_x)
                )
            quotients = divide(values, row, tile)
            results = []
            for field in range(fields):
                value = keep * centers[field][tile] + quotients[field]
                if level > 1:
                    value = value + iterates[0][field, row, tile, middle, :]
                results.append(value)
            yield tile, results

    for level in range(1, levels):
        for row in range(*rows_of(level)):
            for tile, results in sweep(row, level):
                for field in range(fields):
                    iterates[level][field, row, tile, middle, :] = results[field]

    last_rows = rows_of(levels)
    early = (rows - reach) * tiles
    places = [(ahead, 0) for ahead in range(steps)]
    if second_half:
        whole = [ahead for ahead in range(steps) if in_one(ahead)]
        for ahead, block in zip(whole, finished, strict=True):
            places[ahead] = (ahead, early)
            outs[ahead][pl.ds(0, early)] = block[...]
    else:
        places = [finished_place(ahead, early) for ahead in range(steps)]

    for row in range(*last_rows):
        for tile, results in sweep(row, levels):
            for ahead in range(steps):
                terms, field = [], 0
                for k, is_complex in freqs:
                    factor = relax_weights[levels] * (2.0 if is_complex else 1.0) / steps
                    terms.append((factor * cosine(k * ahead, steps), results[field]))
                    field += 1
                    if is_complex:
                        terms.append((-factor * sine(k * ahead, steps), results[field]))
                        field += 1
                which, start = places[ahead]
                outs[which][start + (row - last_rows[0]) * tiles + tile] = combine(terms)


def join_kernel(block, early, joined):
    count = block.shape[0]
    joined[pl.ds(0, count)] = block[...]
    handed = joined.shape[0] - count
    joined[pl.ds(count, handed)] = early[pl.ds(handed, handed)]


def unpack_kernel(tm, space, log_alpha, steps, own_early, early, *refs):
    tails, (out, held, semaphores) = refs[:steps], refs[steps:]
    me, up = lax.axis_index(tm), upwards(space)
    depth, rows, columns = out.shape
    width = columns // steps
    tiles = width // lanes
    shape = (1, depth, lanes)
    scale = jnp.exp(jnp.full(shape, me.astype(jnp.float32) * -log_alpha, jnp.float32))
    first = rows - reach
    rising = up == 1

    def at_row(behind, row, tile):
        if in_one(behind):
            return tails[behind][row * tiles + tile]
        if row >= first:
            return tails[behind][(row - first) * tiles + tile]
        if behind == 3:
            return tails[1][(rows + row) * tiles + tile]
        return (early if behind else own_early)[row * tiles + tile]

    copies = []
    for behind in range(steps):
        owner = slot_owner(me, behind, steps)
        for tile in range(tiles):
            column = [
                jnp.where(rising, at_row(behind, y, tile), at_row(behind, rows - 1 - y, tile))
                for y in range(rows)
            ]
            column = pltpu.einshape("yzx->zyx", jnp.stack(column) * scale)
            place = pl.multiple_of((owner * tiles + tile) * lanes, lanes)
            held[:, :, pl.ds(place, lanes)] = column
        part = pl.ds(pl.multiple_of(owner * width, lanes), width)
        copies.append(
            pltpu.make_async_copy(
                held.at[:, :, part], out.at[:, :, part], semaphores.at[behind]
            )
        )
        copies[-1].start()
    for copy in copies:
        copy.wait()


def gather(blocks, steps):
    result = [blocks[0]] + [None] * (steps - 1)
    for d in reversed(range(1, steps)):
        pairs = [(slot_time(t, d, steps), t) for t in range(steps)]
        result[d] = lax.ppermute(blocks[d], "tm", pairs)
    return result


def scatter(block, d, steps):
    return lax.ppermute(block, "tm", [(t, slot_time(t, d, steps)) for t in range(steps)])


def swap(value, first):
    names = ("parts", "tm", "space")
    parts, steps, size = (lax.axis_size(name) for name in names)
    pairs = []
    for part in range(parts):
        for step in range(steps):
            beside = (part ^ 1, step) if parts % 2 == 0 else (part, (step + 1) % steps)
            for slab in range(size):
                partner = slab + 1 if (slab - first) % 2 == 0 else slab - 1
                target = (part, step, partner) if 0 <= partner < size else (*beside, slab)
                here, there = (
                    (p * steps + t) * size + c for p, t, c in ((part, step, slab), target)
                )
                pairs.append((here, there))
    return lax.ppermute(value, names, pairs)


def fast_local(rhs, diffusivity, velocity):
    _, depth, rows, columns = rhs.shape
    steps = lax.axis_size("tm")
    tiles = columns // steps // lanes
    sheets = depth // sublanes
    log_alpha = math.log(circ_alpha) / steps
    extended, wide = rows + 2 * reach, tiles + 1
    fields = steps
    blocks = gather(pack(rhs[0], steps), steps)
    piece = reach * tiles * sheets + 1
    made = [(extended, wide, depth, lanes), (fields, extended, wide, depth, lanes)]
    iterates = [(fields, extended, wide, depth + 16, lanes)] * reach
    own, own_far, drift = call(
        functools.partial(kappa_kernel, "tm", "space", steps),
        [
            (rows * tiles * sheets + 1, sublanes, lanes),
            (2 * piece, sublanes, lanes),
            (3, depth, lanes),
        ],
        diffusivity,
        velocity,
        blocks[0],
        specs={0: hbm, 1: hbm},
        scratch=[
            *staging(diffusivity.shape),
            pltpu.SMEM(velocity.shape, jnp.float32),
            pltpu.SemaphoreType.DMA,
        ],
    )
    kappa_far = swap(own_far, 1)
    kappa, inverse, *margins = call(
        functools.partial(prepare_kernel, "tm", rows, tiles, steps), [*made, *iterates], own
    )
    near, far = halos(blocks, own, kappa, piece)
    far = swap(far, 1)
    near = swap(near, 0)
    state = [*made, *iterates]
    early = (rows - reach) * tiles
    solve = functools.partial(solve_kernel, "tm", "space", rows, tiles, steps)
    kept = [kappa, inverse, *margins]
    counts = [early, early, 2 * early] + [early] * (steps - 4)
    held = call(
        functools.partial(solve, False),
        state + [(n, depth, lanes) for n in counts],
        *blocks,
        near,
        drift,
        *kept,
        aliases={steps + 2 + i: i for i in range(len(kept))},
    )
    state_now, finished = held[: len(state)], held[len(state) :]
    moved = scatter(finished[2], 2, steps)
    held = call(
        functools.partial(solve, True),
        state
        + [((rows if in_one(d) else reach) * tiles, depth, lanes) for d in range(steps)],
        far,
        kappa_far,
        drift,
        *state_now,
        *(finished[finished_place(d, early)[0]] for d in range(steps) if in_one(d)),
        aliases={3 + i: i for i in range(len(state))},
    )
    tails = list(held[len(state) :])
    (tails[1],) = call(join_kernel, [(rows * tiles + early, depth, lanes)], tails[1], moved)
    for d in reversed(range(1, steps)):
        tails[d] = scatter(tails[d], d, steps)
    (result,) = call(
        functools.partial(unpack_kernel, "tm", "space", log_alpha, steps),
        [(depth, rows, columns)],
        finished[0],
        moved,
        *tails,
        kept=False,
        scratch=[
            pltpu.VMEM((depth, rows, columns), jnp.float32),
            pltpu.SemaphoreType.DMA((steps,)),
        ],
    )
    return result[None]


def padded(shard, sides, width):
    for axis, dim in sides:
        size, length = (lax.axis_size(axis), shard.shape[dim])
        up = [(i, (i + 1) % size) for i in range(size - 1)]
        down = [(j, i) for i, j in up]
        last = lax.slice_in_dim(shard, length - width, length, axis=dim)
        initial = lax.slice_in_dim(shard, 0, width, axis=dim)
        before = lax.ppermute(last, axis, up)
        after = lax.ppermute(initial, axis, down)
        shard = jnp.concatenate([before, shard, after], axis=dim)
    return shard


def stencil(extended, diffusivity, diag_re, diag_im, velocity):
    center = extended[:, :, :, 1:-1, :]
    upper_y = extended[:, :, :, 2:, :]
    lower_y = extended[:, :, :, :-2, :]
    zero_z = jnp.zeros_like(center[:, :, :1])
    upper_z = jnp.concatenate([center[:, :, 1:], zero_z], axis=2)
    lower_z = jnp.concatenate([zero_z, center[:, :, :-1]], axis=2)
    zero_x = jnp.zeros_like(center[:, :, :, :, :1])
    upper_x = jnp.concatenate([center[:, :, :, :, 1:], zero_x], axis=4)
    lower_x = jnp.concatenate([zero_x, center[:, :, :, :, :-1]], axis=4)
    coefficient = diffusivity[None, None]
    half_velocity = 0.5 * velocity
    beside = (coefficient - half_velocity[0]) * upper_z + (coefficient + half_velocity[0]) * lower_z
    beside = (
        beside
        + (coefficient - half_velocity[1]) * upper_y
        + (coefficient + half_velocity[1]) * lower_y
    )
    beside = (
        beside
        + (coefficient - half_velocity[2]) * upper_x
        + (coefficient + half_velocity[2]) * lower_x
    )
    denominator = diag_re + 6.0 * diffusivity
    center_re = center[:, 0]
    center_im = center[:, 1]
    total_re = denominator * center_re - diag_im * center_im
    total_im = denominator * center_im + diag_im * center_re
    return jnp.stack([total_re, total_im], axis=1) - beside


def divide(residual, diffusivity, diag_re, diag_im):
    denominator = diag_re + 6.0 * diffusivity
    modulus = denominator * denominator + diag_im * diag_im
    residual_re = residual[:, 0]
    residual_im = residual[:, 1]
    quotient_re = (residual_re * denominator + residual_im * diag_im) / modulus
    quotient_im = (residual_im * denominator - residual_re * diag_im) / modulus
    return jnp.stack([quotient_re, quotient_im], axis=1)


def highest(left, right):
    return jnp.dot(left, right, precision=lax.Precision.HIGHEST, preferred_element_type=jnp.float32)


def twiddle(row_index, column_index, length):
    product = row_index[:, None] * column_index[None, :] % length
    phase_table = product.astype(jnp.float32) * (2.0 * math.pi / length)
    return (jnp.cos(phase_table), jnp.sin(phase_table))


def general_local(rhs, diffusivity, velocity):
    local_steps, depth, rows_y, rows_x = rhs.shape
    length = local_steps * lax.axis_size("tm")
    first_step = lax.axis_index("tm") * local_steps
    own_index = first_step + jnp.arange(local_steps, dtype=jnp.int32)
    log_alpha = math.log(circ_alpha) / length
    cell_count = depth * rows_y * rows_x
    scaled = (
        rhs.reshape(local_steps, cell_count)
        * jnp.exp(own_index.astype(jnp.float32) * log_alpha)[:, None]
    )
    regrouped = lax.all_to_all(scaled, "tm", split_axis=1, concat_axis=0, tiled=True)
    full_index = jnp.arange(length, dtype=jnp.int32)
    cosine_table, sine_table = twiddle(full_index, full_index, length)
    spectrum_re = highest(cosine_table, regrouped)
    spectrum_im = -highest(sine_table, regrouped)
    source_re, source_im = (
        lax.all_to_all(spectrum_re, "tm", split_axis=0, concat_axis=1, tiled=True),
        lax.all_to_all(spectrum_im, "tm", split_axis=0, concat_axis=1, tiled=True),
    )
    source = jnp.stack([source_re, source_im], axis=1).reshape(
        local_steps, 2, depth, rows_y, rows_x
    )
    phase_angle = own_index.astype(jnp.float32) * (2.0 * math.pi / length)
    shift_factor = circ_alpha ** (1.0 / length)
    diag_re = (1.0 - shift_factor * jnp.cos(phase_angle))[:, None, None, None]
    diag_im = (shift_factor * jnp.sin(phase_angle))[:, None, None, None]
    field = relax_weights[0] * divide(source, diffusivity, diag_re, diag_im)
    for weight in relax_weights[1:]:
        extended = padded(field, (("space", 3),), 1)
        applied = stencil(extended, diffusivity, diag_re, diag_im, velocity)
        field = field + weight * divide(source - applied, diffusivity, diag_re, diag_im)
    field_re = field[:, 0].reshape(local_steps, cell_count)
    field_im = field[:, 1].reshape(local_steps, cell_count)
    mixed_re, mixed_im = (
        lax.all_to_all(field_re, "tm", split_axis=1, concat_axis=0, tiled=True),
        lax.all_to_all(field_im, "tm", split_axis=1, concat_axis=0, tiled=True),
    )
    values = (highest(cosine_table, mixed_re) - highest(sine_table, mixed_im)) / length
    restored = lax.all_to_all(values, "tm", split_axis=0, concat_axis=1, tiled=True)
    result = restored * jnp.exp(-own_index.astype(jnp.float32) * log_alpha)[:, None]
    return result.reshape(local_steps, depth, rows_y, rows_x)


def local(rhs, diffusivity, velocity):
    steps = lax.axis_size("tm")
    local_steps, depth, rows, columns = rhs.shape
    slots = rows * (depth // sublanes)
    tiled = columns % (steps * lanes) == 0 and depth % sublanes == 0
    paired = steps % 2 == 0 and steps >= 4
    if local_steps == 1 and rows > reach and tiled and paired and 2 * reach * slots <= lanes:
        return fast_local(rhs, diffusivity, velocity)
    return general_local(rhs, diffusivity, velocity)


def solution(mesh):
    return jax.shard_map(
        local,
        mesh=mesh,
        in_specs=(P(("parts", "tm"), None, "space", None), P("parts", "space", None), P("parts")),
        out_specs=P(("parts", "tm"), None, "space", None),
        check_vma=False,
    )
```

```python
import functools
import math

import jax
import jax.numpy as jnp
from jax import lax
from jax.experimental import pallas as pl
from jax.experimental.pallas import tpu as pltpu
from jax.sharding import PartitionSpec as P


circ_alpha = 0.1
relax_weights = (
    1.0 / (1.0 - 0.5 * math.cos(math.pi / 8.0)),
    1.0 / (1.0 - 0.5 * math.cos(3.0 * math.pi / 8.0)),
    1.0 / (1.0 - 0.5 * math.cos(5.0 * math.pi / 8.0)),
    1.0 / (1.0 - 0.5 * math.cos(7.0 * math.pi / 8.0)),
)


reach = len(relax_weights) - 1
lanes = 128
sublanes = 8
vmem = pl.BlockSpec(memory_space=pltpu.VMEM)
smem = pl.BlockSpec(memory_space=pltpu.SMEM)
hbm = pl.BlockSpec(memory_space=pltpu.HBM)


def call(kernel, outs, *operands, specs=None, kept=True, aliases=None, scratch=()):
    specs = specs or {}
    on_chip = [
        x
        if specs.get(i) is smem
        else pltpu.with_memory_space_constraint(x, pltpu.HBM if i in specs else pltpu.VMEM)
        for i, x in enumerate(operands)
    ]
    make = pltpu.VMEM if kept else jax.ShapeDtypeStruct
    return pl.pallas_call(
        kernel,
        out_shape=[make(o, jnp.float32) for o in outs],
        in_specs=[specs.get(i, vmem) for i in range(len(operands))],
        out_specs=[vmem if kept else hbm] * len(outs),
        scratch_shapes=scratch,
        input_output_aliases=aliases or {},
        compiler_params=pltpu.CompilerParams(vmem_limit_bytes=16 << 20),
    )(*on_chip)


def column_mask(left, right, shape):
    lane = lax.broadcasted_iota(jnp.int32, shape, 1)
    keep_right = (lane < reach).astype(jnp.float32) * right
    keep_left = (lane >= lanes - reach).astype(jnp.float32) * left
    return keep_right, keep_left


def upwards(space):
    return lax.rem(lax.axis_index(space), 2)


def row_of(y, rows, up):
    return up * y + (1 - up) * (rows - 1 - y)


def heading(step, steps):
    return 1 - 2 * (step % 2) if steps % 2 == 0 else 1


def slot_time(step, slot, steps):
    return (step + heading(step, steps) * slot) % steps


def slot_owner(me, slot, steps):
    forwards = 1 - 2 * lax.rem(me, 2) if steps % 2 == 0 else 1
    turn = forwards * slot if steps % 2 == 0 and slot % 2 else -forwards * slot
    return lax.rem(me + turn + steps, steps)


def finished_place(slot, count):
    return (slot, 0) if slot < 3 else (2, count) if slot == 3 else (slot - 1, 0)


def in_one(slot):
    return slot == 1 or slot > 3


def put(block, index, value):
    sheets = value.shape[0] // sublanes
    block[pl.ds(index * sheets, sheets)] = value.reshape(sheets, sublanes, lanes)


def slot_width(rows, sheets):
    return lanes // (rows * sheets)


def turn(source, target, scale=None):
    _, rows, columns = source.shape
    for tile in range(columns // lanes):
        column = pltpu.einshape("zyx->yzx", source[:, :, tile * lanes : (tile + 1) * lanes])
        target[pl.ds(tile * rows, rows)] = column if scale is None else column * scale


def pick_block(source, rows, out, owner, owners, up):
    count, depth, _ = source.shape
    sheets = depth // sublanes
    width = slot_width(rows, sheets)
    total = count // rows
    tiles = total // owners
    left_tile = jnp.maximum(owner * tiles - 1, 0)
    right_tile = jnp.minimum((owner + 1) * tiles, total - 1)
    left = (owner > 0).astype(jnp.float32)
    right = (owner < owners - 1).astype(jnp.float32)
    keep_right, keep_left = column_mask(left, right, (depth, lanes))
    packed = None
    for y in range(rows):
        row = row_of(y, rows, up)
        for tile in range(tiles):
            put(out, row * tiles + tile, source[(owner * tiles + tile) * rows + y])
        halo = source[right_tile * rows + y] * keep_right + source[left_tile * rows + y] * keep_left
        for sheet in range(sheets):
            part = halo[sheet * sublanes : (sheet + 1) * sublanes]
            part = pltpu.roll(part, (row * sheets + sheet) * width, 1)
            packed = part if packed is None else packed + part
    out[out.shape[0] - 1] = packed


def fetch(source, target, semaphores):
    pieces = semaphores.shape[0]
    size = source.shape[0] // pieces
    copies = [
        pltpu.make_async_copy(
            source.at[pl.ds(i * size, size)], target.at[pl.ds(i * size, size)], semaphores.at[i]
        )
        for i in range(pieces)
    ]
    for copy in copies:
        copy.start()
    for copy in copies:
        copy.wait()


def pack_kernel(tm, space, log_alpha, steps, rhs, *refs):
    outs, (held, semaphores, turned) = refs[:steps], refs[steps:]
    me, up = lax.axis_index(tm), upwards(space)
    fetch(rhs, held, semaphores)
    shape = (1, rhs.shape[0], lanes)
    turn(held, turned, jnp.exp(jnp.full(shape, me.astype(jnp.float32) * log_alpha, jnp.float32)))
    for ahead in reversed(range(steps)):
        pick_block(turned, rhs.shape[1], outs[ahead], slot_owner(me, ahead, steps), steps, up)


def staging(shape):
    depth, rows, columns = shape
    return [
        pltpu.VMEM(shape, jnp.float32),
        pltpu.SemaphoreType.DMA((math.gcd(depth, 4),)),
        pltpu.VMEM((columns // lanes * rows, depth, lanes), jnp.float32),
    ]


def pack(rhs, steps):
    depth, rows, columns = rhs.shape
    tiles = columns // steps // lanes
    log_alpha = math.log(circ_alpha) / steps
    kernel = functools.partial(pack_kernel, "tm", "space", log_alpha, steps)
    out = (rows * tiles * depth // sublanes + 1, sublanes, lanes)
    return call(kernel, [out] * steps, rhs, specs={0: hbm}, scratch=staging(rhs.shape))


def copy_piece(block, is_near, piece, target, first):
    last = block.shape[0] - 1
    start = 0 if is_near else last - (piece - 1)
    target[pl.ds(first, piece - 1)] = block[pl.ds(start, piece - 1)]
    target[first + piece - 1] = block[last]


def halo_kernel(piece, *refs):
    blocks, (near, far) = refs[:-3], refs[-2:]
    for step, block in enumerate(blocks):
        copy_piece(block, True, piece, near, step * piece)
        if 0 < step < len(blocks) - 1:
            copy_piece(block, False, piece, far, (step - 1) * piece)


def halos(blocks, own, ready, piece):
    outs = [(count * piece, sublanes, lanes) for count in (len(blocks) + 1, len(blocks) - 1)]
    return call(functools.partial(halo_kernel, piece), outs, *blocks, own, ready)


def row_piece(own, near, far, step, row, tile, rows, tiles, depth):
    sheets = depth // sublanes
    piece = reach * tiles * sheets + 1
    base, start, held = step * piece, 0, reach
    if row < reach:
        source, there = near, reach - 1 - row
    elif row < reach + rows:
        source, base, there, held = own, 0, row - reach, rows
    else:
        source, there, start = far, 2 * rows + reach - 1 - row, rows - reach
    if tile < tiles:
        first = base + ((there - start) * tiles + tile) * sheets
        return source[pl.ds(first, sheets)].reshape(depth, lanes)
    value = source[base + held * tiles * sheets]
    width = slot_width(rows, sheets)
    parts = []
    for sheet in range(sheets):
        shift = (there * sheets + sheet) * width
        parts.append(pltpu.roll(value, lanes - shift, 1) if shift else value)
    return jnp.concatenate(parts)


def frequencies(steps):
    return [(k, 2 * k % steps != 0) for k in range(steps // 2 + 1)]


def write_coefficients(tm, row, tile, value, mask, steps, kappa, inverse):
    backwards = lax.rem(lax.axis_index(tm), 2) if steps % 2 == 0 else 0
    turn = jnp.float32(1 - 2 * backwards)
    shift_factor = circ_alpha ** (1.0 / steps)
    kappa[row, tile] = value
    place = 0
    for k, is_complex in frequencies(steps):
        phase = 2.0 * math.pi * k / steps
        real = (1.0 - shift_factor * math.cos(phase)) + 6.0 * value
        if is_complex:
            imag = shift_factor * math.sin(phase)
            reciprocal = 1.0 / (real * real + imag * imag)
            pair = (real * reciprocal, (imag * turn) * reciprocal)
        else:
            pair = (1.0 / real,)
        for part in pair:
            inverse[place, row, tile] = part if mask is None else part * mask
            place += 1


def side_mask(tm, steps, depth):
    me = lax.axis_index(tm)
    keep_right, keep_left = column_mask(
        (me > 0).astype(jnp.float32), (me < steps - 1).astype(jnp.float32), (depth, lanes)
    )
    return keep_right + keep_left


def kappa_kernel(tm, space, steps, diffusivity, velocity, block, *refs):
    own, own_far, drift, held, semaphores, turned, speeds, semaphore = refs
    up = upwards(space)
    copy = pltpu.make_async_copy(velocity, speeds, semaphore)
    copy.start()
    fetch(diffusivity, held, semaphores)

    turn(held, turned)
    pick_block(turned, diffusivity.shape[1], own, lax.axis_index(tm), steps, up)
    piece = own_far.shape[0] // 2
    copy_piece(own, False, piece, own_far, 0)
    copy_piece(block, False, piece, own_far, piece)
    copy.wait()
    direction = (2 * up - 1).astype(jnp.float32)
    for j in range(3):
        speed = 0.5 * speeds[j]
        drift[j] = jnp.full(drift.shape[1:], speed * direction if j == 1 else speed, jnp.float32)


def prepare_kernel(tm, rows, tiles, steps, own, kappa, inverse, *iterates):
    depth = kappa.shape[2]
    zero = jnp.zeros((8, lanes), jnp.float32)
    for level, ref in enumerate(iterates):
        fields, extended, wide = ref.shape[:3]
        for field in range(fields):
            for row in range(level, extended - level):
                for tile in range(wide):
                    ref[field, row, tile, pl.ds(0, 8), :] = zero
                    ref[field, row, tile, pl.ds(8 + depth, 8), :] = zero
    halo_mask = side_mask(tm, steps, depth)
    for row in range(reach, reach + rows):
        for tile in range(tiles + 1):
            value = row_piece(own, None, None, 0, row, tile, rows, tiles, depth)
            mask = halo_mask if tile == tiles else None
            write_coefficients(tm, row, tile, value, mask, steps, kappa, inverse)


def combine(terms):
    total = None
    for factor, value in terms:
        if factor == 0.0:
            continue
        if total is None:
            total = value if factor == 1.0 else factor * value
        elif factor == 1.0:
            total = total + value
        elif factor == -1.0:
            total = total - value
        else:
            total = total + factor * value
    return total


def exact(value):
    return float(round(value)) if abs(value - round(value)) < 1e-12 else value


def cosine(product, steps):
    return exact(math.cos(2.0 * math.pi * (product % steps) / steps))


def sine(product, steps):
    return exact(math.sin(2.0 * math.pi * (product % steps) / steps))


def solve_kernel(tm, space, rows, tiles, steps, second_half, *refs):
    freqs = frequencies(steps)
    fields = sum(2 if c else 1 for _, c in freqs)
    levels = reach
    made = 2 + levels
    if second_half:
        far, kappa_far, drift = refs[:3]
        done = sum(in_one(ahead) for ahead in range(steps))
        finished, refs = refs[3 + made : 3 + made + done], refs[3 + made + done :]
        kappa, inverse, *iterates = refs[:made]
        outs = refs[made:]
        blocks, near = [None] * steps, None
    else:
        blocks, (near, drift) = refs[:steps], refs[steps : steps + 2]
        kappa, inverse, *iterates = refs[steps + 2 + made :][:made]
        outs = refs[steps + 2 + made + made :]
        far, kappa_far = None, None
    depth = kappa.shape[2]
    pad = 8
    middle = pl.ds(pad, depth)
    lane = lax.broadcasted_iota(jnp.int32, (depth, lanes), 1)
    at_first, at_last = lane == 0, lane == lanes - 1
    half = [drift[j] for j in range(3)]
    known = reach + rows
    extended = known + reach
    wide = tiles + 1

    def rows_of(level):
        split = known - level
        return (split, extended - level) if second_half else (level, split)

    slab, slabs, up = lax.axis_index(space), lax.axis_size(space), upwards(space)
    beyond = slab < slabs - 1 if second_half else slab > 0
    before = slab > 0 if second_half else slab < slabs - 1
    inside = jnp.where(up == 1, beyond, before).astype(jnp.float32)
    halo_mask = side_mask(tm, steps, depth) * inside
    row_mask = jnp.full((depth, lanes), inside, jnp.float32)
    for row in range(known, extended) if second_half else range(reach):
        for tile in range(wide):
            step = 0 if second_half else steps
            value = row_piece(None, near, kappa_far, step, row, tile, rows, tiles, depth)
            mask = halo_mask if tile == tiles else row_mask
            write_coefficients(tm, row, tile, value, mask, steps, kappa, inverse)

    def divide(values, row, tile):
        result, place = [], 0
        for _, is_complex in freqs:
            if is_complex:
                re, im = values[place], values[place + 1]
                p, q = inverse[place, row, tile], inverse[place + 1, row, tile]
                result += [re * p + im * q, im * p - re * q]
                place += 2
            else:
                result.append(values[place] * inverse[place, row, tile])
                place += 1
        return result

    for row in range(*rows_of(0)):
        for tile in range(wide):
            if tile == tiles and not 1 <= row < extended - 1:
                continue
            held = [
                row_piece(
                    blocks[b],
                    near,
                    far if b else kappa_far,
                    (b - 1 if b else 1) if second_half else b,
                    row,
                    tile,
                    rows,
                    tiles,
                    depth,
                )
                for b in range(steps)
            ]
            values = []
            for k, is_complex in freqs:
                values.append(combine((cosine(k * b, steps), held[b]) for b in range(steps)))
                if is_complex:
                    values.append(combine((-sine(k * b, steps), held[b]) for b in range(steps)))
            quotients = divide(values, row, tile)
            for field in range(fields):
                iterates[0][field, row, tile, middle, :] = quotients[field]


    def sweep(row, level):
        with_halo = level < row < extended - 1 - level and level < levels
        old = iterates[level - 1]
        scale, weight = relax_weights[level - 1], relax_weights[level]
        keep = (1.0 - weight) * scale / weight + (1.0 if level == 1 else 0.0)
        tilt = [scale * h for h in half]
        rolled = {}

        def around(field, tile):
            if (field, tile) not in rolled:
                center = old[field, row, tile, middle, :]
                rolled[field, tile] = (
                    center, pltpu.roll(center, 1, 1), pltpu.roll(center, lanes - 1, 1)
                )
            return rolled[field, tile]

        for tile in range(wide if with_halo else tiles):
            values = []
            scaled = scale * kappa[row, tile]
            below = [scaled + t for t in tilt]
            above = [scaled - t for t in tilt]
            for field in range(fields):
                _, down, up = around(field, tile)
                lower_x = jnp.where(at_first, around(field, (tile - 1) % wide)[1], down)
                upper_x = jnp.where(at_last, around(field, (tile + 1) % wide)[2], up)
                lower_z = old[field, row, tile, pl.ds(pad - 1, depth), :]
                upper_z = old[field, row, tile, pl.ds(pad + 1, depth), :]
                lower_y = old[field, row - 1, tile, middle, :]
                upper_y = old[field, row + 1, tile, middle, :]
                values.append(
                    (below[0] * lower_z + above[0] * upper_z)
                    + (below[1] * lower_y + above[1] * upper_y)
                    + (below[2] * lower_x + above[2] * upper_x)
                )
            quotients = divide(values, row, tile)
            results = []
            for field in range(fields):
                value = keep * old[field, row, tile, middle, :] + quotients[field]
                if level > 1:
                    value = value + iterates[0][field, row, tile, middle, :]
                results.append(value)
            yield tile, results

    for level in range(1, levels):
        for row in range(*rows_of(level)):
            for tile, results in sweep(row, level):
                for field in range(fields):
                    iterates[level][field, row, tile, middle, :] = results[field]

    last_rows = rows_of(levels)
    early = (rows - reach) * tiles
    places = [(ahead, 0) for ahead in range(steps)]
    if second_half:
        whole = [ahead for ahead in range(steps) if in_one(ahead)]
        for ahead, block in zip(whole, finished, strict=True):
            places[ahead] = (ahead, early)
            outs[ahead][pl.ds(0, early)] = block[...]
    else:
        places = [finished_place(ahead, early) for ahead in range(steps)]

    for row in range(*last_rows):
        for tile, results in sweep(row, levels):
            for ahead in range(steps):
                terms, field = [], 0
                for k, is_complex in freqs:
                    factor = relax_weights[levels] * (2.0 if is_complex else 1.0) / steps
                    terms.append((factor * cosine(k * ahead, steps), results[field]))
                    field += 1
                    if is_complex:
                        terms.append((-factor * sine(k * ahead, steps), results[field]))
                        field += 1
                which, start = places[ahead]
                outs[which][start + (row - last_rows[0]) * tiles + tile] = combine(terms)


def join_kernel(block, early, joined):
    count = block.shape[0]
    joined[pl.ds(0, count)] = block[...]
    handed = joined.shape[0] - count
    joined[pl.ds(count, handed)] = early[pl.ds(handed, handed)]


def unpack_kernel(tm, space, log_alpha, steps, own_early, early, *refs):
    tails, (out, held, semaphores) = refs[:steps], refs[steps:]
    me, up = lax.axis_index(tm), upwards(space)
    depth, rows, columns = out.shape
    width = columns // steps
    tiles = width // lanes
    shape = (1, depth, lanes)
    scale = jnp.exp(jnp.full(shape, me.astype(jnp.float32) * -log_alpha, jnp.float32))
    first = rows - reach
    rising = up == 1

    def at_row(behind, row, tile):
        if in_one(behind):
            return tails[behind][row * tiles + tile]
        if row >= first:
            return tails[behind][(row - first) * tiles + tile]
        if behind == 3:
            return tails[1][(rows + row) * tiles + tile]
        return (early if behind else own_early)[row * tiles + tile]

    copies = []
    for behind in range(steps):
        owner = slot_owner(me, behind, steps)
        for tile in range(tiles):
            column = [
                jnp.where(rising, at_row(behind, y, tile), at_row(behind, rows - 1 - y, tile))
                for y in range(rows)
            ]
            column = pltpu.einshape("yzx->zyx", jnp.stack(column) * scale)
            place = pl.multiple_of((owner * tiles + tile) * lanes, lanes)
            held[:, :, pl.ds(place, lanes)] = column
        part = pl.ds(pl.multiple_of(owner * width, lanes), width)
        copies.append(
            pltpu.make_async_copy(
                held.at[:, :, part], out.at[:, :, part], semaphores.at[behind]
            )
        )
        copies[-1].start()
    for copy in copies:
        copy.wait()


def gather(blocks, steps):
    result = [blocks[0]] + [None] * (steps - 1)
    for d in reversed(range(1, steps)):
        pairs = [(slot_time(t, d, steps), t) for t in range(steps)]
        result[d] = lax.ppermute(blocks[d], "tm", pairs)
    return result


def scatter(block, d, steps):
    return lax.ppermute(block, "tm", [(t, slot_time(t, d, steps)) for t in range(steps)])


def swap(value, first):
    names = ("parts", "tm", "space")
    parts, steps, size = (lax.axis_size(name) for name in names)
    pairs = []
    for part in range(parts):
        for step in range(steps):
            beside = (part, step ^ 1)
            for slab in range(size):
                partner = slab + 1 if (slab - first) % 2 == 0 else slab - 1
                target = (part, step, partner) if 0 <= partner < size else (*beside, slab)
                here, there = (
                    (p * steps + t) * size + c for p, t, c in ((part, step, slab), target)
                )
                pairs.append((here, there))
    return lax.ppermute(value, names, pairs)


def fast_local(rhs, diffusivity, velocity):
    _, depth, rows, columns = rhs.shape
    steps = lax.axis_size("tm")
    tiles = columns // steps // lanes
    sheets = depth // sublanes
    log_alpha = math.log(circ_alpha) / steps
    extended, wide = rows + 2 * reach, tiles + 1
    fields = steps
    blocks = gather(pack(rhs[0], steps), steps)
    piece = reach * tiles * sheets + 1
    made = [(extended, wide, depth, lanes), (fields, extended, wide, depth, lanes)]
    iterates = [(fields, extended, wide, depth + 16, lanes)] * reach
    own, own_far, drift = call(
        functools.partial(kappa_kernel, "tm", "space", steps),
        [
            (rows * tiles * sheets + 1, sublanes, lanes),
            (2 * piece, sublanes, lanes),
            (3, depth, lanes),
        ],
        diffusivity,
        velocity,
        blocks[0],
        specs={0: hbm, 1: hbm},
        scratch=[
            *staging(diffusivity.shape),
            pltpu.SMEM(velocity.shape, jnp.float32),
            pltpu.SemaphoreType.DMA,
        ],
    )
    kappa_far = swap(own_far, 1)
    kappa, inverse, *margins = call(
        functools.partial(prepare_kernel, "tm", rows, tiles, steps), [*made, *iterates], own
    )
    near, far = halos(blocks, own, kappa, piece)
    far = swap(far, 1)
    near = swap(near, 0)
    state = [*made, *iterates]
    early = (rows - reach) * tiles
    solve = functools.partial(solve_kernel, "tm", "space", rows, tiles, steps)
    kept = [kappa, inverse, *margins]
    counts = [early, early, 2 * early] + [early] * (steps - 4)
    held = call(
        functools.partial(solve, False),
        state + [(n, depth, lanes) for n in counts],
        *blocks,
        near,
        drift,
        *kept,
        aliases={steps + 2 + i: i for i in range(len(kept))},
    )
    state_now, finished = held[: len(state)], held[len(state) :]
    moved = scatter(finished[2], 2, steps)
    held = call(
        functools.partial(solve, True),
        state
        + [((rows if in_one(d) else reach) * tiles, depth, lanes) for d in range(steps)],
        far,
        kappa_far,
        drift,
        *state_now,
        *(finished[finished_place(d, early)[0]] for d in range(steps) if in_one(d)),
        aliases={3 + i: i for i in range(len(state))},
    )
    tails = list(held[len(state) :])
    (tails[1],) = call(join_kernel, [(rows * tiles + early, depth, lanes)], tails[1], moved)
    for d in reversed(range(1, steps)):
        tails[d] = scatter(tails[d], d, steps)
    (result,) = call(
        functools.partial(unpack_kernel, "tm", "space", log_alpha, steps),
        [(depth, rows, columns)],
        finished[0],
        moved,
        *tails,
        kept=False,
        scratch=[
            pltpu.VMEM((depth, rows, columns), jnp.float32),
            pltpu.SemaphoreType.DMA((steps,)),
        ],
    )
    return result[None]


def padded(shard, sides, width):
    for axis, dim in sides:
        size, length = (lax.axis_size(axis), shard.shape[dim])
        up = [(i, (i + 1) % size) for i in range(size - 1)]
        down = [(j, i) for i, j in up]
        last = lax.slice_in_dim(shard, length - width, length, axis=dim)
        initial = lax.slice_in_dim(shard, 0, width, axis=dim)
        before = lax.ppermute(last, axis, up)
        after = lax.ppermute(initial, axis, down)
        shard = jnp.concatenate([before, shard, after], axis=dim)
    return shard


def stencil(extended, diffusivity, diag_re, diag_im, velocity):
    center = extended[:, :, :, 1:-1, :]
    upper_y = extended[:, :, :, 2:, :]
    lower_y = extended[:, :, :, :-2, :]
    zero_z = jnp.zeros_like(center[:, :, :1])
    upper_z = jnp.concatenate([center[:, :, 1:], zero_z], axis=2)
    lower_z = jnp.concatenate([zero_z, center[:, :, :-1]], axis=2)
    zero_x = jnp.zeros_like(center[:, :, :, :, :1])
    upper_x = jnp.concatenate([center[:, :, :, :, 1:], zero_x], axis=4)
    lower_x = jnp.concatenate([zero_x, center[:, :, :, :, :-1]], axis=4)
    coefficient = diffusivity[None, None]
    half_velocity = 0.5 * velocity
    beside = (coefficient - half_velocity[0]) * upper_z + (coefficient + half_velocity[0]) * lower_z
    beside = (
        beside
        + (coefficient - half_velocity[1]) * upper_y
        + (coefficient + half_velocity[1]) * lower_y
    )
    beside = (
        beside
        + (coefficient - half_velocity[2]) * upper_x
        + (coefficient + half_velocity[2]) * lower_x
    )
    denominator = diag_re + 6.0 * diffusivity
    center_re = center[:, 0]
    center_im = center[:, 1]
    total_re = denominator * center_re - diag_im * center_im
    total_im = denominator * center_im + diag_im * center_re
    return jnp.stack([total_re, total_im], axis=1) - beside


def divide(residual, diffusivity, diag_re, diag_im):
    denominator = diag_re + 6.0 * diffusivity
    modulus = denominator * denominator + diag_im * diag_im
    residual_re = residual[:, 0]
    residual_im = residual[:, 1]
    quotient_re = (residual_re * denominator + residual_im * diag_im) / modulus
    quotient_im = (residual_im * denominator - residual_re * diag_im) / modulus
    return jnp.stack([quotient_re, quotient_im], axis=1)


def highest(left, right):
    return jnp.dot(left, right, precision=lax.Precision.HIGHEST, preferred_element_type=jnp.float32)


def twiddle(row_index, column_index, length):
    product = row_index[:, None] * column_index[None, :] % length
    phase_table = product.astype(jnp.float32) * (2.0 * math.pi / length)
    return (jnp.cos(phase_table), jnp.sin(phase_table))


def general_local(rhs, diffusivity, velocity):
    local_steps, depth, rows_y, rows_x = rhs.shape
    length = local_steps * lax.axis_size("tm")
    first_step = lax.axis_index("tm") * local_steps
    own_index = first_step + jnp.arange(local_steps, dtype=jnp.int32)
    log_alpha = math.log(circ_alpha) / length
    cell_count = depth * rows_y * rows_x
    scaled = (
        rhs.reshape(local_steps, cell_count)
        * jnp.exp(own_index.astype(jnp.float32) * log_alpha)[:, None]
    )
    regrouped = lax.all_to_all(scaled, "tm", split_axis=1, concat_axis=0, tiled=True)
    full_index = jnp.arange(length, dtype=jnp.int32)
    cosine_table, sine_table = twiddle(full_index, full_index, length)
    spectrum_re = highest(cosine_table, regrouped)
    spectrum_im = -highest(sine_table, regrouped)
    source_re, source_im = (
        lax.all_to_all(spectrum_re, "tm", split_axis=0, concat_axis=1, tiled=True),
        lax.all_to_all(spectrum_im, "tm", split_axis=0, concat_axis=1, tiled=True),
    )
    source = jnp.stack([source_re, source_im], axis=1).reshape(
        local_steps, 2, depth, rows_y, rows_x
    )
    phase_angle = own_index.astype(jnp.float32) * (2.0 * math.pi / length)
    shift_factor = circ_alpha ** (1.0 / length)
    diag_re = (1.0 - shift_factor * jnp.cos(phase_angle))[:, None, None, None]
    diag_im = (shift_factor * jnp.sin(phase_angle))[:, None, None, None]
    field = relax_weights[0] * divide(source, diffusivity, diag_re, diag_im)
    for weight in relax_weights[1:]:
        extended = padded(field, (("space", 3),), 1)
        applied = stencil(extended, diffusivity, diag_re, diag_im, velocity)
        field = field + weight * divide(source - applied, diffusivity, diag_re, diag_im)
    field_re = field[:, 0].reshape(local_steps, cell_count)
    field_im = field[:, 1].reshape(local_steps, cell_count)
    mixed_re, mixed_im = (
        lax.all_to_all(field_re, "tm", split_axis=1, concat_axis=0, tiled=True),
        lax.all_to_all(field_im, "tm", split_axis=1, concat_axis=0, tiled=True),
    )
    values = (highest(cosine_table, mixed_re) - highest(sine_table, mixed_im)) / length
    restored = lax.all_to_all(values, "tm", split_axis=0, concat_axis=1, tiled=True)
    result = restored * jnp.exp(-own_index.astype(jnp.float32) * log_alpha)[:, None]
    return result.reshape(local_steps, depth, rows_y, rows_x)


def local(rhs, diffusivity, velocity):
    steps = lax.axis_size("tm")
    local_steps, depth, rows, columns = rhs.shape
    slots = rows * (depth // sublanes)
    tiled = columns % (steps * lanes) == 0 and depth % sublanes == 0
    paired = steps % 2 == 0 and steps >= 4
    if local_steps == 1 and rows > reach and tiled and paired and 2 * reach * slots <= lanes:
        return fast_local(rhs, diffusivity, velocity)
    return general_local(rhs, diffusivity, velocity)


def solution(mesh):
    return jax.shard_map(
        local,
        mesh=mesh,
        in_specs=(P(("parts", "tm"), None, "space", None), P("parts", "space", None), P("parts")),
        out_specs=P(("parts", "tm"), None, "space", None),
        check_vma=False,
    )
```
